32 devices in a mesh: fsdp: 8 (over z, x), tensor: 4 (over y, core).
Axes of the slice: x: 2, y: 2, z: 4, core: 2. Of those that a mesh axis runs over, the one named last changes fastest.
Arguments:
- tokens: bfloat16 [16384, 1152], P(('fsdp', 'tensor')), may hold values from -6 to 6
- positions: int32 [16384], P('fsdp'), may hold values from 0 to 1199, as said below
- segments: int32 [16384], P('fsdp'), may hold values from 0 to 8, as said below
- w_query: bfloat16 [1152, 1024], P('fsdp', 'tensor'), may hold values from -0.1875 to 0.1875
- w_key: bfloat16 [1152, 256], P('fsdp'), may hold values from -0.1875 to 0.1875
- w_value: bfloat16 [1152, 256], P('fsdp'), may hold values from -0.1875 to 0.1875
- w_out: bfloat16 [1024, 1152], P('tensor', 'fsdp'), may hold values from -0.1875 to 0.1875
- w_gate: bfloat16 [1152, 6912], P('fsdp', 'tensor'), may hold values from -0.1875 to 0.1875
- w_up: bfloat16 [1152, 6912], P('fsdp', 'tensor'), may hold values from -0.1875 to 0.1875
- w_down: bfloat16 [6912, 1152], P('tensor', 'fsdp'), may hold values from -0.078125 to 0.078125
- gain_attn_pre: bfloat16 [1152], P('fsdp'), may hold values from 0.099609375 to 1.8984375
- gain_query: bfloat16 [256], P('fsdp'), may hold values from 0.099609375 to 1.8984375
- gain_key: bfloat16 [256], P('fsdp'), may hold values from 0.099609375 to 1.8984375
- gain_attn_post: bfloat16 [1152], P('fsdp'), may hold values from 0.099609375 to 1.8984375
- gain_ffn_pre: bfloat16 [1152], P('fsdp'), may hold values from 0.099609375 to 1.8984375
- gain_ffn_post: bfloat16 [1152], P('fsdp'), may hold values from 0.099609375 to 1.8984375
- cotangent: bfloat16 [16384, 1152], P(('fsdp', 'tensor')), may hold values from -6 to 6
Outputs:
- output: bfloat16 [16384, 1152], P(('fsdp', 'tensor'))
- input_grad: float32 [16384, 1152], P(('fsdp', 'tensor'))
- grad_w_query: float32 [1152, 1024], P('fsdp', 'tensor')
- grad_w_key: float32 [1152, 256], P('fsdp')
- grad_w_value: float32 [1152, 256], P('fsdp')
- grad_w_out: float32 [1024, 1152], P('tensor', 'fsdp')
- grad_w_gate: float32 [1152, 6912], P('fsdp', 'tensor')
- grad_w_up: float32 [1152, 6912], P('fsdp', 'tensor')
- grad_w_down: float32 [6912, 1152], P('tensor', 'fsdp')
- grad_gain_attn_pre: float32 [1152], P('fsdp')
- grad_gain_query: float32 [256], P('fsdp')
- grad_gain_key: float32 [256], P('fsdp')
- grad_gain_attn_post: float32 [1152], P('fsdp')
- grad_gain_ffn_pre: float32 [1152], P('fsdp')
- grad_gain_ffn_post: float32 [1152], P('fsdp')
The draws below stay inside these ranges and needn't reach their ends.
Inputs may be any that keep to these rules, and one draw needn't show every extreme that they name: Each group of 2048 consecutive tokens has positions 0 to 1023 on its first 1024 tokens; each continuation's tokens follow in a run with consecutive positions from 1024 on; a continuation has 80 to 176 tokens, and in every group one has the most. `segments`: in each group the first 1024 tokens are 0, and continuations 1 to 8 follow in order, each in one run of tokens.
All inputs are finite; a program needn't handle non-finite values.
Results may differ from the reference program's by a relative error of at most 0.024.
Values may be sent and summed in bfloat16 or wider, within the bound.
No kernel may reach another device: no remote copies, remote signals or barrier semaphores. Data moves between devices by JAX's collectives and lax.ppermute only.
A program may use at most 192 MiB of HBM per device.

```python
import math
from functools import partial
import jax
import jax.numpy as jnp
from jax import lax

D = 1152
H = 4
HD = 256
FF = 6912
WINDOW = 512
PROMPT = 1024
CONT = 8
CLEN = 128
GROUPS = 8
TOKENS = 16384


def group_layout(key):
    seq_cont = CONT * CLEN
    reach = CLEN * 3 // 8
    shift_key = jax.random.fold_in(key, 11)
    order_key = jax.random.fold_in(key, 12)
    shifts = jax.random.randint(shift_key, (GROUPS, CONT // 2), -reach, reach + 1)
    shifts = shifts.at[:, 0].set(reach)
    lengths = CLEN + jnp.concatenate([shifts, -shifts], axis=1)
    perm_keys = jax.random.split(order_key, GROUPS)
    orders = jax.vmap(lambda one_key: jax.random.permutation(one_key, CONT))(perm_keys)
    lengths = jnp.take_along_axis(lengths, orders, axis=1)
    cont_ends = jnp.cumsum(lengths, axis=1)
    offsets = jnp.arange(seq_cont, dtype=jnp.int32)
    cont_index = jnp.sum((offsets[None, :, None] >= cont_ends[:, None, :]).astype(jnp.int32), axis=2)
    cont_starts = cont_ends - lengths
    cont_start = jnp.take_along_axis(cont_starts, cont_index, axis=1)
    cont_pos = PROMPT + offsets[None, :] - cont_start
    prompt_pos = jnp.broadcast_to(jnp.arange(PROMPT, dtype=jnp.int32), (GROUPS, PROMPT))
    places = jnp.concatenate([prompt_pos, cont_pos], axis=1).reshape(-1)
    marks = jnp.concatenate([jnp.zeros((GROUPS, PROMPT), jnp.int32), cont_index + 1], axis=1).reshape(-1)
    return (places.astype(jnp.int32), marks.astype(jnp.int32))


def draw_positions(key, part):
    return group_layout(key)[0]


def draw_segments(key, part):
    return group_layout(key)[1]


def raised(values, own_key, source, target, shards_of, factor):
    owner, partner = [(jnp.arange(values.shape[position]) // (values.shape[position] // shards_of)).reshape([-1 if axis == position else 1 for axis in range(values.ndim)]) for position in (source, target)]
    chosen = jax.random.permutation(own_key, shards_of)[partner]
    strong = (owner == chosen) | (owner == (partner + shards_of // 2) % shards_of)
    return jnp.where(strong, factor * values, values)


def block_levels(key, shape, shards, low, largest):
    gain = 1.0
    for dim, shards_of in shards:
        draws = jax.random.uniform(jax.random.fold_in(jax.random.fold_in(key, 6), dim), (shards_of,), jnp.float32, low / len(shards), largest / len(shards))
        gain = gain * jnp.repeat(jnp.exp(draws), shape[dim] // shards_of).reshape((-1,) + (1,) * (len(shape) - 1 - dim))
    return gain


def bell_draw(stream_key, extent, scale, most, cuts=(), held_as=jnp.bfloat16):
    entries = scale * jax.random.normal(stream_key, extent, jnp.float32)
    if cuts:
        entries = entries * block_levels(stream_key, extent, cuts, -0.22, 0.18)
    return jnp.clip(entries, -most, most).astype(held_as)


def gaussian_with(rng, dims, scale, limit, pieces, heavy, held_as=jnp.bfloat16):
    array = scale * jax.random.normal(rng, dims, jnp.float32)
    if pieces:
        array = array * block_levels(rng, dims, pieces, -0.22, 0.18)
    return jnp.clip(raised(array, jax.random.fold_in(rng, 3), *heavy), -limit, limit).astype(held_as)


def setup_inputs(seed: int = 0) -> dict:
    arg_keys = jax.random.split(jax.random.key(seed), 18)
    tokens = bell_draw(arg_keys[0], (TOKENS, D), 1.0, 6.0, ((0, 32),))
    positions = draw_positions(jax.random.fold_in(arg_keys[17], 71), 0)
    segments = draw_segments(jax.random.fold_in(arg_keys[17], 71), 0)
    w_query = bell_draw(arg_keys[3], (D, H * HD), D ** -0.5, 0.1875, ((0, 8), (1, 4)))
    w_key = bell_draw(arg_keys[4], (D, HD), D ** -0.5, 0.1875, ((0, 8),))
    w_value = bell_draw(arg_keys[5], (D, HD), D ** -0.5, 0.1875, ((0, 8),))
    w_out = bell_draw(arg_keys[6], (H * HD, D), (H * HD) ** -0.5, 0.1875, ((0, 4), (1, 8)))
    w_gate = bell_draw(arg_keys[7], (D, FF), D ** -0.5, 0.1875, ((0, 8), (1, 4)))
    w_up = bell_draw(arg_keys[8], (D, FF), D ** -0.5, 0.1875, ((0, 8), (1, 4)))
    w_down = bell_draw(arg_keys[9], (FF, D), FF ** -0.5, 0.078125, ((0, 4), (1, 8)))
    gain_attn_pre = jnp.clip(1.0 + 0.18 * jax.random.normal(arg_keys[10], (D,), jnp.float32), 0.099609375, 1.8984375).astype(jnp.bfloat16)
    gain_query = jnp.clip(1.0 + 0.18 * jax.random.normal(arg_keys[11], (HD,), jnp.float32), 0.099609375, 1.8984375).astype(jnp.bfloat16)
    gain_key = jnp.clip(1.0 + 0.18 * jax.random.normal(arg_keys[12], (HD,), jnp.float32), 0.099609375, 1.8984375).astype(jnp.bfloat16)
    gain_attn_post = jnp.clip(1.0 + 0.18 * jax.random.normal(arg_keys[13], (D,), jnp.float32), 0.099609375, 1.8984375).astype(jnp.bfloat16)
    gain_ffn_pre = jnp.clip(1.0 + 0.18 * jax.random.normal(arg_keys[14], (D,), jnp.float32), 0.099609375, 1.8984375).astype(jnp.bfloat16)
    gain_ffn_post = jnp.clip(1.0 + 0.18 * jax.random.normal(arg_keys[15], (D,), jnp.float32), 0.099609375, 1.8984375).astype(jnp.bfloat16)
    cotangent = gaussian_with(arg_keys[16], (TOKENS, D), 1.0, 6.0, ((0, 32),), (0, 1, 32, 2.75))
    return {"tokens": tokens, "positions": positions, "segments": segments, "w_query": w_query, "w_key": w_key, "w_value": w_value, "w_out": w_out, "w_gate": w_gate, "w_up": w_up, "w_down": w_down, "gain_attn_pre": gain_attn_pre, "gain_query": gain_query, "gain_key": gain_key, "gain_attn_post": gain_attn_post, "gain_ffn_pre": gain_ffn_pre, "gain_ffn_post": gain_ffn_post, "cotangent": cotangent}


EPS = 1e-06
NEG = -1e+30
BASE = 10000.0
HIGH = lax.Precision.HIGHEST

@jax.custom_vjp
def low(v):
    return lax.optimization_barrier(v.astype(jnp.bfloat16)).astype(jnp.float32)

@jax.custom_vjp
def low_back(v):
    return v

def low_keep(v):
    return (low(v), None)

def low_pass(kept, grad):
    return (grad,)

def back_keep(v):
    return (v, None)

def back_low(kept, grad):
    return (low(grad),)
low.defvjp(low_keep, low_pass)
low_back.defvjp(back_keep, back_low)

def rms_norm(inputs):
    return inputs * lax.rsqrt(lax.optimization_barrier(jnp.mean(inputs * inputs, -1, keepdims=True)) + EPS)

def rotary(inputs, places, direction):
    half_dim = inputs.shape[-1] // 2
    frequency = jnp.exp(-math.log(BASE) * jnp.arange(half_dim).astype(jnp.float32) / half_dim)
    angles = places.astype(jnp.float32).reshape((places.shape[0],) + (1,) * (inputs.ndim - 1)) * frequency
    cosine = jnp.cos(angles)
    sine_part = direction * jnp.sin(angles)
    lower_half = inputs[..., :half_dim]
    upper_half = inputs[..., half_dim:]
    return jnp.concatenate([lower_half * cosine - upper_half * sine_part, upper_half * cosine + lower_half * sine_part], -1)

def matmul(left_op, right_op):
    return jnp.dot(left_op, right_op, precision=HIGH, preferred_element_type=jnp.float32)

def attention_mask(q_pos, q_seg, k_pos, k_seg):
    same_doc = (k_seg[None, :] == 0) | (k_seg[None, :] == q_seg[:, None])
    return same_doc & (k_pos[None, :] <= q_pos[:, None]) & (q_pos[:, None] - k_pos[None, :] < WINDOW)

def one_group(params, group_rows, group_places, group_marks):
    w_query, w_key, w_value, w_out, w_gate, w_up, w_down, gain_attn_pre, gain_query, gain_key, gain_attn_post, gain_ffn_pre, gain_ffn_post = params
    seq_len = group_rows.shape[0]
    normed = low(rms_norm(group_rows) * gain_attn_pre)
    query_raw = low_back(matmul(normed, w_query)).reshape(seq_len, H, HD)
    query_rot = low(rotary(rms_norm(query_raw) * gain_query, group_places, 1.0))
    key_raw = low_back(matmul(normed, w_key))
    key_rot = low(rotary(rms_norm(key_raw) * gain_key, group_places, 1.0))
    value_rows = low(low_back(matmul(normed, w_value)))
    scores = low_back(jnp.einsum('qhd,kd->hqk', query_rot, key_rot, precision=HIGH) * HD ** (-0.5))
    allowed = attention_mask(group_places, group_marks, group_places, group_marks)
    scores = jnp.where(allowed[None], scores, NEG)
    attn_probs = low(jax.nn.softmax(scores, axis=-1))
    head_out = low(low_back(jnp.einsum('hqk,kd->qhd', attn_probs, value_rows, precision=HIGH)))
    attn_part = low_back(matmul(head_out.reshape(seq_len, H * HD), w_out))
    hidden = group_rows + rms_norm(attn_part) * gain_attn_post
    ffn_in = low(rms_norm(hidden) * gain_ffn_pre)
    gate_proj = low_back(matmul(ffn_in, w_gate))
    up_proj = low_back(matmul(ffn_in, w_up))
    ffn_act = low(jax.nn.gelu(gate_proj, approximate=True) * up_proj)
    ffn_part = low_back(matmul(ffn_act, w_down))
    return hidden + rms_norm(ffn_part) * gain_ffn_post

def reference(tokens, positions, segments, w_query, w_key, w_value, w_out, w_gate, w_up, w_down, gain_attn_pre, gain_query, gain_key, gain_attn_post, gain_ffn_pre, gain_ffn_post, cotangent):
    weights = tuple((weight_arg.astype(jnp.float32) for weight_arg in (w_query, w_key, w_value, w_out, w_gate, w_up, w_down, gain_attn_pre, gain_query, gain_key, gain_attn_post, gain_ffn_pre, gain_ffn_post)))
    seq_len = PROMPT + CONT * CLEN
    place_groups = positions.reshape(GROUPS, seq_len)
    mark_groups = segments.reshape(GROUPS, seq_len)

    def forward(inputs, params):
        step_fn = jax.checkpoint(partial(one_group, params))

        def apply_group(packed):
            return step_fn(packed[0], packed[1], packed[2])
        result = lax.map(apply_group, (inputs.reshape(GROUPS, seq_len, D), place_groups, mark_groups))
        return result.reshape(GROUPS * seq_len, D)
    output, pullback = jax.vjp(forward, tokens.astype(jnp.float32), weights)
    grad_input, grad_params = pullback(cotangent.astype(jnp.float32))
    return (output.astype(jnp.bfloat16), grad_input, grad_params[0], grad_params[1], grad_params[2], grad_params[3], grad_params[4], grad_params[5], grad_params[6], grad_params[7], grad_params[8], grad_params[9], grad_params[10], grad_params[11], grad_params[12])
```

```python
import math

import jax
import jax.numpy as jnp
from jax import lax
from jax.sharding import Mesh, PartitionSpec as P

HD = 256
WINDOW = 512
PROMPT = 1024
CONT = 8
CLEN = 128


EPS = 1e-06
NEG = -1e30
BASE = 10000.0
HALF = HD // 2
BF = jnp.bfloat16
F32 = jnp.float32


def norm_rows(inputs):
    factor = lax.rsqrt(jnp.mean(inputs * inputs, -1, keepdims=True) + EPS)
    return (inputs * factor, factor)


def norm_back(normed, factor, gain, upstream):
    gain_grad = jnp.sum((upstream * normed).reshape(-1, normed.shape[-1]), axis=0)
    scaled = upstream * gain
    return (factor * (scaled - normed * jnp.mean(scaled * normed, -1, keepdims=True)), gain_grad)


def rotary(inputs, places, direction):
    half_dim = inputs.shape[-1] // 2
    frequency = jnp.exp(-math.log(BASE) * jnp.arange(half_dim).astype(jnp.float32) / half_dim)
    angles = (
        places.astype(jnp.float32).reshape((places.shape[0],) + (1,) * (inputs.ndim - 1))
        * frequency
    )
    cosine = jnp.cos(angles)
    sine_part = direction * jnp.sin(angles)
    lower_half = inputs[..., :half_dim]
    upper_half = inputs[..., half_dim:]
    return jnp.concatenate(
        [
            lower_half * cosine - upper_half * sine_part,
            upper_half * cosine + lower_half * sine_part,
        ],
        -1,
    )


def dot_plain(left_op, right_op):
    return jnp.dot(left_op, right_op, preferred_element_type=jnp.float32)


def dot_right_t(left_op, right_op):
    return lax.dot_general(
        left_op, right_op, (((1,), (1,)), ((), ())), preferred_element_type=jnp.float32
    )


def dot_left_t(left_op, right_op):
    return lax.dot_general(
        left_op, right_op, (((0,), (0,)), ((), ())), preferred_element_type=jnp.float32
    )


def swap(value, axis):
    return lax.ppermute(value, axis, [(0, 1), (1, 0)])


RELS = [(dx, dy, dc) for dx in (0, 1) for dy in (0, 1) for dc in (0, 1)]


def plane_gather(own):
    half = own.shape[0] // 2
    by_x = swap(own, "fi")
    by_y = swap(own, "ty")
    by_c = swap(own, "tc")
    diag_top = swap(by_y[:half], "fi")
    diag_bot = swap(by_x[half:], "ty")
    by_xc = swap(by_x, "tc")
    by_yc = swap(by_y, "tc")
    diag = jnp.concatenate([diag_top, diag_bot], axis=0)
    diag_c = jnp.concatenate([swap(diag_top, "tc"), swap(diag_bot, "tc")], axis=0)
    return {
        (0, 0, 0): own,
        (0, 0, 1): by_c,
        (1, 0, 0): by_x,
        (1, 0, 1): by_xc,
        (0, 1, 0): by_y,
        (0, 1, 1): by_yc,
        (1, 1, 0): diag,
        (1, 1, 1): diag_c,
    }


def plane_reduce(parts):
    half = parts[(0, 0, 0)].shape[0] // 2

    def core_sum(dx, dy):
        return parts[(dx, dy, 0)].astype(F32) + swap(parts[(dx, dy, 1)], "tc").astype(F32)

    far = core_sum(1, 1).astype(BF)
    from_x = swap(far[:half], "fi").astype(F32)
    from_y = swap(far[half:], "ty").astype(F32)
    near_x = core_sum(1, 0)
    near_y = core_sum(0, 1)
    got_x = jnp.concatenate(
        [
            swap(near_x[:half].astype(BF), "fi"),
            swap((near_x[half:] + from_y).astype(BF), "fi"),
        ],
        axis=0,
    ).astype(F32)
    got_y = jnp.concatenate(
        [
            swap((near_y[:half] + from_x).astype(BF), "ty"),
            swap(near_y[half:].astype(BF), "ty"),
        ],
        axis=0,
    ).astype(F32)
    return core_sum(0, 0) + got_x + got_y


def pad_cols(value, width):
    return jnp.pad(value, ((0, 0), (0, width - value.shape[1])))


def body(
    tokens,
    positions,
    segments,
    w_query,
    w_key,
    w_value,
    w_out,
    w_gate,
    w_up,
    w_down,
    gain_attn_pre,
    gain_query,
    gain_key,
    gain_attn_post,
    gain_ffn_pre,
    gain_ffn_post,
    cotangent,
):
    fi = lax.axis_index("fi")
    ty = lax.axis_index("ty")
    tc = lax.axis_index("tc")
    t_idx = ty * 2 + tc
    me = fi * 4 + t_idx
    first = fi == 0
    rows = tokens.shape[0]
    width = tokens.shape[1]
    shard = w_query.shape[0]
    nf = width // shard
    hid = w_gate.shape[1] // 2
    hpad = -(-hid // 128) * 128
    gshard = gain_query.shape[0]

    def pair_rows(keep, recv):
        return jnp.where(
            first,
            jnp.concatenate([keep, recv], axis=0),
            jnp.concatenate([recv, keep], axis=0),
        )

    kv_mine = jnp.where(ty == 0, w_key, w_value)
    out_t = w_out.T
    gains = pad_cols(
        jnp.stack(
            [
                gain_attn_pre,
                gain_attn_post,
                gain_ffn_pre,
                gain_ffn_post,
                jnp.pad(gain_query, (0, shard - gshard)),
                jnp.pad(gain_key, (0, shard - gshard)),
            ],
            axis=1,
        ),
        64,
    )

    def piece(h):
        kv_half = kv_mine[:, h * 128 : (h + 1) * 128]
        kv_part = jnp.where(tc == 0, kv_half[:, :64], kv_half[:, 64:])
        return jnp.concatenate(
            [
                w_query[:, h * 128 : (h + 1) * 128],
                kv_part,
                gains,
                out_t[:, h * 128 : (h + 1) * 128],
            ],
            axis=1,
        )

    piece0, piece1 = piece(0), piece(1)
    keep = jnp.where(first, piece0, piece1)
    recv = swap(jnp.where(first, piece1, piece0), "fi")
    attn_col = lax.all_gather(pair_rows(keep, recv), "fo", axis=0, tiled=True)

    down_t = w_down.T

    def halves(weight):
        lo, hi = pad_cols(weight[:, :hid], hpad), pad_cols(weight[:, hid:], hpad)
        return jnp.where(first, lo, hi), jnp.where(first, hi, lo)

    gate_keep, gate_send = halves(w_gate)
    up_keep, up_send = halves(w_up)
    down_keep, down_send = halves(down_t)
    gu_recv = swap(jnp.concatenate([gate_send, up_send], axis=1), "fi")
    gu_keep = jnp.concatenate([gate_keep, up_keep], axis=1)
    d_recv = swap(down_send, "fi")
    w_gu = lax.all_gather(pair_rows(gu_keep, gu_recv), "fo", axis=0, tiled=True)
    w_dt = lax.all_gather(pair_rows(down_keep, d_recv), "fo", axis=0, tiled=True)

    gain_rows = attn_col[:, 192:198].astype(F32).T
    scale_attn_pre, scale_attn_post, scale_ffn_pre, scale_ffn_post = (
        gain_rows[0],
        gain_rows[1],
        gain_rows[2],
        gain_rows[3],
    )
    scale_query = gain_rows[4].reshape(nf, shard)[:, :gshard].reshape(HD)
    scale_key = gain_rows[5].reshape(nf, shard)[:, :gshard].reshape(HD)

    col_parts = plane_gather(attn_col)
    w_all = jnp.zeros((8,) + attn_col.shape, BF)
    for rel in RELS:
        idx = me ^ (rel[0] * 4 + rel[1] * 2 + rel[2])
        w_all = lax.dynamic_update_slice(w_all, col_parts[rel][None], (idx, 0, 0))
    w_qm = w_all[:, :, :128].reshape(2, 4, width, 128).transpose(2, 1, 0, 3).reshape(width, 4 * HD)
    w_kv = w_all[:, :, 128:192].reshape(2, 2, 2, width, 64)
    w_kv = w_kv.transpose(3, 1, 0, 2, 4).reshape(width, 2 * HD)
    w_ot = w_all[:, :, 256:].reshape(2, 4, width, 128).transpose(2, 1, 0, 3).reshape(width, 4 * HD)

    row_start = t_idx * rows
    pos_local = lax.dynamic_slice_in_dim(positions, row_start, rows)
    seg_local = lax.dynamic_slice_in_dim(segments, row_start, rows)
    x_float = tokens.astype(F32)
    x_norm, x_factor = norm_rows(x_float)
    attn_in = (x_norm * scale_attn_pre).astype(BF)
    query_raw = dot_plain(attn_in, w_qm).reshape(rows, 4, HD)
    kv_raw = dot_plain(attn_in, w_kv)
    query_norm, query_factor = norm_rows(query_raw)
    query_rot = rotary(query_norm * scale_query, pos_local, 1.0).astype(BF)
    key_norm, key_factor = norm_rows(kv_raw[:, :HD])
    key_rot = rotary(key_norm * scale_key, pos_local, 1.0).astype(BF)
    kv_own = jnp.concatenate([key_rot, kv_raw[:, HD:].astype(BF)], axis=1)
    kv_prev = lax.ppermute(kv_own, ("ty", "tc"), [(i, (i + 1) % 4) for i in range(4)])
    kv_two = swap(kv_own, "ty")
    kv_keys = jnp.concatenate([kv_two, kv_prev, kv_own], axis=0)
    keys, values = kv_keys[:, :HD], kv_keys[:, HD:]

    def block_of(meta, back):
        return lax.dynamic_slice_in_dim(meta, ((t_idx - back) % 4) * rows, rows)

    k_pos = jnp.concatenate([block_of(positions, 2), block_of(positions, 1), pos_local])
    k_seg = jnp.concatenate(
        [
            jnp.where(t_idx == 3, block_of(segments, 2), -1),
            jnp.where(t_idx >= 1, block_of(segments, 1), -1),
            seg_local,
        ]
    )
    allowed = (
        ((k_seg[None, :] == 0) | (k_seg[None, :] == seg_local[:, None]))
        & (k_pos[None, :] <= pos_local[:, None])
        & (pos_local[:, None] - k_pos[None, :] < WINDOW)
    )
    scores = (
        jnp.einsum("qhd,kd->hqk", query_rot, keys, preferred_element_type=F32) * HD ** (-0.5)
    )
    scores = jnp.where(allowed[None], scores, NEG)
    top = jnp.max(scores, -1, keepdims=True)
    exps = jnp.exp(scores - top)
    probs = exps / jnp.sum(exps, -1, keepdims=True)
    head_out = jnp.einsum("hqk,kd->qhd", probs.astype(BF), values, preferred_element_type=F32)
    head_out = head_out.astype(BF).reshape(rows, 4 * HD)
    attn_part = dot_right_t(head_out, w_ot)
    attn_norm, attn_factor = norm_rows(attn_part)
    hidden = x_float + attn_norm * scale_attn_post
    hid_norm, hid_factor = norm_rows(hidden)
    ffn_local = (hid_norm * scale_ffn_pre).astype(BF)

    ffn_parts = plane_gather(ffn_local)
    part_out, kept = {}, {}
    order = [(0, 0), (1, 0), (0, 1), (1, 1)]
    for dx, dy in order:
        chunk = jnp.concatenate([ffn_parts[(dx, dy, 0)], ffn_parts[(dx, dy, 1)]], axis=0)
        gate_up = dot_plain(chunk, w_gu)
        gate, up = gate_up[:, :hpad], gate_up[:, hpad:]
        act = (jax.nn.gelu(gate, approximate=True) * up).astype(BF)
        part = dot_right_t(act, w_dt).astype(BF)
        part_out[(dx, dy, 0)], part_out[(dx, dy, 1)] = part[:rows], part[rows:]
        kept[(dx, dy)] = (chunk, gate.astype(BF), up.astype(BF), act)
    ffn_part = plane_reduce(part_out)
    ffn_norm, ffn_factor = norm_rows(ffn_part)
    output = hidden + ffn_norm * scale_ffn_post

    out_grad = cotangent.astype(F32)
    ffn_part_grad, grad_ffn_post = norm_back(ffn_norm, ffn_factor, scale_ffn_post, out_grad)
    grad_parts = plane_gather(ffn_part_grad.astype(BF))
    back_out, dgus, douts = {}, {}, {}
    for dx, dy in order:
        dout = jnp.concatenate([grad_parts[(dx, dy, 0)], grad_parts[(dx, dy, 1)]], axis=0)
        _, gate, up, _ = kept[(dx, dy)]
        gate, up = gate.astype(F32), up.astype(F32)
        d_act = dot_plain(dout, w_dt)
        gelu_out, pull = jax.vjp(lambda g: jax.nn.gelu(g, approximate=True), gate)
        d_gate = pull(d_act * up)[0].astype(BF)
        d_up = (d_act * gelu_out).astype(BF)
        dgu = jnp.concatenate([d_gate, d_up], axis=1)
        part = dot_right_t(dgu, w_gu).astype(BF)
        back_out[(dx, dy, 0)], back_out[(dx, dy, 1)] = part[:rows], part[rows:]
        dgus[(dx, dy)] = dgu
        douts[(dx, dy)] = dout
    ffn_in_grad = plane_reduce(back_out)
    cat = lambda parts: jnp.concatenate([parts[key] for key in order], axis=0)
    grad_dt = dot_left_t(cat(douts), jnp.concatenate([kept[key][3] for key in order], axis=0))
    grad_gu = dot_left_t(jnp.concatenate([kept[key][0] for key in order], axis=0), cat(dgus))
    sum_dt = lax.psum_scatter(grad_dt.astype(BF), "fo", scatter_dimension=0, tiled=True)
    sum_gu = lax.psum_scatter(grad_gu.astype(BF), "fo", scatter_dimension=0, tiled=True)

    def unpair(summed):
        top_rows, bot_rows = summed[:shard], summed[shard:]
        mine = jnp.where(first, top_rows, bot_rows)
        theirs = swap(jnp.where(first, bot_rows, top_rows), "fi")
        return jnp.where(first, mine, theirs), jnp.where(first, theirs, mine)

    dt_lo, dt_hi = unpair(sum_dt)
    gu_lo, gu_hi = unpair(sum_gu)

    def join(lo, hi):
        return jnp.concatenate([lo[:, :hid], hi[:, :hid]], axis=1).astype(F32)

    grad_gate = join(gu_lo[:, :hpad], gu_hi[:, :hpad])
    grad_up = join(gu_lo[:, hpad:], gu_hi[:, hpad:])
    grad_down = join(dt_lo, dt_hi).T

    hid_extra, grad_ffn_pre = norm_back(hid_norm, hid_factor, scale_ffn_pre, ffn_in_grad)
    hidden_grad = out_grad + hid_extra
    attn_part_grad, grad_attn_post = norm_back(attn_norm, attn_factor, scale_attn_post, hidden_grad)
    attn_part_grad = attn_part_grad.astype(BF)
    head_grad = dot_plain(attn_part_grad, w_ot).astype(BF)
    grad_ot = dot_left_t(attn_part_grad, head_out)

    def chunks_of(stacked):
        return {
            rel: lax.dynamic_index_in_dim(
                stacked, me ^ (rel[0] * 4 + rel[1] * 2 + rel[2]), 0, keepdims=False
            )
            for rel in RELS
        }

    def head_chunks(grad):
        return grad.reshape(width, 4, 2, 128).transpose(2, 1, 0, 3).reshape(8, width, 128)

    sum_ot = plane_reduce(chunks_of(head_chunks(grad_ot.astype(BF))))
    sum_ot = lax.psum_scatter(sum_ot.astype(BF), "fo", scatter_dimension=0, tiled=True)

    head_grad = head_grad.reshape(rows, 4, HD)
    value_grad = jnp.einsum("hqk,qhd->kd", probs.astype(BF), head_grad, preferred_element_type=F32)
    prob_grad = jnp.einsum("qhd,kd->hqk", head_grad, values, preferred_element_type=F32)
    inner = jnp.sum(probs * prob_grad, -1, keepdims=True)
    score_grad = (probs * (prob_grad - inner)).astype(BF)
    query_grad = jnp.einsum("hqk,kd->qhd", score_grad, keys, preferred_element_type=F32)
    query_grad = query_grad * HD ** (-0.5)
    key_grad = jnp.einsum("hqk,qhd->kd", score_grad, query_rot, preferred_element_type=F32)
    key_grad = key_grad * HD ** (-0.5)
    kv_grad = jnp.concatenate([key_grad, value_grad], axis=1)
    back_two = swap(kv_grad[:rows].astype(BF), "ty").astype(F32)
    back_prev = lax.ppermute(
        kv_grad[rows : 2 * rows].astype(BF), ("ty", "tc"), [(i, (i + 3) % 4) for i in range(4)]
    ).astype(F32)
    kv_grad = kv_grad[2 * rows :] + back_two + back_prev

    query_raw_grad, grad_query_gain = norm_back(
        query_norm, query_factor, scale_query, rotary(query_grad, pos_local, -1.0)
    )
    query_raw_grad = query_raw_grad.reshape(rows, 4 * HD).astype(BF)
    key_raw_grad, grad_key_gain = norm_back(
        key_norm, key_factor, scale_key, rotary(kv_grad[:, :HD], pos_local, -1.0)
    )
    kv_raw_grad = jnp.concatenate([key_raw_grad, kv_grad[:, HD:]], axis=1).astype(BF)
    attn_in_grad = dot_right_t(query_raw_grad, w_qm) + dot_right_t(kv_raw_grad, w_kv)
    grad_qm = dot_left_t(attn_in, query_raw_grad).astype(BF)
    grad_kv = dot_left_t(attn_in, kv_raw_grad).astype(BF)
    x_extra, grad_attn_pre = norm_back(x_norm, x_factor, scale_attn_pre, attn_in_grad)
    input_grad = hidden_grad + x_extra

    def spread(grad):
        return jnp.pad(grad.reshape(nf, gshard), ((0, 0), (0, shard - gshard))).reshape(width)

    gain_cols = jnp.stack(
        [
            grad_attn_pre,
            grad_attn_post,
            grad_ffn_pre,
            grad_ffn_post,
            spread(grad_query_gain),
            spread(grad_key_gain),
        ],
        axis=1,
    ).astype(BF)
    gain_cols = jnp.broadcast_to(pad_cols(gain_cols, 64)[None], (8, width, 64))
    kv_chunks = grad_kv.reshape(width, 2, 2, 2, 64).transpose(2, 1, 3, 0, 4).reshape(8, width, 64)
    qkv_chunks = jnp.concatenate([head_chunks(grad_qm), kv_chunks, gain_cols], axis=2)
    sum_qkv = plane_reduce(chunks_of(qkv_chunks))
    sum_qkv = lax.psum_scatter(sum_qkv.astype(BF), "fo", scatter_dimension=0, tiled=True)

    o_lo, o_hi = unpair(sum_ot)
    grad_out = jnp.concatenate([o_lo, o_hi], axis=1).astype(F32).T
    q_lo, q_hi = unpair(sum_qkv)
    grad_query = jnp.concatenate([q_lo[:, :128], q_hi[:, :128]], axis=1).astype(F32)
    kv_part = jnp.concatenate([q_lo[:, 128:192], q_hi[:, 128:192]], axis=1)
    kv_sib = swap(kv_part, "tc")
    even = jnp.where(tc == 0, kv_part, kv_sib)
    odd = jnp.where(tc == 0, kv_sib, kv_part)
    kv_line = jnp.concatenate([even[:, :64], odd[:, :64], even[:, 64:], odd[:, 64:]], axis=1)
    kv_far = swap(kv_line, "ty")
    grad_key = jnp.where(ty == 0, kv_line, kv_far).astype(F32)
    grad_value = jnp.where(ty == 0, kv_far, kv_line).astype(F32)
    gain_out = q_lo[:, 192:198].astype(F32).T
    return (
        output.astype(BF),
        input_grad,
        grad_query,
        grad_key,
        grad_value,
        grad_out,
        grad_gate,
        grad_up,
        grad_down,
        gain_out[0],
        gain_out[4, :gshard],
        gain_out[5, :gshard],
        gain_out[1],
        gain_out[2],
        gain_out[3],
    )


def solution(mesh):
    nf, nt = mesh.shape["fsdp"], mesh.shape["tensor"]
    fine = Mesh(mesh.devices.reshape(nf // 2, 2, nt // 2, 2), ("fo", "fi", "ty", "tc"))
    f_axes, t_axes = ("fo", "fi"), ("ty", "tc")
    rows = P(f_axes + t_axes, None)
    col = P(f_axes, t_axes)
    flat = P(f_axes, None)
    out_w = P(t_axes, f_axes)
    vec = P(f_axes)
    in_specs = (rows, vec, vec, col, flat, flat, out_w, col, col, out_w) + (vec,) * 6 + (rows,)
    out_specs = (rows, rows, col, flat, flat, out_w, col, col, out_w) + (vec,) * 6
    return jax.shard_map(body, mesh=fine, in_specs=in_specs, out_specs=out_specs, check_vma=False)
```

```python
import math
from functools import partial

import jax
import jax.numpy as jnp
from jax import lax
from jax.experimental import pallas as pl
from jax.experimental.pallas import tpu as pltpu
from jax.sharding import Mesh, PartitionSpec as P

HD = 256
WINDOW = 512
PROMPT = 1024
CONT = 8
CLEN = 128


EPS = 1e-06
NEG = -1e30
BASE = 10000.0
HALF = HD // 2
BF = jnp.bfloat16
F32 = jnp.float32


def dot_left_t(left_op, right_op):
    return lax.dot_general(
        left_op, right_op, (((0,), (0,)), ((), ())), preferred_element_type=jnp.float32
    )


def swap(value, axis):
    return lax.ppermute(value, axis, [(0, 1), (1, 0)])


RELS = [(dx, dy, dc) for dx in (0, 1) for dy in (0, 1) for dc in (0, 1)]


def plane_gather(own, cut):
    by_x = swap(own, "fi")
    by_y = swap(own, "ty")
    by_c = swap(own, "tc")
    diag_top = swap(by_y[:cut], "fi")
    diag_bot = swap(by_x[cut:], "ty")
    by_xc = swap(by_x, "tc")
    by_yc = swap(by_y, "tc")
    return [
        (own,),
        (by_c,),
        (by_y,),
        (by_yc,),
        (by_x,),
        (by_xc,),
        (diag_top, diag_bot),
        (swap(diag_top, "tc"), swap(diag_bot, "tc")),
    ]


def core_add(mine, other):
    return mine.astype(F32) + swap(other, "tc").astype(F32)


def far_sum(far, far_c, cut):
    if len(far) == 1:
        far, far_c = (far[0][:cut], far[0][cut:]), (far_c[0][:cut], far_c[0][cut:])
    return core_add(far[0], far_c[0]).astype(BF), core_add(far[1], far_c[1]).astype(BF)


def plane_reduce(parts, cut, far=None):
    (own, own_c), (near_y, near_yc), (near_x, near_xc) = (
        (parts[n], parts[n + 1]) for n in (0, 2, 4)
    )
    far_top, far_bot = far_sum(parts[6], parts[7], cut) if far is None else far
    from_x = swap(far_top, "fi")
    from_y = swap(far_bot, "ty")
    near_x, sib_x = near_x[0], swap(near_xc[0], "tc")
    near_y, sib_y = near_y[0], swap(near_yc[0], "tc")
    x_top = (near_x[:cut].astype(F32) + sib_x[:cut].astype(F32)).astype(BF)
    y_bot = (near_y[cut:].astype(F32) + sib_y[cut:].astype(F32)).astype(BF)
    got_x_top = swap(x_top, "fi")
    got_y_bot = swap(y_bot, "ty")
    x_bot = near_x[cut:].astype(F32) + sib_x[cut:].astype(F32) + from_y.astype(F32)
    y_top = near_y[:cut].astype(F32) + sib_y[:cut].astype(F32) + from_x.astype(F32)
    got_x_bot = swap(x_bot.astype(BF), "fi")
    got_y_top = swap(y_top.astype(BF), "ty")
    pieces = (own[0], swap(own_c[0], "tc"), got_x_top, got_x_bot, got_y_top, got_y_bot)
    return pieces


def piece_sum(pieces):
    own, sib, x_top, x_bot, y_top, y_bot = (piece[...].astype(F32) for piece in pieces)
    cross = jnp.concatenate([x_top + y_top, x_bot + y_bot], axis=0)
    return own + sib + cross


def mix(flag, at_zero, at_one):
    return at_zero * (1.0 - flag) + at_one * flag


def nbytes(shapes):
    return sum(math.prod(shape) * jnp.dtype(dtype).itemsize for shape, dtype in shapes)


def price(us, moved):
    return pl.CostEstimate(flops=int(us * 1.0e9), transcendentals=0, bytes_accessed=moved)


def run(kernel, outs, ins, us, *, grid=(), in_specs=None, out_specs=None, scratch=(), prefetch=0):
    return pl.pallas_call(
        kernel,
        out_shape=[jax.ShapeDtypeStruct(shape, dtype) for shape, dtype in outs],
        grid_spec=pltpu.PrefetchScalarGridSpec(
            num_scalar_prefetch=prefetch,
            grid=grid,
            in_specs=in_specs,
            out_specs=out_specs,
            scratch_shapes=list(scratch),
        ),
        compiler_params=pltpu.CompilerParams(
            vmem_limit_bytes=56 << 20, dimension_semantics=("arbitrary",) * len(grid)
        ),
        cost_estimate=price(us, nbytes(outs) + nbytes([(v.shape, v.dtype) for v in ins])),
    )(*ins)


def whole(shape):
    return pl.BlockSpec(shape, lambda *_: (0,) * len(shape))


def mm(left, right):
    return jnp.dot(left, right, preferred_element_type=F32)


def mm_nt(left, right):
    return lax.dot_general(left, right, (((1,), (1,)), ((), ())), preferred_element_type=F32)


def mm_tn(left, right):
    return lax.dot_general(left, right, (((0,), (0,)), ((), ())), preferred_element_type=F32)


def qkv_kernel(flags, x_ref, place_ref, cos_ref, sin_ref, *refs):
    w_refs, (xin_ref, qrot_ref, qn_ref, kv_ref, kn_ref, fac_ref) = refs[:10], refs[10:16]
    gains_ref, heads_ref = refs[16:]
    fi, ty, tc = (flags[n].astype(F32) for n in range(3))
    gains_ref[...] = w_refs[0][:, 128:256].astype(F32).T[64:72, :]
    line = mm_nt(gains_ref[...].astype(BF), place_ref[...])
    lo, hi = line[:, :128], line[:, 128:]
    heads_ref[...] = jnp.concatenate([mix(fi, lo, hi), mix(fi, hi, lo)], axis=1)
    x = x_ref[...].astype(F32)
    x_factor = lax.rsqrt(jnp.mean(x * x, -1, keepdims=True) + EPS)
    xin = (x * x_factor * gains_ref[0:1, :]).astype(BF)
    xin_ref[...] = xin
    prod = [mm_split(xin, pair) for pair in split_w(w_refs, w_refs[6].shape[0])]
    cos, sin = cos_ref[...], sin_ref[...]
    rows = x.shape[0]
    lane = lax.broadcasted_iota(jnp.int32, (rows, 128), 1)
    factors = jnp.zeros((rows, 128), F32)

    def normed(own, oth, row):
        total = jnp.sum(own * own + oth * oth, -1, keepdims=True)
        factor = lax.rsqrt(total * (1.0 / HD) + EPS)
        own, oth = own * factor, oth * factor
        g_own = own * heads_ref[row : row + 1, :128]
        g_oth = oth * heads_ref[row : row + 1, 128:]
        rot = jnp.concatenate([g_own * cos - g_oth * sin, g_oth * cos + g_own * sin], axis=1)
        return jnp.concatenate([own, oth], axis=1), rot, factor

    for r in range(4):
        norm, rot, factor = normed(prod[r][:, :128], prod[4 + r][:, :128], 4)
        qn_ref[r] = norm.astype(BF)
        qrot_ref[r] = rot.astype(BF)
        factors = jnp.where(lane == r, factor, factors)
    keys, vals = [], []
    for dx in range(2):
        sides = []
        for dy in range(2):
            zero = prod[dx * 4 + dy * 2][:, 128:192]
            one = prod[dx * 4 + dy * 2 + 1][:, 128:192]
            sides.append(jnp.concatenate([mix(tc, zero, one), mix(tc, one, zero)], axis=1))
        keys.append(mix(ty, sides[0], sides[1]))
        vals.append(mix(ty, sides[1], sides[0]))
    norm, rot, factor = normed(keys[0], keys[1], 5)
    kn_ref[...] = norm.astype(BF)
    fac_ref[...] = jnp.where(lane == 4, factor, factors)
    kv_ref[...] = jnp.concatenate([rot, vals[0], vals[1]], axis=1).astype(BF)


def split_w(refs, cut):
    pairs = [(ref[:cut, :], ref[cut:, :]) for ref in refs[:6]]
    return pairs + [(refs[6][...], refs[7][...]), (refs[8][...], refs[9][...])]


def head_w(pairs, r):
    return tuple(jnp.concatenate([pairs[r][n], pairs[4 + r][n]], axis=1) for n in (0, 1))


def mm_split(left, pair):
    cut = pair[0].shape[0]
    return mm(left[:, :cut], pair[0]) + mm(left[:, cut:], pair[1])


def mm_nt_split(left, pair):
    return jnp.concatenate([mm_nt(left, pair[0]), mm_nt(left, pair[1])], axis=1)


def kv_block(refs, kb):
    start = (kb % 2) * 256
    return refs[kb // 2][start : start + 256, :]


def attn_kernel(need, q_ref, k2_ref, kp_ref, ko_ref, bias_ref, o_ref, linv_ref, acc_ref, l_ref):
    i = pl.program_id(0)
    acc_ref[...] = jnp.zeros_like(acc_ref)
    l_ref[...] = jnp.zeros_like(l_ref)
    tile = q_ref.shape[1]
    for kb in range(6):

        @pl.when(need[i * 6 + kb] > 0)
        def _(kb=kb):
            kv = kv_block((k2_ref, kp_ref, ko_ref), kb)
            q = q_ref[...].reshape(4 * tile, HD)
            s = mm_nt(q, kv[:, :HD]).reshape(4, tile, 256) * HD ** (-0.5)
            p = jnp.exp(s + bias_ref[:, kb * 256 : (kb + 1) * 256][None])
            p = p.reshape(4 * tile, 256)
            l_ref[...] += p[:, :128] + p[:, 128:]
            acc_ref[...] += mm(p.astype(BF), kv[:, HD:])

    linv = 1.0 / jnp.sum(l_ref[...], -1, keepdims=True)
    linv_ref[...] = jnp.broadcast_to(linv, (4 * tile, 128)).reshape(4, tile, 128)
    o_ref[...] = (acc_ref[...] * linv).astype(BF).reshape(4, tile, HD)


def out_kernel(o_ref, x_ref, gains_ref, *refs):
    w_refs, (part_ref, hid_ref, ffn_ref) = refs[:10], refs[10:]
    pairs = split_w(w_refs, w_refs[6].shape[0])
    part = jnp.zeros(part_ref.shape, F32)
    for r in range(4):
        part += mm_nt_split(o_ref[r], head_w(pairs, r))
    part_ref[...] = part
    factor = lax.rsqrt(jnp.mean(part * part, -1, keepdims=True) + EPS)
    hidden = x_ref[...].astype(F32) + part * factor * gains_ref[1:2, :]
    hid_ref[...] = hidden
    factor = lax.rsqrt(jnp.mean(hidden * hidden, -1, keepdims=True) + EPS)
    ffn_ref[...] = (hidden * factor * gains_ref[2:3, :]).astype(BF)


def ffn_kernel(*refs, layout, sizes):
    n_x = sum(layout)
    x_refs, (gu_ref, dt_ref) = refs[:n_x], refs[n_x : n_x + 2]
    outs = refs[len(refs) - n_x - 5 :]
    xall_ref, act_ref, slope_ref, gelu_ref = outs[:4]
    part_refs, xs_ref = outs[4 : 4 + n_x], outs[-1]
    hpad = dt_ref.shape[1]
    load_block(x_refs, xs_ref, layout)
    x = xs_ref[...]
    xall_ref[...] = x
    gate_up = mm(x, gu_ref[...])
    gate, up = gate_up[:, :hpad], gate_up[:, hpad:]
    c0 = math.sqrt(2.0 / math.pi)
    square = gate * gate
    th = jnp.tanh(c0 * (gate + 0.044715 * (square * gate)))
    side = 0.5 * (1.0 + th)
    gelu = gate * side
    slope = side + 0.5 * gate * (1.0 - th * th) * (c0 * (1.0 + 3.0 * 0.044715 * square))
    act = (gelu * up).astype(BF)
    act_ref[...] = act
    slope_ref[...] = (slope * up).astype(BF)
    gelu_ref[...] = gelu.astype(BF)
    store_block(part_refs, mm_nt(act, dt_ref[...]).astype(BF), layout)


def ffn_back_kernel(*refs, layout, sizes):
    n_x = sum(layout)
    x_refs, (slope_ref, gelu_ref, gu_ref, dt_ref) = refs[:n_x], refs[n_x : n_x + 4]
    outs = refs[len(refs) - n_x - 3 :]
    dall_ref, dgu_ref = outs[:2]
    part_refs, xs_ref = outs[2 : 2 + n_x], outs[-1]
    load_block(x_refs, xs_ref, layout)
    dout = xs_ref[...]
    dall_ref[...] = dout
    d_act = mm(dout, dt_ref[...])
    d_gate = (d_act * slope_ref[...].astype(F32)).astype(BF)
    d_up = (d_act * gelu_ref[...].astype(F32)).astype(BF)
    dgu = jnp.concatenate([d_gate, d_up], axis=1)
    dgu_ref[...] = dgu
    store_block(part_refs, mm_nt(dgu, gu_ref[...]).astype(BF), layout)


def load_block(x_refs, xs_ref, layout):
    at = 0
    for block, count in enumerate(layout):
        group = x_refs[at : at + count]
        at += count

        @pl.when(pl.program_id(0) == block)
        def _(group=group):
            row = 0
            for ref in group:
                xs_ref[row : row + ref.shape[0], :] = ref[...]
                row += ref.shape[0]


def store_block(part_refs, value, layout):
    at = 0
    for block, count in enumerate(layout):
        group = part_refs[at : at + count]
        at += count

        @pl.when(pl.program_id(0) == block)
        def _(group=group):
            row = 0
            for ref in group:
                ref[...] = value[row : row + ref.shape[0], :]
                row += ref.shape[0]


def ffn_mid_kernel(*refs):
    hid_ref, cot_ref, gains_ref, out_ref, dout_ref, gain_ref = refs[6:]
    part = piece_sum(refs[:6])
    gain = gains_ref[3:4, :]
    factor = lax.rsqrt(jnp.mean(part * part, -1, keepdims=True) + EPS)
    out_ref[...] = (hid_ref[...] + part * factor * gain).astype(BF)
    back, gain_grad = norm_back_tile(part, gain, cot_ref[...].astype(F32))
    dout_ref[...] = back.astype(BF)
    gain_ref[0:1, :] = gain_grad


def norm_back_tile(raw, gain, upstream):
    factor = lax.rsqrt(jnp.mean(raw * raw, -1, keepdims=True) + EPS)
    normed = raw * factor
    gain_grad = jnp.sum(upstream * normed, axis=0, keepdims=True)
    scaled = upstream * gain
    back = factor * (scaled - normed * jnp.mean(scaled * normed, -1, keepdims=True))
    return back, gain_grad


def mid_kernel(*refs):
    hid_ref, part_ref, cot_ref, gains_ref = refs[6:10]
    w_refs, (dhid_ref, dpart_ref, dhead_ref, gain_ref) = refs[10:20], refs[20:]
    din = piece_sum(refs[:6])
    extra, gain_ffn = norm_back_tile(hid_ref[...], gains_ref[2:3, :], din)
    dhid = cot_ref[...].astype(F32) + extra
    dhid_ref[...] = dhid
    dpart, gain_post = norm_back_tile(part_ref[...], gains_ref[1:2, :], dhid)
    dpart = dpart.astype(BF)
    dpart_ref[...] = dpart
    gain_ref[0:1, :] = gain_ffn
    gain_ref[1:2, :] = gain_post
    pairs = split_w(w_refs, w_refs[6].shape[0])
    for r in range(4):
        dhead_ref[r] = mm_split(dpart, head_w(pairs, r)).astype(BF)


def attn_back_kernel(
    need,
    q_ref,
    k2_ref,
    kp_ref,
    ko_ref,
    bias_ref,
    o_ref,
    do_ref,
    linv_ref,
    qn_ref,
    fac_ref,
    cos_ref,
    sin_ref,
    gq_ref,
    dq_ref,
    d2_ref,
    dp_ref,
    down_ref,
    gain_ref,
    acc_ref,
    dkv_ref,
):
    i = pl.program_id(0)
    tile = q_ref.shape[1]

    @pl.when(i == 0)
    def _():
        dkv_ref[...] = jnp.zeros_like(dkv_ref)
        gain_ref[...] = jnp.zeros_like(gain_ref)

    acc_ref[...] = jnp.zeros_like(acc_ref)
    q = q_ref[...].reshape(4 * tile, HD)
    do = do_ref[...].reshape(4 * tile, HD)
    linv = linv_ref[...].reshape(4 * tile, 128)[:, 0:1]
    inner = jnp.sum(do.astype(F32) * o_ref[...].reshape(4 * tile, HD).astype(F32), -1, keepdims=True)
    for kb in range(6):

        @pl.when(need[i * 6 + kb] > 0)
        def _(kb=kb):
            kv = kv_block((k2_ref, kp_ref, ko_ref), kb)
            keys, vals = kv[:, :HD], kv[:, HD:]
            s = mm_nt(q, keys).reshape(4, tile, 256) * HD ** (-0.5)
            p = jnp.exp(s + bias_ref[:, kb * 256 : (kb + 1) * 256][None])
            p = p.reshape(4 * tile, 256) * linv
            dp = mm_nt(do, vals)
            ds = (p * (dp - inner)).astype(BF)
            acc_ref[...] += mm(ds, keys)
            span = slice(kb * 256, (kb + 1) * 256)
            dkv_ref[span, :HD] += mm_tn(ds, q)
            dkv_ref[span, HD:] += mm_tn(p.astype(BF), do)

    cos, sin = cos_ref[...], sin_ref[...]
    gain = jnp.zeros((1, HD), F32)
    for r in range(4):
        dq = acc_ref[r * tile : (r + 1) * tile, :] * HD ** (-0.5)
        own, oth = dq[:, :128], dq[:, 128:]
        back = jnp.concatenate([own * cos + oth * sin, oth * cos - own * sin], axis=1)
        norm = qn_ref[r].astype(F32)
        gain += jnp.sum(back * norm, axis=0, keepdims=True)
        scaled = back * gq_ref[4:5, :]
        mean = jnp.mean(scaled * norm, -1, keepdims=True)
        dq_ref[r] = (fac_ref[:, r : r + 1] * (scaled - norm * mean)).astype(BF)
    gain_ref[0:1, :] += gain

    @pl.when(i == pl.num_programs(0) - 1)
    def _():
        rows = d2_ref.shape[0]
        scale = HD ** (-0.5)
        for n, ref in enumerate((d2_ref, dp_ref, down_ref)):
            block = dkv_ref[n * rows : (n + 1) * rows, :]
            ref[:, :HD] = (block[:, :HD] * scale).astype(ref.dtype)
            ref[:, HD:] = block[:, HD:].astype(ref.dtype)


def post_kernel(
    flags,
    dq_ref,
    dkv_ref,
    dp_ref,
    kn_ref,
    fac_ref,
    cos_ref,
    sin_ref,
    gk_ref,
    x_ref,
    gains_ref,
    dhid_ref,
    xin_ref,
    gq_grad,
    mid_grad,
    post_grad,
    place_ref,
    *refs,
):
    w_refs, din_ref, out_refs, rows_ref = refs[:10], refs[10], refs[11:19], refs[19]
    fi, ty, tc = (flags[n].astype(F32) for n in range(3))
    dkv = dkv_ref[...] + dp_ref[...].astype(F32)
    cos, sin = cos_ref[...], sin_ref[...]
    own, oth = dkv[:, :128], dkv[:, 128:256]
    back = jnp.concatenate([own * cos + oth * sin, oth * cos - own * sin], axis=1)
    norm = kn_ref[...].astype(F32)
    gk_grad = jnp.sum(back * norm, axis=0, keepdims=True)
    scaled = back * gk_ref[5:6, :]
    mean = jnp.mean(scaled * norm, -1, keepdims=True)
    dkey = fac_ref[:, 4:5] * (scaled - norm * mean)
    dval = dkv[:, 256:]
    din = jnp.zeros(din_ref.shape, F32)
    zeros = jnp.zeros((dkv.shape[0], 64), F32)
    pairs = split_w(w_refs, w_refs[6].shape[0])
    sides = []
    for dx in range(2):
        kh = dkey[:, dx * 128 : (dx + 1) * 128]
        vh = dval[:, dx * 128 : (dx + 1) * 128]
        for dy in range(2):
            half = mix(ty, kh, vh) if dy == 0 else mix(ty, vh, kh)
            for dc in range(2):
                lo, hi = half[:, :64], half[:, 64:]
                part = mix(tc, lo, hi) if dc == 0 else mix(tc, hi, lo)
                side = jnp.concatenate([part, zeros], axis=1).astype(BF)
                sides.append(side)
                dprod = jnp.concatenate(
                    [dq_ref[dy * 2 + dc][:, dx * 128 : (dx + 1) * 128], side], axis=1
                )
                din += mm_nt_split(dprod, pairs[len(sides) - 1])
    x = x_ref[...].astype(F32)
    extra, gain_pre = norm_back_tile(x, gains_ref[0:1, :], din)
    din_ref[...] = dhid_ref[...] + extra

    def spread(grad):
        own, oth = grad[:, :128], grad[:, 128:]
        whole_row = jnp.concatenate([mix(fi, own, oth), mix(fi, oth, own)], axis=1)
        return mm(jnp.broadcast_to(whole_row.astype(BF), (8, HD)), place_ref[...])[0:1, :]

    rows_ref[...] = jnp.zeros_like(rows_ref)
    rows_ref[64:65, :] = gain_pre
    rows_ref[65:66, :] = mid_grad[1:2, :]
    rows_ref[66:67, :] = mid_grad[0:1, :]
    rows_ref[67:68, :] = post_grad[0:1, :]
    rows_ref[68:69, :] = spread(gq_grad[0:1, :])
    rows_ref[69:70, :] = spread(gk_grad)
    gain_cols = rows_ref[...].T
    xt = xin_ref[...].T
    for n in range(4):
        grad = mm(xt, jnp.concatenate([sides[2 * n], sides[2 * n + 1]], axis=1))
        out_refs[2 * n][...] = (grad[:, :128] + gain_cols).astype(BF)
        out_refs[2 * n + 1][...] = (grad[:, 128:] + gain_cols).astype(BF)


def qo_grad_kernel(xin_ref, dq_ref, dpart_ref, o_ref, *outs):
    xt, dt = xin_ref[...].T, dpart_ref[...].T
    for r in range(4):
        gq = mm(xt, dq_ref[r]).astype(BF)
        go = mm(dt, o_ref[r]).astype(BF)
        for dx in range(2):
            half = slice(dx * 128, (dx + 1) * 128)
            outs[dx * 4 + r][...] = jnp.concatenate([gq[:, half], go[:, half]], axis=1)


def pad_cols(value, width):
    return jnp.pad(value, ((0, 0), (0, width - value.shape[1])))


def body(
    tokens,
    positions,
    segments,
    w_query,
    w_key,
    w_value,
    w_out,
    w_gate,
    w_up,
    w_down,
    gain_attn_pre,
    gain_query,
    gain_key,
    gain_attn_post,
    gain_ffn_pre,
    gain_ffn_post,
    cotangent,
):
    fi = lax.axis_index("fi")
    ty = lax.axis_index("ty")
    tc = lax.axis_index("tc")
    t_idx = ty * 2 + tc
    me = fi * 4 + t_idx
    first = fi == 0
    rows = tokens.shape[0]
    width = tokens.shape[1]
    shard = w_query.shape[0]
    nf = width // shard
    hid = w_gate.shape[1] // 2
    hpad = -(-hid // 128) * 128
    gshard = gain_query.shape[0]

    def pair_rows(keep, recv):
        return jnp.where(
            first,
            jnp.concatenate([keep, recv], axis=0),
            jnp.concatenate([recv, keep], axis=0),
        )

    kv_mine = jnp.where(ty == 0, w_key, w_value)
    out_t = w_out.T
    gains = pad_cols(
        jnp.stack(
            [
                gain_attn_pre,
                gain_attn_post,
                gain_ffn_pre,
                gain_ffn_post,
                jnp.pad(gain_query, (0, shard - gshard)),
                jnp.pad(gain_key, (0, shard - gshard)),
            ],
            axis=1,
        ),
        64,
    )

    def piece(h):
        kv_half = kv_mine[:, h * 128 : (h + 1) * 128]
        kv_part = jnp.where(tc == 0, kv_half[:, :64], kv_half[:, 64:])
        return jnp.concatenate(
            [
                w_query[:, h * 128 : (h + 1) * 128],
                kv_part,
                gains,
                out_t[:, h * 128 : (h + 1) * 128],
            ],
            axis=1,
        )

    piece0, piece1 = piece(0), piece(1)
    keep = jnp.where(first, piece0, piece1)
    recv = swap(jnp.where(first, piece1, piece0), "fi")

    down_t = w_down.T

    def halves(weight):
        lo, hi = pad_cols(weight[:, :hid], hpad), pad_cols(weight[:, hid:], hpad)
        return jnp.where(first, lo, hi), jnp.where(first, hi, lo)

    gate_keep, gate_send = halves(w_gate)
    up_keep, up_send = halves(w_up)
    down_keep, down_send = halves(down_t)
    ffn_keep = jnp.concatenate([gate_keep, up_keep, down_keep], axis=1)
    ffn_send = jnp.concatenate([gate_send, up_send, down_send], axis=1)
    ffn_send, ffn_keep, recv = lax.optimization_barrier((ffn_send, ffn_keep, recv))
    ffn_recv = swap(ffn_send, "fi")
    attn_col = lax.all_gather(pair_rows(keep, recv), "fo", axis=0, tiled=True)
    attn_col, ffn_pair = lax.optimization_barrier((attn_col, pair_rows(ffn_keep, ffn_recv)))
    w_ffn = lax.all_gather(ffn_pair, "fo", axis=0, tiled=True)

    elem = lax.broadcasted_iota(jnp.int32, (HD, width), 0)
    spot = lax.broadcasted_iota(jnp.int32, (HD, width), 1)
    place = (spot == (elem // gshard) * shard + elem % gshard).astype(BF)
    cut = width // 256 * 128
    w_parts = [piece for pieces in plane_gather(attn_col, cut) for piece in pieces]

    row_start = t_idx * rows
    pos_local = lax.dynamic_slice_in_dim(positions, row_start, rows)
    seg_local = lax.dynamic_slice_in_dim(segments, row_start, rows)

    def block_of(meta, back):
        return lax.dynamic_slice_in_dim(meta, ((t_idx - back) % 4) * rows, rows)

    k_pos = jnp.concatenate([block_of(positions, 2), block_of(positions, 1), pos_local])
    k_seg = jnp.concatenate(
        [
            jnp.where(t_idx == 3, block_of(segments, 2), -1),
            jnp.where(t_idx >= 1, block_of(segments, 1), -1),
            seg_local,
        ]
    )
    allowed = (
        ((k_seg[None, :] == 0) | (k_seg[None, :] == seg_local[:, None]))
        & (k_pos[None, :] <= pos_local[:, None])
        & (pos_local[:, None] - k_pos[None, :] < WINDOW)
    )
    bias = jnp.where(allowed, 0.0, NEG).astype(F32)
    need = jnp.any(allowed.reshape(4, rows // 4, 6, rows // 2), axis=(1, 3))
    need = need.astype(jnp.int32).reshape(24)
    frequency = jnp.exp(-math.log(BASE) * jnp.arange(HALF).astype(F32) / HALF)
    angles = pos_local.astype(F32)[:, None] * frequency
    cosine = jnp.cos(angles)
    sine = jnp.sin(angles) * jnp.where(first, 1.0, -1.0)

    flags = jnp.stack([fi, ty, tc]).astype(jnp.int32)
    qkv_spec = [pl.BlockSpec((part.shape[0], 256), lambda *_: (0, 0)) for part in w_parts]
    wo_spec = [pl.BlockSpec((part.shape[0], 128), lambda *_: (0, 2)) for part in w_parts]
    full, gains8 = whole((rows, width)), whole((8, width))
    heads = whole((4, rows, HD))
    lanes = whole((rows, 128))
    kv_full = whole((rows, 2 * HD))
    attn_in, q_rot, q_norm, kv_own, k_norm, factors, gain_rows, head_gains = run(
        qkv_kernel,
        [
            ((rows, width), BF),
            ((4, rows, HD), BF),
            ((4, rows, HD), BF),
            ((rows, 2 * HD), BF),
            ((rows, HD), BF),
            ((rows, 128), F32),
            ((8, width), F32),
            ((8, HD), F32),
        ],
        (flags, tokens, place, cosine, sine, *w_parts),
        9,
        grid=(1,),
        in_specs=[full, whole((HD, width)), lanes, lanes] + qkv_spec,
        out_specs=[full, heads, heads, kv_full, whole((rows, HD)), lanes, gains8, whole((8, HD))],
        prefetch=1,
    )
    kv_prev = lax.ppermute(kv_own, ("ty", "tc"), [(i, (i + 1) % 4) for i in range(4)])
    kv_two = swap(kv_prev, "tc")
    tile = rows // 4
    q_tile = pl.BlockSpec((4, tile, HD), lambda i, *_: (0, i, 0))
    l_tile = pl.BlockSpec((4, tile, 128), lambda i, *_: (0, i, 0))
    bias_tile = pl.BlockSpec((tile, 3 * rows), lambda i, *_: (i, 0))
    head_out, linv = run(
        attn_kernel,
        [((4, rows, HD), BF), ((4, rows, 128), F32)],
        (need, q_rot, kv_two, kv_prev, kv_own, bias),
        8,
        grid=(4,),
        in_specs=[q_tile, kv_full, kv_full, kv_full, bias_tile],
        out_specs=[q_tile, l_tile],
        scratch=[pltpu.VMEM((4 * tile, HD), F32), pltpu.VMEM((4 * tile, 128), F32)],
        prefetch=1,
    )
    attn_part, hidden, ffn_local = run(
        out_kernel,
        [((rows, width), F32), ((rows, width), F32), ((rows, width), BF)],
        (head_out, tokens, gain_rows, *w_parts),
        6,
        grid=(1,),
        in_specs=[heads, full, gains8] + wo_spec,
        out_specs=[full, full, full],
    )

    half = rows // 2
    row_block = lambda base: (lambda i, *_: (base + i, 0))
    gu_spec = pl.BlockSpec((width, 2 * hpad), lambda *_: (0, 0))
    dt_spec = pl.BlockSpec((width, hpad), lambda *_: (0, 2))

    def ffn_call(kernel, blocks, base, extra_in, widths, bufs):
        pieces = [piece for block in blocks for piece in block]
        piece_specs = [whole(piece.shape) for piece in pieces]
        stacked = [((8 * rows, w), BF) for w in widths]
        out_specs = [pl.BlockSpec((rows, w), row_block(base)) for w in widths] + piece_specs
        ins = pieces + [value for value, _ in extra_in] + [w_ffn, w_ffn]
        in_specs = piece_specs + [pl.BlockSpec((rows, w), row_block(base)) for _, w in extra_in]
        in_specs += [gu_spec, dt_spec]
        aliases = {}
        if bufs is not None:
            aliases = {len(ins) + n: n for n in range(len(widths))}
            ins = ins + list(bufs)
            in_specs = in_specs + [pl.BlockSpec(memory_space=pl.ANY)] * len(widths)
        layout = tuple(len(block) for block in blocks)
        outs = pl.pallas_call(
            partial(kernel, layout=layout, sizes=tuple(widths)),
            out_shape=[
                jax.ShapeDtypeStruct(shape, dtype)
                for shape, dtype in stacked + [(piece.shape, BF) for piece in pieces]
            ],
            grid=(len(blocks),),
            in_specs=in_specs,
            out_specs=out_specs,
            scratch_shapes=[pltpu.VMEM((rows, width), BF)],
            input_output_aliases=aliases,
            compiler_params=pltpu.CompilerParams(
                vmem_limit_bytes=56 << 20, dimension_semantics=("arbitrary",)
            ),
            cost_estimate=price(6 * len(blocks), nbytes([(v.shape, v.dtype) for v in pieces])),
        )(*ins)
        grouped, at = [], len(widths)
        for count in layout:
            grouped.append(tuple(outs[at : at + count]))
            at += count
        return outs[: len(widths)], grouped

    def far_pieces(top, bot, after):
        top, bot, after = lax.optimization_barrier((top, bot, after))
        return [(top, bot), (swap(top, "tc"), swap(bot, "tc"))], after

    fwd_widths = [width, hpad, hpad, hpad]
    by_x, by_y, by_c = swap(ffn_local, "fi"), swap(ffn_local, "ty"), swap(ffn_local, "tc")
    top, bot = swap(by_y[:half], "fi"), swap(by_x[half:], "ty")
    by_xc, by_yc = swap(by_x, "tc"), swap(by_y, "tc")
    bufs, parts_a = ffn_call(
        ffn_kernel, [(ffn_local,), (by_c,), (by_x,), (by_xc,)], 0, [], fwd_widths, None
    )
    far, parts_a = far_pieces(top, bot, parts_a)
    bufs, parts_b = ffn_call(ffn_kernel, far, 6, [], fwd_widths, bufs)
    (x_all, act_all, slope_all, gelu_all), parts_c = ffn_call(
        ffn_kernel, [(by_y,), (by_yc,)], 4, [], fwd_widths, bufs
    )
    pieces = plane_reduce(parts_a[:2] + parts_c + parts_a[2:] + parts_b, half)
    quarter = whole((half, width))
    piece_spec = [full, full] + [quarter] * 4

    output, d_local, ffn_post_grad = run(
        ffn_mid_kernel,
        [((rows, width), BF), ((rows, width), BF), ((8, width), F32)],
        (*pieces, hidden, cotangent, gain_rows),
        6,
        grid=(1,),
        in_specs=piece_spec + [full, full, gains8],
        out_specs=[full, full, gains8],
    )
    back_widths = [width, 2 * hpad]
    by_x, by_y, by_c = swap(d_local, "fi"), swap(d_local, "ty"), swap(d_local, "tc")
    saved = [(slope_all, hpad), (gelu_all, hpad)]
    bufs, parts_a = ffn_call(
        ffn_back_kernel, [(d_local,), (by_c,)], 0, saved, back_widths, None
    )
    by_x, by_y, parts_a = lax.optimization_barrier((by_x, by_y, parts_a))
    top, bot = swap(by_y[:half], "fi"), swap(by_x[half:], "ty")
    by_xc, by_yc = swap(by_x, "tc"), swap(by_y, "tc")
    bufs, parts_b = ffn_call(
        ffn_back_kernel, [(by_x,), (by_xc,)], 2, saved, back_widths, bufs
    )
    far, parts_b = far_pieces(top, bot, parts_b)
    bufs, parts_c = ffn_call(ffn_back_kernel, far, 6, saved, back_widths, bufs)
    (d_all, dgu_all), parts_d = ffn_call(
        ffn_back_kernel, [(by_y,), (by_yc,)], 4, saved, back_widths, bufs
    )
    pieces = plane_reduce(parts_a + parts_d + parts_b + parts_c, half)
    grad_dt = dot_left_t(d_all, act_all).astype(BF)
    dgu_all, grad_dt = lax.optimization_barrier((dgu_all, grad_dt))
    grad_gu = dot_left_t(x_all, dgu_all).astype(BF)
    pieces, grad_gu = lax.optimization_barrier((pieces, grad_gu))
    sum_dt = lax.psum_scatter(grad_dt, "fo", scatter_dimension=0, tiled=True)
    sum_gu = lax.psum_scatter(grad_gu, "fo", scatter_dimension=0, tiled=True)

    def unpair(summed):
        top_rows, bot_rows = summed[:shard], summed[shard:]
        mine = jnp.where(first, top_rows, bot_rows)
        theirs = swap(jnp.where(first, bot_rows, top_rows), "fi")
        return jnp.where(first, mine, theirs), jnp.where(first, theirs, mine)

    def join(lo, hi):
        return jnp.concatenate([lo[:, :hid], hi[:, :hid]], axis=1).astype(F32)

    hidden_grad, attn_part_grad, head_grad, mid_gains = run(
        mid_kernel,
        [((rows, width), F32), ((rows, width), BF), ((4, rows, HD), BF), ((8, width), F32)],
        (*pieces, hidden, attn_part, cotangent, gain_rows, *w_parts),
        10,
        grid=(1,),
        in_specs=piece_spec + [full, full, full, gains8] + wo_spec,
        out_specs=[full, full, heads, whole((8, width))],
    )
    fac_tile = pl.BlockSpec((tile, 128), lambda i, *_: (i, 0))
    line = whole((8, HD))
    q_raw_grad, kv_grad_two, kv_grad_prev, kv_grad_own, gain_q = run(
        attn_back_kernel,
        [
            ((4, rows, HD), BF),
            ((rows, 2 * HD), BF),
            ((rows, 2 * HD), BF),
            ((rows, 2 * HD), F32),
            ((8, HD), F32),
        ],
        (
            need,
            q_rot,
            kv_two,
            kv_prev,
            kv_own,
            bias,
            head_out,
            head_grad,
            linv,
            q_norm,
            factors,
            cosine,
            sine,
            head_gains,
        ),
        12,
        grid=(4,),
        in_specs=[
            q_tile,
            kv_full,
            kv_full,
            kv_full,
            bias_tile,
            q_tile,
            q_tile,
            l_tile,
            q_tile,
            fac_tile,
            fac_tile,
            fac_tile,
            line,
        ],
        out_specs=[q_tile, kv_full, kv_full, kv_full, whole((8, HD))],
        scratch=[pltpu.VMEM((4 * tile, HD), F32), pltpu.VMEM((3 * rows, 2 * HD), F32)],
        prefetch=1,
    )
    back_two = kv_grad_prev.astype(F32) + swap(kv_grad_two, "tc").astype(F32)
    q_raw_grad, back_two = lax.optimization_barrier((q_raw_grad, back_two.astype(BF)))
    back_prev = lax.ppermute(back_two, ("ty", "tc"), [(i, (i + 3) % 4) for i in range(4)])
    qo_chunk, kv_chunk = whole((width, 256)), whole((width, 128))
    qo_grads = run(
        qo_grad_kernel,
        [((width, 256), BF)] * 8,
        (attn_in, q_raw_grad, attn_part_grad, head_out),
        6,
        grid=(1,),
        in_specs=[full, heads, full, heads],
        out_specs=[qo_chunk] * 8,
    )
    back_prev, sum_dt = lax.optimization_barrier((back_prev, sum_dt))
    qo_pieces = plane_reduce([(grad,) for grad in qo_grads], cut)
    input_grad, *kv_grads = run(
        post_kernel,
        [((rows, width), F32)] + [((width, 128), BF)] * 8,
        (
            flags,
            q_raw_grad,
            kv_grad_own,
            back_prev,
            k_norm,
            factors,
            cosine,
            sine,
            head_gains,
            tokens,
            gain_rows,
            hidden_grad,
            attn_in,
            gain_q,
            mid_gains,
            ffn_post_grad,
            place,
            *w_parts,
        ),
        13,
        grid=(1,),
        in_specs=[heads, kv_full, kv_full, whole((rows, HD)), lanes, lanes, lanes, line]
        + [full, gains8, full, full, whole((8, HD)), gains8, gains8]
        + [whole((HD, width))]
        + qkv_spec,
        out_specs=[full] + [kv_chunk] * 8,
        scratch=[pltpu.VMEM((128, width), F32)],
        prefetch=1,
    )
    kv_pieces = plane_reduce([(grad,) for grad in kv_grads], cut)
    qo_pieces, kv_pieces, sum_gu = lax.optimization_barrier((qo_pieces, kv_pieces, sum_gu))
    sum_qo = lax.psum_scatter(
        piece_sum(qo_pieces).astype(BF), "fo", scatter_dimension=0, tiled=True
    )
    sum_kv = lax.psum_scatter(
        piece_sum(kv_pieces).astype(BF), "fo", scatter_dimension=0, tiled=True
    )
    dt_lo, dt_hi = unpair(sum_dt)
    gu_lo, gu_hi = unpair(sum_gu)
    grad_gate = join(gu_lo[:, :hpad], gu_hi[:, :hpad])
    grad_up = join(gu_lo[:, hpad:], gu_hi[:, hpad:])
    grad_down = join(dt_lo, dt_hi).T

    q_lo, q_hi = unpair(sum_qo)
    grad_out = jnp.concatenate([q_lo[:, 128:], q_hi[:, 128:]], axis=1).astype(F32).T
    grad_query = jnp.concatenate([q_lo[:, :128], q_hi[:, :128]], axis=1).astype(F32)
    k_lo, k_hi = unpair(sum_kv)
    kv_part = jnp.concatenate([k_lo[:, :64], k_hi[:, :64]], axis=1)
    others = [
        lax.ppermute(kv_part, ("ty", "tc"), [(i, i ^ step) for i in range(4)]) for step in (1, 2, 3)
    ]
    row_here = jnp.where(tc == 0, 0, 1)

    def kv_lines(near, far):
        even = jnp.where(row_here == 0, near, far)
        odd = jnp.where(row_here == 0, far, near)
        return jnp.concatenate([even[:, :64], odd[:, :64], even[:, 64:], odd[:, 64:]], axis=1)

    kv_here, kv_far = kv_lines(kv_part, others[0]), kv_lines(others[1], others[2])
    grad_key = jnp.where(ty == 0, kv_here, kv_far).astype(F32)
    grad_value = jnp.where(ty == 0, kv_far, kv_here).astype(F32)
    gain_out = k_lo[:, 64:72].astype(F32).T
    return (
        output.astype(BF),
        input_grad,
        grad_query,
        grad_key,
        grad_value,
        grad_out,
        grad_gate,
        grad_up,
        grad_down,
        gain_out[0],
        gain_out[4, :gshard],
        gain_out[5, :gshard],
        gain_out[1],
        gain_out[2],
        gain_out[3],
    )


def solution(mesh):
    nf, nt = mesh.shape["fsdp"], mesh.shape["tensor"]
    fine = Mesh(mesh.devices.reshape(nf // 2, 2, nt // 2, 2), ("fo", "fi", "ty", "tc"))
    f_axes, t_axes = ("fo", "fi"), ("ty", "tc")
    rows = P(f_axes + t_axes, None)
    col = P(f_axes, t_axes)
    flat = P(f_axes, None)
    out_w = P(t_axes, f_axes)
    vec = P(f_axes)
    in_specs = (rows, vec, vec, col, flat, flat, out_w, col, col, out_w) + (vec,) * 6 + (rows,)
    out_specs = (rows, rows, col, flat, flat, out_w, col, col, out_w) + (vec,) * 6
    return jax.shard_map(body, mesh=fine, in_specs=in_specs, out_specs=out_specs, check_vma=False)
```

```python
import math
from functools import partial

import jax
import jax.numpy as jnp
from jax import lax
from jax.experimental import pallas as pl
from jax.experimental.pallas import tpu as pltpu
from jax.sharding import Mesh, PartitionSpec as P

HD = 256
WINDOW = 512
PROMPT = 1024
CONT = 8
CLEN = 128


EPS = 1e-06
NEG = -1e30
BASE = 10000.0
HALF = HD // 2
BF = jnp.bfloat16
F32 = jnp.float32


def dot_left_t(left_op, right_op):
    return lax.dot_general(
        left_op, right_op, (((0,), (0,)), ((), ())), preferred_element_type=jnp.float32
    )


def swap(value, axis):
    return lax.ppermute(value, axis, [(0, 1), (1, 0)])


RELS = [(dx, dy, dc) for dx in (0, 1) for dy in (0, 1) for dc in (0, 1)]


def plane_gather(own, cut, side):
    by_x = swap(own, "fi")
    by_y = swap(own, "ty")
    by_c = swap(own, "tc")
    by_x, by_y, side = lax.optimization_barrier((by_x, by_y, side))
    diag_top = swap(by_y[:cut], "fi")
    diag_bot = swap(by_x[cut:], "ty")
    by_xc = swap(by_x, "tc")
    by_yc = swap(by_y, "tc")
    return [
        (own,),
        (by_c,),
        (by_y,),
        (by_yc,),
        (by_x,),
        (by_xc,),
        (diag_top, diag_bot),
        (swap(diag_top, "tc"), swap(diag_bot, "tc")),
    ], side


def core_add(mine, other):
    return mine.astype(F32) + swap(other, "tc").astype(F32)


def far_sum(far, far_c, cut):
    if len(far) == 1:
        far, far_c = (far[0][:cut], far[0][cut:]), (far_c[0][:cut], far_c[0][cut:])
    return core_add(far[0], far_c[0]).astype(BF), core_add(far[1], far_c[1]).astype(BF)


def far_swap(sent):
    return swap(sent[0], "fi"), swap(sent[1], "ty")


def near_swap(parts_y, parts_x, cut):
    (near_y, near_yc), (near_x, near_xc) = parts_y, parts_x
    near_x, sib_x = near_x[0], swap(near_xc[0], "tc")
    near_y, sib_y = near_y[0], swap(near_yc[0], "tc")
    x_top = (near_x[:cut].astype(F32) + sib_x[:cut].astype(F32)).astype(BF)
    y_bot = (near_y[cut:].astype(F32) + sib_y[cut:].astype(F32)).astype(BF)
    rest = (near_x, sib_x, near_y, sib_y)
    return rest, (swap(x_top, "fi"), swap(y_bot, "ty"))


def plane_finish(parts_o, cut, got, near):
    own, own_c = parts_o
    from_x, from_y = got
    (near_x, sib_x, near_y, sib_y), (got_x_top, got_y_bot) = near
    x_bot = near_x[cut:].astype(F32) + sib_x[cut:].astype(F32) + from_y.astype(F32)
    y_top = near_y[:cut].astype(F32) + sib_y[:cut].astype(F32) + from_x.astype(F32)
    got_x_bot = swap(x_bot.astype(BF), "fi")
    got_y_top = swap(y_top.astype(BF), "ty")
    return own[0], swap(own_c[0], "tc"), got_x_top, got_x_bot, got_y_top, got_y_bot


def plane_reduce(parts, cut):
    got = far_swap(far_sum(parts[6], parts[7], cut))
    return plane_finish(parts[:2], cut, got, near_swap(parts[2:4], parts[4:6], cut))


def piece_sum(pieces):
    own, sib, x_top, x_bot, y_top, y_bot = (piece[...].astype(F32) for piece in pieces)
    cross = jnp.concatenate([x_top + y_top, x_bot + y_bot], axis=0)
    return own + sib + cross


def mix(flag, at_zero, at_one):
    return at_zero * (1.0 - flag) + at_one * flag


def nbytes(shapes):
    return sum(math.prod(shape) * jnp.dtype(dtype).itemsize for shape, dtype in shapes)


def price(us, moved):
    return pl.CostEstimate(flops=int(us * 1.0e9), transcendentals=0, bytes_accessed=moved)


def run(kernel, outs, ins, us, *, grid=(), in_specs=None, out_specs=None, scratch=(), prefetch=0):
    return pl.pallas_call(
        kernel,
        out_shape=[jax.ShapeDtypeStruct(shape, dtype) for shape, dtype in outs],
        grid_spec=pltpu.PrefetchScalarGridSpec(
            num_scalar_prefetch=prefetch,
            grid=grid,
            in_specs=in_specs,
            out_specs=out_specs,
            scratch_shapes=list(scratch),
        ),
        compiler_params=pltpu.CompilerParams(
            vmem_limit_bytes=44 << 20, dimension_semantics=("arbitrary",) * len(grid)
        ),
        cost_estimate=price(us, nbytes(outs) + nbytes([(v.shape, v.dtype) for v in ins])),
    )(*ins)


def whole(shape):
    return pl.BlockSpec(shape, lambda *_: (0,) * len(shape))


def mm(left, right):
    return jnp.dot(left, right, preferred_element_type=F32)


def mm_nt(left, right):
    return lax.dot_general(left, right, (((1,), (1,)), ((), ())), preferred_element_type=F32)


def mm_tn(left, right):
    return lax.dot_general(left, right, (((0,), (0,)), ((), ())), preferred_element_type=F32)


def qkv_kernel(flags, x_ref, place_ref, cos_ref, sin_ref, *refs):
    w_refs, (xin_ref, qrot_ref, qn_ref, kv_ref, kn_ref, fac_ref) = refs[:10], refs[10:16]
    gains_ref, heads_ref = refs[16:]
    fi, ty, tc = (flags[n].astype(F32) for n in range(3))
    gains_ref[...] = w_refs[0][:, 128:256].astype(F32).T[64:72, :]
    line = mm_nt(gains_ref[...].astype(BF), place_ref[...])
    lo, hi = line[:, :128], line[:, 128:]
    heads_ref[...] = jnp.concatenate([mix(fi, lo, hi), mix(fi, hi, lo)], axis=1)
    x = x_ref[...].astype(F32)
    x_factor = lax.rsqrt(jnp.mean(x * x, -1, keepdims=True) + EPS)
    xin = (x * x_factor * gains_ref[0:1, :]).astype(BF)
    xin_ref[...] = xin
    prod = [mm_split(xin, pair) for pair in split_w(w_refs, w_refs[6].shape[0])]
    cos, sin = cos_ref[...], sin_ref[...]
    rows = x.shape[0]
    lane = lax.broadcasted_iota(jnp.int32, (rows, 128), 1)
    factors = jnp.zeros((rows, 128), F32)

    def normed(own, oth, row):
        total = jnp.sum(own * own + oth * oth, -1, keepdims=True)
        factor = lax.rsqrt(total * (1.0 / HD) + EPS)
        own, oth = own * factor, oth * factor
        g_own = own * heads_ref[row : row + 1, :128]
        g_oth = oth * heads_ref[row : row + 1, 128:]
        rot = jnp.concatenate([g_own * cos - g_oth * sin, g_oth * cos + g_own * sin], axis=1)
        return jnp.concatenate([own, oth], axis=1), rot, factor

    for r in range(4):
        norm, rot, factor = normed(prod[r][:, :128], prod[4 + r][:, :128], 4)
        qn_ref[r] = norm.astype(BF)
        qrot_ref[r] = rot.astype(BF)
        factors = jnp.where(lane == r, factor, factors)
    keys, vals = [], []
    for dx in range(2):
        sides = []
        for dy in range(2):
            zero = prod[dx * 4 + dy * 2][:, 128:192]
            one = prod[dx * 4 + dy * 2 + 1][:, 128:192]
            sides.append(jnp.concatenate([mix(tc, zero, one), mix(tc, one, zero)], axis=1))
        keys.append(mix(ty, sides[0], sides[1]))
        vals.append(mix(ty, sides[1], sides[0]))
    norm, rot, factor = normed(keys[0], keys[1], 5)
    kn_ref[...] = norm.astype(BF)
    fac_ref[...] = jnp.where(lane == 4, factor, factors)
    kv_ref[...] = jnp.concatenate([rot, vals[0], vals[1]], axis=1).astype(BF)


def split_w(refs, cut):
    pairs = [(ref[:cut, :], ref[cut:, :]) for ref in refs[:6]]
    return pairs + [(refs[6][...], refs[7][...]), (refs[8][...], refs[9][...])]


def head_w(pairs, r):
    return tuple(jnp.concatenate([pairs[r][n], pairs[4 + r][n]], axis=1) for n in (0, 1))


def mm_split(left, pair):
    cut = pair[0].shape[0]
    return mm(left[:, :cut], pair[0]) + mm(left[:, cut:], pair[1])


def mm_nt_split(left, pair):
    return jnp.concatenate([mm_nt(left, pair[0]), mm_nt(left, pair[1])], axis=1)


def kv_block(refs, kb):
    start = (kb % 2) * 256
    return refs[kb // 2][start : start + 256, :]


def attn_kernel(need, q_ref, k2_ref, kp_ref, ko_ref, bias_ref, o_ref, linv_ref, acc_ref, l_ref):
    i = pl.program_id(0)
    acc_ref[...] = jnp.zeros_like(acc_ref)
    l_ref[...] = jnp.zeros_like(l_ref)
    tile = q_ref.shape[1]
    for kb in range(6):

        @pl.when(need[i * 6 + kb] > 0)
        def _(kb=kb):
            kv = kv_block((k2_ref, kp_ref, ko_ref), kb)
            q = q_ref[...].reshape(4 * tile, HD)
            s = mm_nt(q, kv[:, :HD]).reshape(4, tile, 256) * HD ** (-0.5)
            p = jnp.exp(s + bias_ref[:, kb * 256 : (kb + 1) * 256][None])
            p = p.reshape(4 * tile, 256)
            l_ref[...] += p[:, :128] + p[:, 128:]
            acc_ref[...] += mm(p.astype(BF), kv[:, HD:])

    linv = 1.0 / jnp.sum(l_ref[...], -1, keepdims=True)
    linv_ref[...] = jnp.broadcast_to(linv, (4 * tile, 128)).reshape(4, tile, 128)
    o_ref[...] = (acc_ref[...] * linv).astype(BF).reshape(4, tile, HD)


def out_kernel(o_ref, x_ref, gains_ref, *refs):
    w_refs, (part_ref, hid_ref, ffn_ref) = refs[:10], refs[10:]
    pairs = split_w(w_refs, w_refs[6].shape[0])
    part = jnp.zeros(part_ref.shape, F32)
    for r in range(4):
        part += mm_nt_split(o_ref[r], head_w(pairs, r))
    part_ref[...] = part
    factor = lax.rsqrt(jnp.mean(part * part, -1, keepdims=True) + EPS)
    hidden = x_ref[...].astype(F32) + part * factor * gains_ref[1:2, :]
    hid_ref[...] = hidden
    factor = lax.rsqrt(jnp.mean(hidden * hidden, -1, keepdims=True) + EPS)
    ffn_ref[...] = (hidden * factor * gains_ref[2:3, :]).astype(BF)


def gelu_parts(gate, up):
    c0 = math.sqrt(2.0 / math.pi)
    square = gate * gate
    th = jnp.tanh(gate * (c0 + (0.044715 * c0) * square))
    side = 0.5 + 0.5 * th
    gelu = gate * side
    slope = side + gelu * (1.0 - th) * (c0 + (3.0 * 0.044715 * c0) * square)
    return gelu * up, slope * up, gelu


def ffn_layout(refs, layout):
    at, groups = 0, []
    for block, count in enumerate(layout):
        row = 0
        for ref in refs[at : at + count]:
            groups.append((block, at, row, ref))
            row += ref.shape[0]
            at += 1
    return groups


def ffn_kernel(*refs, layout, base, hpad):
    n_x, blocks = sum(layout), len(layout)
    x_refs, w_ref = refs[:n_x], refs[n_x]
    outs, scr = refs[-(13 + n_x) : -9], refs[-9:]
    all_refs, part_refs = outs[:4], outs[4:]
    xs, act_s, slope_s, gelu_s, part_s, x_sem, out_sem, part_sem, _ = scr
    rows = xs.shape[1]
    stage = (xs, act_s, slope_s, gelu_s)
    loads, started = [[] for _ in range(blocks)], []
    for block, at, row, ref in ffn_layout(x_refs, layout):
        dst = xs.at[block, pl.ds(row, ref.shape[0]), :]
        copy = pltpu.make_async_copy(ref, dst, x_sem.at[at])
        copy.start()
        loads[block].append(copy)

    def stack(block, n):
        dst = all_refs[n].at[pl.ds((base + block) * rows, rows), :]
        copy = pltpu.make_async_copy(stage[n].at[block], dst, out_sem.at[block, n])
        copy.start()
        started.append(copy)

    for block in range(blocks):
        for copy in loads[block]:
            copy.wait()
        stack(block, 0)
        x = xs[block]
        for c in range(0, hpad, 256):
            wide = min(256, hpad - c)
            gate = mm(x, w_ref[:, c : c + wide])
            up = mm(x, w_ref[:, hpad + c : hpad + c + wide])
            act, slope, gelu = gelu_parts(gate, up)
            act_s[block, :, c : c + wide] = act.astype(BF)
            slope_s[block, :, c : c + wide] = slope.astype(BF)
            gelu_s[block, :, c : c + wide] = gelu.astype(BF)
        for n in (1, 2, 3):
            stack(block, n)
        part_s[block] = mm_nt(act_s[block], w_ref[:, 2 * hpad :]).astype(BF)
        for b, at, row, ref in ffn_layout(part_refs, layout):
            if b == block:
                src = part_s.at[block, pl.ds(row, ref.shape[0]), :]
                copy = pltpu.make_async_copy(src, ref, part_sem.at[at])
                copy.start()
                started.append(copy)
    for copy in started:
        copy.wait()


def ffn_back_kernel(*refs, layout, base, hpad):
    n_x, blocks = sum(layout), len(layout)
    x_refs, w_ref, saved_refs = refs[:n_x], refs[n_x], refs[n_x + 1 : n_x + 3]
    outs, scr = refs[-(11 + n_x) : -9], refs[-9:]
    all_refs, part_refs = outs[:2], outs[2:]
    xs, dgu_s, slope_s, gelu_s, part_s, x_sem, out_sem, part_sem, saved_sem = scr
    rows = xs.shape[1]
    stage = (xs, dgu_s)
    loads, started = [[] for _ in range(blocks)], []

    def saved(block, n):
        src = saved_refs[n].at[pl.ds((base + block) * rows, rows), :]
        dst = (slope_s, gelu_s)[n].at[block]
        copy = pltpu.make_async_copy(src, dst, saved_sem.at[block, n])
        copy.start()
        loads[block].append(copy)

    for block, at, row, ref in ffn_layout(x_refs, layout):
        dst = xs.at[block, pl.ds(row, ref.shape[0]), :]
        copy = pltpu.make_async_copy(ref, dst, x_sem.at[at])
        copy.start()
        loads[block].append(copy)
        if row == 0:
            saved(block, 0)
            saved(block, 1)

    def stack(block, n):
        dst = all_refs[n].at[pl.ds((base + block) * rows, rows), :]
        copy = pltpu.make_async_copy(stage[n].at[block], dst, out_sem.at[block, n])
        copy.start()
        started.append(copy)

    for block in range(blocks):
        for copy in loads[block]:
            copy.wait()
        stack(block, 0)
        dout = xs[block]
        for c in range(0, hpad, 256):
            wide = min(256, hpad - c)
            d_act = mm(dout, w_ref[:, 2 * hpad + c : 2 * hpad + c + wide])
            slope = slope_s[block, :, c : c + wide].astype(F32)
            gelu = gelu_s[block, :, c : c + wide].astype(F32)
            dgu_s[block, :, c : c + wide] = (d_act * slope).astype(BF)
            dgu_s[block, :, hpad + c : hpad + c + wide] = (d_act * gelu).astype(BF)
        stack(block, 1)
        part_s[block] = mm_nt(dgu_s[block], w_ref[:, : 2 * hpad]).astype(BF)
        for b, at, row, ref in ffn_layout(part_refs, layout):
            if b == block:
                src = part_s.at[block, pl.ds(row, ref.shape[0]), :]
                copy = pltpu.make_async_copy(src, ref, part_sem.at[at])
                copy.start()
                started.append(copy)
    for copy in started:
        copy.wait()


def hold_kernel(src_ref, dst_ref, sem):
    copy = pltpu.make_async_copy(src_ref, dst_ref, sem.at[0])
    copy.start()
    copy.wait()


def hold(value):
    return pl.pallas_call(
        hold_kernel,
        out_shape=pltpu.VMEM(value.shape, value.dtype),
        in_specs=[pl.BlockSpec(memory_space=pltpu.HBM)],
        out_specs=pl.BlockSpec(memory_space=pltpu.VMEM),
        scratch_shapes=[pltpu.SemaphoreType.DMA((1,))],
        compiler_params=pltpu.CompilerParams(vmem_limit_bytes=16 << 20),
        cost_estimate=price(3, 1000000),
    )(in_hbm(value))


def in_hbm(value):
    return pltpu.with_memory_space_constraint(value, pltpu.HBM)


def ffn_call(kernel, blocks, base, saved, w_ffn, bufs):
    pieces = [piece for block in blocks for piece in block]
    layout = tuple(len(block) for block in blocks)
    n, back = len(blocks), bool(saved)
    width, hpad = w_ffn.shape[0], w_ffn.shape[1] // 3
    rows = sum(piece.shape[0] for piece in blocks[0])
    widths = [width, 2 * hpad] if back else [width, hpad, hpad, hpad]
    ins = [in_hbm(v) for v in pieces] + [w_ffn] + [in_hbm(v) for v in saved]
    aliases = {}
    if bufs is not None:
        aliases = {len(ins) + k: k for k in range(len(widths))}
        ins = ins + [in_hbm(v) for v in bufs]
    hbm = pl.BlockSpec(memory_space=pltpu.HBM)
    in_specs = [hbm] * len(ins)
    in_specs[len(pieces)] = pl.BlockSpec(memory_space=pltpu.VMEM)
    shapes = [((8 * rows, w), BF) for w in widths] + [(piece.shape, BF) for piece in pieces]
    mid = [2 * hpad, hpad, hpad] if back else [hpad, hpad, hpad]
    scratch = [pltpu.VMEM((n, rows, w), BF) for w in [width] + mid + [width]]
    scratch += [
        pltpu.SemaphoreType.DMA((len(pieces),)),
        pltpu.SemaphoreType.DMA((n, 4)),
        pltpu.SemaphoreType.DMA((len(pieces),)),
        pltpu.SemaphoreType.DMA((n, 2)),
    ]
    outs = pl.pallas_call(
        partial(kernel, layout=layout, base=base, hpad=hpad),
        out_shape=[pltpu.HBM(shape, dtype) for shape, dtype in shapes],
        in_specs=in_specs,
        out_specs=[hbm] * len(shapes),
        scratch_shapes=scratch,
        input_output_aliases=aliases,
        compiler_params=pltpu.CompilerParams(vmem_limit_bytes=28 << 20),
        cost_estimate=price(6 * n, 1000000 * n),
    )(*ins)
    grouped, at = [], len(widths)
    for count in layout:
        grouped.append(tuple(outs[at : at + count]))
        at += count
    return outs[: len(widths)], grouped


def ffn_mid_kernel(*refs):
    hid_ref, cot_ref, gains_ref, out_ref, dout_ref, gain_ref = refs[6:]
    part = piece_sum(refs[:6])
    gain = gains_ref[3:4, :]
    factor = lax.rsqrt(jnp.mean(part * part, -1, keepdims=True) + EPS)
    out_ref[...] = (hid_ref[...] + part * factor * gain).astype(BF)
    back, gain_grad = norm_back_tile(part, gain, cot_ref[...].astype(F32))
    dout_ref[...] = back.astype(BF)
    gain_ref[0:1, :] = gain_grad


def norm_back_tile(raw, gain, upstream):
    factor = lax.rsqrt(jnp.mean(raw * raw, -1, keepdims=True) + EPS)
    normed = raw * factor
    gain_grad = jnp.sum(upstream * normed, axis=0, keepdims=True)
    scaled = upstream * gain
    back = factor * (scaled - normed * jnp.mean(scaled * normed, -1, keepdims=True))
    return back, gain_grad


def mid_kernel(*refs):
    hid_ref, part_ref, cot_ref, gains_ref = refs[6:10]
    w_refs, (dhid_ref, dpart_ref, dhead_ref, gain_ref) = refs[10:20], refs[20:]
    din = piece_sum(refs[:6])
    extra, gain_ffn = norm_back_tile(hid_ref[...], gains_ref[2:3, :], din)
    dhid = cot_ref[...].astype(F32) + extra
    dhid_ref[...] = dhid
    dpart, gain_post = norm_back_tile(part_ref[...], gains_ref[1:2, :], dhid)
    dpart = dpart.astype(BF)
    dpart_ref[...] = dpart
    gain_ref[0:1, :] = gain_ffn
    gain_ref[1:2, :] = gain_post
    pairs = split_w(w_refs, w_refs[6].shape[0])
    for r in range(4):
        dhead_ref[r] = mm_split(dpart, head_w(pairs, r)).astype(BF)


def attn_back_kernel(
    need,
    q_ref,
    k2_ref,
    kp_ref,
    ko_ref,
    bias_ref,
    o_ref,
    do_ref,
    linv_ref,
    qn_ref,
    fac_ref,
    cos_ref,
    sin_ref,
    gq_ref,
    dq_ref,
    d2_ref,
    dp_ref,
    down_ref,
    gain_ref,
    acc_ref,
    dkv_ref,
):
    i = pl.program_id(0)
    tile = q_ref.shape[1]

    @pl.when(i == 0)
    def _():
        dkv_ref[...] = jnp.zeros_like(dkv_ref)
        gain_ref[...] = jnp.zeros_like(gain_ref)

    acc_ref[...] = jnp.zeros_like(acc_ref)
    q = q_ref[...].reshape(4 * tile, HD)
    do = do_ref[...].reshape(4 * tile, HD)
    linv = linv_ref[...].reshape(4 * tile, 128)[:, 0:1]
    inner = jnp.sum(do.astype(F32) * o_ref[...].reshape(4 * tile, HD).astype(F32), -1, keepdims=True)
    for kb in range(6):

        @pl.when(need[i * 6 + kb] > 0)
        def _(kb=kb):
            kv = kv_block((k2_ref, kp_ref, ko_ref), kb)
            keys, vals = kv[:, :HD], kv[:, HD:]
            s = mm_nt(q, keys).reshape(4, tile, 256) * HD ** (-0.5)
            p = jnp.exp(s + bias_ref[:, kb * 256 : (kb + 1) * 256][None])
            p = p.reshape(4 * tile, 256) * linv
            dp = mm_nt(do, vals)
            ds = (p * (dp - inner)).astype(BF)
            acc_ref[...] += mm(ds, keys)
            span = slice(kb * 256, (kb + 1) * 256)
            dkv_ref[span, :HD] += mm_tn(ds, q)
            dkv_ref[span, HD:] += mm_tn(p.astype(BF), do)

    cos, sin = cos_ref[...], sin_ref[...]
    gain = jnp.zeros((1, HD), F32)
    for r in range(4):
        dq = acc_ref[r * tile : (r + 1) * tile, :] * HD ** (-0.5)
        own, oth = dq[:, :128], dq[:, 128:]
        back = jnp.concatenate([own * cos + oth * sin, oth * cos - own * sin], axis=1)
        norm = qn_ref[r].astype(F32)
        gain += jnp.sum(back * norm, axis=0, keepdims=True)
        scaled = back * gq_ref[4:5, :]
        mean = jnp.mean(scaled * norm, -1, keepdims=True)
        dq_ref[r] = (fac_ref[:, r : r + 1] * (scaled - norm * mean)).astype(BF)
    gain_ref[0:1, :] += gain

    @pl.when(i == pl.num_programs(0) - 1)
    def _():
        rows = d2_ref.shape[0]
        scale = HD ** (-0.5)
        for n, ref in enumerate((d2_ref, dp_ref, down_ref)):
            block = dkv_ref[n * rows : (n + 1) * rows, :]
            ref[:, :HD] = (block[:, :HD] * scale).astype(ref.dtype)
            ref[:, HD:] = block[:, HD:].astype(ref.dtype)


def post_kernel(
    flags,
    dq_ref,
    dkv_ref,
    dp_ref,
    kn_ref,
    fac_ref,
    cos_ref,
    sin_ref,
    gk_ref,
    x_ref,
    gains_ref,
    dhid_ref,
    gq_grad,
    mid_grad,
    post_grad,
    place_ref,
    *refs,
):
    w_refs, din_ref, kvraw_ref, gain_ref = refs[:10], *refs[10:]
    fi, ty, tc = (flags[n].astype(F32) for n in range(3))
    dkv = dkv_ref[...] + dp_ref[...].astype(F32)
    cos, sin = cos_ref[...], sin_ref[...]
    own, oth = dkv[:, :128], dkv[:, 128:256]
    back = jnp.concatenate([own * cos + oth * sin, oth * cos - own * sin], axis=1)
    norm = kn_ref[...].astype(F32)
    gk_grad = jnp.sum(back * norm, axis=0, keepdims=True)
    scaled = back * gk_ref[5:6, :]
    mean = jnp.mean(scaled * norm, -1, keepdims=True)
    dkey = fac_ref[:, 4:5] * (scaled - norm * mean)
    dval = dkv[:, 256:]
    kvraw_ref[...] = jnp.concatenate([dkey, dval], axis=1).astype(BF)
    din = jnp.zeros(din_ref.shape, F32)
    zeros = jnp.zeros((dkv.shape[0], 64), F32)
    pairs = split_w(w_refs, w_refs[6].shape[0])
    rel = 0
    for dx in range(2):
        kh = dkey[:, dx * 128 : (dx + 1) * 128]
        vh = dval[:, dx * 128 : (dx + 1) * 128]
        for dy in range(2):
            half = mix(ty, kh, vh) if dy == 0 else mix(ty, vh, kh)
            for dc in range(2):
                lo, hi = half[:, :64], half[:, 64:]
                part = mix(tc, lo, hi) if dc == 0 else mix(tc, hi, lo)
                side = jnp.concatenate([part, zeros], axis=1).astype(BF)
                dprod = jnp.concatenate(
                    [dq_ref[dy * 2 + dc][:, dx * 128 : (dx + 1) * 128], side], axis=1
                )
                din += mm_nt_split(dprod, pairs[rel])
                rel += 1
    x = x_ref[...].astype(F32)
    extra, gain_pre = norm_back_tile(x, gains_ref[0:1, :], din)
    din_ref[...] = dhid_ref[...] + extra

    def spread(grad):
        own, oth = grad[:, :128], grad[:, 128:]
        whole_row = jnp.concatenate([mix(fi, own, oth), mix(fi, oth, own)], axis=1)
        return mm(jnp.broadcast_to(whole_row.astype(BF), (8, HD)), place_ref[...])[0:1, :]

    gain_ref[...] = jnp.zeros_like(gain_ref)
    gain_ref[0:1, :] = gain_pre
    gain_ref[1:2, :] = mid_grad[1:2, :]
    gain_ref[2:3, :] = mid_grad[0:1, :]
    gain_ref[3:4, :] = post_grad[0:1, :]
    gain_ref[4:5, :] = spread(gq_grad[0:1, :])
    gain_ref[5:6, :] = spread(gk_grad)


def store_rows(refs, value):
    cut = refs[0].shape[0]
    refs[0][...] = value[:cut, :]
    refs[1][...] = value[cut:, :]


def qo_grad_kernel(xin, xin_c, dq, dq_c, dpart, dpart_c, head, head_c, *outs):
    xt, xt_c, dt, dt_c = (ref[...].T for ref in (xin, xin_c, dpart, dpart_c))
    for dy in range(2):
        gq = (mm(xt, dq[2 * dy]) + mm(xt_c, dq_c[dy])).astype(BF)
        go = (mm(dt, head[2 * dy]) + mm(dt_c, head_c[dy])).astype(BF)
        for dx in range(2):
            half = slice(dx * 128, (dx + 1) * 128)
            at = 4 * dx + 2 * dy
            store_rows(outs[at : at + 2], jnp.concatenate([gq[:, half], go[:, half]], axis=1))


def kv_grad_kernel(flags, xin, xin_c, kv, kv_c, gain, gain_c, *refs):
    outs, rows_ref = refs[:8], refs[8]
    ty, tc = flags[1].astype(F32), flags[2].astype(F32)
    rows_ref[...] = jnp.zeros_like(rows_ref)
    rows_ref[64:72, :] = gain[...] + gain_c[...]
    gain_cols = rows_ref[...].T
    xt, xt_c = xin[...].T, xin_c[...].T

    def sides(ref):
        block = ref[...].astype(F32)
        picked = []
        for dy in range(2):
            for dx in range(2):
                kh = block[:, dx * 128 : (dx + 1) * 128]
                vh = block[:, 256 + dx * 128 : 256 + (dx + 1) * 128]
                half = mix(ty, kh, vh) if dy == 0 else mix(ty, vh, kh)
                picked.append(mix(tc, half[:, :64], half[:, 64:]))
        return jnp.concatenate(picked, axis=1).astype(BF)

    grad = mm(xt, sides(kv)) + mm(xt_c, sides(kv_c))
    zeros = jnp.zeros((grad.shape[0], 64), F32)
    for dy in range(2):
        for dx in range(2):
            at = 4 * dx + 2 * dy
            col = (2 * dy + dx) * 64
            part = jnp.concatenate([grad[:, col : col + 64], zeros], axis=1) + gain_cols
            store_rows(outs[at : at + 2], part.astype(BF))


def chip_reduce(parts):
    own, near_y, near_x, far = (parts[n : n + 2] for n in (0, 2, 4, 6))
    from_x, from_y = swap(far[0], "fi"), swap(far[1], "ty")
    got_x_top, got_y_bot = swap(near_x[0], "fi"), swap(near_y[1], "ty")
    x_bot = (near_x[1].astype(F32) + from_y.astype(F32)).astype(BF)
    y_top = (near_y[0].astype(F32) + from_x.astype(F32)).astype(BF)
    return (*own, got_x_top, swap(x_bot, "fi"), swap(y_top, "ty"), got_y_bot)


def gather_sum_kernel(*refs):
    out_ref = refs[12]
    for n, cols in ((0, slice(0, 256)), (6, slice(256, 384))):
        own_top, own_bot, x_top, x_bot, y_top, y_bot = (ref[...].astype(F32) for ref in refs[n : n + 6])
        cut = own_top.shape[0]
        out_ref[:cut, cols] = (own_top + x_top + y_top).astype(BF)
        out_ref[cut:, cols] = (own_bot + x_bot + y_bot).astype(BF)


def pad_cols(value, width):
    return jnp.pad(value, ((0, 0), (0, width - value.shape[1])))


def body(
    tokens,
    positions,
    segments,
    w_query,
    w_key,
    w_value,
    w_out,
    w_gate,
    w_up,
    w_down,
    gain_attn_pre,
    gain_query,
    gain_key,
    gain_attn_post,
    gain_ffn_pre,
    gain_ffn_post,
    cotangent,
):
    fi = lax.axis_index("fi")
    ty = lax.axis_index("ty")
    tc = lax.axis_index("tc")
    t_idx = ty * 2 + tc
    me = fi * 4 + t_idx
    first = fi == 0
    rows = tokens.shape[0]
    width = tokens.shape[1]
    shard = w_query.shape[0]
    nf = width // shard
    hid = w_gate.shape[1] // 2
    hpad = -(-hid // 128) * 128
    gshard = gain_query.shape[0]

    def pair_rows(keep, recv):
        return jnp.where(
            first,
            jnp.concatenate([keep, recv], axis=0),
            jnp.concatenate([recv, keep], axis=0),
        )

    kv_mine = jnp.where(ty == 0, w_key, w_value)
    out_t = w_out.T
    gains = pad_cols(
        jnp.stack(
            [
                gain_attn_pre,
                gain_attn_post,
                gain_ffn_pre,
                gain_ffn_post,
                jnp.pad(gain_query, (0, shard - gshard)),
                jnp.pad(gain_key, (0, shard - gshard)),
            ],
            axis=1,
        ),
        64,
    )

    def piece(h):
        kv_half = kv_mine[:, h * 128 : (h + 1) * 128]
        kv_part = jnp.where(tc == 0, kv_half[:, :64], kv_half[:, 64:])
        return jnp.concatenate(
            [
                w_query[:, h * 128 : (h + 1) * 128],
                kv_part,
                gains,
                out_t[:, h * 128 : (h + 1) * 128],
            ],
            axis=1,
        )

    piece0, piece1 = piece(0), piece(1)
    keep = jnp.where(first, piece0, piece1)
    recv = swap(jnp.where(first, piece1, piece0), "fi")

    down_t = w_down.T

    def halves(weight):
        lo, hi = pad_cols(weight[:, :hid], hpad), pad_cols(weight[:, hid:], hpad)
        return jnp.where(first, lo, hi), jnp.where(first, hi, lo)

    gate_keep, gate_send = halves(w_gate)
    up_keep, up_send = halves(w_up)
    down_keep, down_send = halves(down_t)
    ffn_keep = jnp.concatenate([gate_keep, up_keep, down_keep], axis=1)
    ffn_send = jnp.concatenate([gate_send, up_send, down_send], axis=1)
    ffn_send, ffn_keep, recv = lax.optimization_barrier((ffn_send, ffn_keep, recv))
    ffn_recv = swap(ffn_send, "fi")
    attn_col = lax.all_gather(pair_rows(keep, recv), "fo", axis=0, tiled=True)
    attn_col, ffn_pair = lax.optimization_barrier((attn_col, pair_rows(ffn_keep, ffn_recv)))
    w_ffn = lax.all_gather(ffn_pair, "fo", axis=0, tiled=True)

    elem = lax.broadcasted_iota(jnp.int32, (HD, width), 0)
    spot = lax.broadcasted_iota(jnp.int32, (HD, width), 1)
    place = (spot == (elem // gshard) * shard + elem % gshard).astype(BF)
    cut = width // 256 * 128
    row_start = t_idx * rows
    pos_local = lax.dynamic_slice_in_dim(positions, row_start, rows)
    seg_local = lax.dynamic_slice_in_dim(segments, row_start, rows)

    def block_of(meta, back):
        return lax.dynamic_slice_in_dim(meta, ((t_idx - back) % 4) * rows, rows)

    k_pos = jnp.concatenate([block_of(positions, 2), block_of(positions, 1), pos_local])
    k_seg = jnp.concatenate(
        [
            jnp.where(t_idx == 3, block_of(segments, 2), -1),
            jnp.where(t_idx >= 1, block_of(segments, 1), -1),
            seg_local,
        ]
    )
    allowed = (
        ((k_seg[None, :] == 0) | (k_seg[None, :] == seg_local[:, None]))
        & (k_pos[None, :] <= pos_local[:, None])
        & (pos_local[:, None] - k_pos[None, :] < WINDOW)
    )
    bias = jnp.where(allowed, 0.0, NEG).astype(F32)
    need = jnp.any(allowed.reshape(4, rows // 4, 6, rows // 2), axis=(1, 3))
    need = need.astype(jnp.int32).reshape(24)
    frequency = jnp.exp(-math.log(BASE) * jnp.arange(HALF).astype(F32) / HALF)
    angles = pos_local.astype(F32)[:, None] * frequency
    cosine = jnp.cos(angles)
    sine = jnp.sin(angles) * jnp.where(first, 1.0, -1.0)

    w_parts, (bias, need, cosine, sine, place) = plane_gather(
        attn_col, cut, (bias, need, cosine, sine, place)
    )
    w_parts = [in_hbm(piece) for pieces in w_parts for piece in pieces]
    flags = jnp.stack([fi, ty, tc]).astype(jnp.int32)
    qkv_spec = [pl.BlockSpec((part.shape[0], 256), lambda *_: (0, 0)) for part in w_parts]
    wo_spec = [pl.BlockSpec((part.shape[0], 128), lambda *_: (0, 2)) for part in w_parts]
    full, gains8 = whole((rows, width)), whole((8, width))
    heads = whole((4, rows, HD))
    lanes = whole((rows, 128))
    kv_full = whole((rows, 2 * HD))
    attn_in, q_rot, q_norm, kv_own, k_norm, factors, gain_rows, head_gains = run(
        qkv_kernel,
        [
            ((rows, width), BF),
            ((4, rows, HD), BF),
            ((4, rows, HD), BF),
            ((rows, 2 * HD), BF),
            ((rows, HD), BF),
            ((rows, 128), F32),
            ((8, width), F32),
            ((8, HD), F32),
        ],
        (flags, tokens, place, cosine, sine, *w_parts),
        9,
        grid=(1,),
        in_specs=[full, whole((HD, width)), lanes, lanes] + qkv_spec,
        out_specs=[full, heads, heads, kv_full, whole((rows, HD)), lanes, gains8, whole((8, HD))],
        prefetch=1,
    )
    kv_prev = lax.ppermute(kv_own, ("ty", "tc"), [(i, (i + 1) % 4) for i in range(4)])
    kv_two = swap(kv_prev, "tc")
    tile = rows // 4
    q_tile = pl.BlockSpec((4, tile, HD), lambda i, *_: (0, i, 0))
    l_tile = pl.BlockSpec((4, tile, 128), lambda i, *_: (0, i, 0))
    bias_tile = pl.BlockSpec((tile, 3 * rows), lambda i, *_: (i, 0))
    head_out, linv = run(
        attn_kernel,
        [((4, rows, HD), BF), ((4, rows, 128), F32)],
        (need, q_rot, kv_two, kv_prev, kv_own, bias),
        8,
        grid=(4,),
        in_specs=[q_tile, kv_full, kv_full, kv_full, bias_tile],
        out_specs=[q_tile, l_tile],
        scratch=[pltpu.VMEM((4 * tile, HD), F32), pltpu.VMEM((4 * tile, 128), F32)],
        prefetch=1,
    )
    attn_part, hidden, ffn_local = run(
        out_kernel,
        [((rows, width), F32), ((rows, width), F32), ((rows, width), BF)],
        (head_out, tokens, gain_rows, *w_parts),
        6,
        grid=(1,),
        in_specs=[heads, full, gains8] + wo_spec,
        out_specs=[full, full, full],
    )

    half = rows // 2
    def far_pieces(top, bot, after):
        top, bot, after = lax.optimization_barrier((top, bot, after))
        return [(top, bot), (swap(top, "tc"), swap(bot, "tc"))], after

    by_x, by_y, by_c = swap(ffn_local, "fi"), swap(ffn_local, "ty"), swap(ffn_local, "tc")
    top, bot = swap(by_y[:half], "fi"), swap(by_x[half:], "ty")
    by_xc, by_yc = swap(by_x, "tc"), swap(by_y, "tc")
    w_ffn = hold(w_ffn)
    bufs, parts_x = ffn_call(ffn_kernel, [(by_x,), (by_xc,)], 2, [], w_ffn, None)
    far, parts_x = far_pieces(top, bot, parts_x)
    bufs, parts_f = ffn_call(ffn_kernel, far, 6, [], w_ffn, bufs)
    bufs, parts_y = ffn_call(ffn_kernel, [(by_y,), (by_yc,)], 4, [], w_ffn, bufs)
    got = far_swap(far_sum(*parts_f, half))
    near = near_swap(parts_y, parts_x, half)
    ffn_local, got = lax.optimization_barrier((ffn_local, got))
    bufs, parts_o = ffn_call(ffn_kernel, [(ffn_local,)], 0, [], w_ffn, bufs)
    by_c, near, parts_o = lax.optimization_barrier((by_c, near, parts_o))
    (x_all, act_all, slope_all, gelu_all), parts_c = ffn_call(
        ffn_kernel, [(by_c,)], 1, [], w_ffn, bufs
    )
    pieces = plane_finish(parts_o + parts_c, half, got, near)
    quarter = whole((half, width))
    piece_spec = [full, full] + [quarter] * 4

    other = swap(jnp.stack([head_out[1], head_out[3]]), "tc"), swap(attn_in, "tc")
    pieces, (head_out_c, attn_in_c) = lax.optimization_barrier((pieces, other))
    output, d_local, ffn_post_grad = run(
        ffn_mid_kernel,
        [((rows, width), BF), ((rows, width), BF), ((8, width), F32)],
        (*pieces, hidden, cotangent, gain_rows),
        6,
        grid=(1,),
        in_specs=piece_spec + [full, full, gains8],
        out_specs=[full, full, gains8],
    )
    by_x, by_y, by_c = swap(d_local, "fi"), swap(d_local, "ty"), swap(d_local, "tc")
    saved = [slope_all, gelu_all]
    bufs, parts_o = ffn_call(ffn_back_kernel, [(d_local,), (by_c,)], 0, saved, w_ffn, None)
    by_x, by_y, parts_o = lax.optimization_barrier((by_x, by_y, parts_o))
    top, bot = swap(by_y[:half], "fi"), swap(by_x[half:], "ty")
    by_xc, by_yc = swap(by_x, "tc"), swap(by_y, "tc")
    bufs, parts_x = ffn_call(ffn_back_kernel, [(by_x,), (by_xc,)], 2, saved, w_ffn, bufs)
    far, parts_x = far_pieces(top, bot, parts_x)
    bufs, parts_f = ffn_call(ffn_back_kernel, far, 6, saved, w_ffn, bufs)
    (d_all, dgu_all), parts_y = ffn_call(
        ffn_back_kernel, [(by_y,), (by_yc,)], 4, saved, w_ffn, bufs
    )
    got = far_swap(far_sum(*parts_f, half))
    pieces = plane_finish(parts_o, half, got, near_swap(parts_y, parts_x, half))
    grad_dt = dot_left_t(d_all, act_all).astype(BF)
    dgu_all, grad_dt = lax.optimization_barrier((dgu_all, grad_dt))
    grad_gu = dot_left_t(x_all, dgu_all).astype(BF)
    pieces, grad_gu = lax.optimization_barrier((pieces, grad_gu))
    sum_dt = lax.psum_scatter(grad_dt, "fo", scatter_dimension=0, tiled=True)
    sum_gu = lax.psum_scatter(grad_gu, "fo", scatter_dimension=0, tiled=True)

    def unpair(summed):
        top_rows, bot_rows = summed[:shard], summed[shard:]
        mine = jnp.where(first, top_rows, bot_rows)
        theirs = swap(jnp.where(first, bot_rows, top_rows), "fi")
        return jnp.where(first, mine, theirs), jnp.where(first, theirs, mine)

    def join(lo, hi):
        return jnp.concatenate([lo[:, :hid], hi[:, :hid]], axis=1).astype(F32)

    hidden_grad, attn_part_grad, head_grad, mid_gains = run(
        mid_kernel,
        [((rows, width), F32), ((rows, width), BF), ((4, rows, HD), BF), ((8, width), F32)],
        (*pieces, hidden, attn_part, cotangent, gain_rows, *w_parts),
        10,
        grid=(1,),
        in_specs=piece_spec + [full, full, full, gains8] + wo_spec,
        out_specs=[full, full, heads, whole((8, width))],
    )
    fac_tile = pl.BlockSpec((tile, 128), lambda i, *_: (i, 0))
    line = whole((8, HD))
    q_raw_grad, kv_grad_two, kv_grad_prev, kv_grad_own, gain_q = run(
        attn_back_kernel,
        [
            ((4, rows, HD), BF),
            ((rows, 2 * HD), BF),
            ((rows, 2 * HD), BF),
            ((rows, 2 * HD), F32),
            ((8, HD), F32),
        ],
        (
            need,
            q_rot,
            kv_two,
            kv_prev,
            kv_own,
            bias,
            head_out,
            head_grad,
            linv,
            q_norm,
            factors,
            cosine,
            sine,
            head_gains,
        ),
        12,
        grid=(4,),
        in_specs=[
            q_tile,
            kv_full,
            kv_full,
            kv_full,
            bias_tile,
            q_tile,
            q_tile,
            l_tile,
            q_tile,
            fac_tile,
            fac_tile,
            fac_tile,
            line,
        ],
        out_specs=[q_tile, kv_full, kv_full, kv_full, whole((8, HD))],
        scratch=[pltpu.VMEM((4 * tile, HD), F32), pltpu.VMEM((3 * rows, 2 * HD), F32)],
        prefetch=1,
    )
    back_two = kv_grad_prev.astype(F32) + swap(kv_grad_two, "tc").astype(F32)
    q_raw_grad, back_two = lax.optimization_barrier((q_raw_grad, back_two.astype(BF)))
    back_prev = lax.ppermute(back_two, ("ty", "tc"), [(i, (i + 3) % 4) for i in range(4)])
    def row_pieces(cols):
        return [((n, cols), BF) for n in (cut, width - cut)] * 4

    other_heads = lambda value: swap(jnp.stack([value[1], value[3]]), "tc")
    two_heads = whole((2, rows, HD))
    qo_grads = run(
        qo_grad_kernel,
        row_pieces(256),
        (
            attn_in,
            attn_in_c,
            q_raw_grad,
            other_heads(q_raw_grad),
            attn_part_grad,
            swap(attn_part_grad, "tc"),
            head_out,
            head_out_c,
        ),
        5,
        grid=(1,),
        in_specs=[full, full, heads, two_heads, full, full, heads, two_heads],
        out_specs=[whole(shape) for shape, _ in row_pieces(256)],
    )
    back_prev, sum_dt = lax.optimization_barrier((back_prev, sum_dt))
    qo_pieces = chip_reduce(qo_grads)
    input_grad, kv_raw_grad, gain_grads = run(
        post_kernel,
        [((rows, width), F32), ((rows, 2 * HD), BF), ((8, width), F32)],
        (
            flags,
            q_raw_grad,
            kv_grad_own,
            back_prev,
            k_norm,
            factors,
            cosine,
            sine,
            head_gains,
            tokens,
            gain_rows,
            hidden_grad,
            gain_q,
            mid_gains,
            ffn_post_grad,
            place,
            *w_parts,
        ),
        9,
        grid=(1,),
        in_specs=[heads, kv_full, kv_full, whole((rows, HD)), lanes, lanes, lanes, line]
        + [full, gains8, full, whole((8, HD)), gains8, gains8]
        + [whole((HD, width))]
        + qkv_spec,
        out_specs=[full, kv_full, gains8],
        prefetch=1,
    )
    kv_grads = run(
        kv_grad_kernel,
        row_pieces(128),
        (
            flags,
            attn_in,
            attn_in_c,
            kv_raw_grad,
            swap(kv_raw_grad, "tc"),
            gain_grads,
            swap(gain_grads, "tc"),
        ),
        3,
        grid=(1,),
        in_specs=[full, full, kv_full, kv_full, gains8, gains8],
        out_specs=[whole(shape) for shape, _ in row_pieces(128)],
        scratch=[pltpu.VMEM((128, width), F32)],
        prefetch=1,
    )
    kv_pieces = chip_reduce(kv_grads)
    qo_pieces, kv_pieces, sum_gu = lax.optimization_barrier((qo_pieces, kv_pieces, sum_gu))
    (attn_grads,) = run(
        gather_sum_kernel,
        [((width, 384), BF)],
        (*qo_pieces, *kv_pieces),
        2,
        grid=(1,),
        in_specs=[whole(piece.shape) for piece in (*qo_pieces, *kv_pieces)],
        out_specs=[whole((width, 384))],
    )
    sum_attn = lax.psum_scatter(attn_grads, "fo", scatter_dimension=0, tiled=True)
    dt_lo, dt_hi = unpair(sum_dt)
    gu_lo, gu_hi = unpair(sum_gu)
    grad_gate = join(gu_lo[:, :hpad], gu_hi[:, :hpad])
    grad_up = join(gu_lo[:, hpad:], gu_hi[:, hpad:])
    grad_down = join(dt_lo, dt_hi).T

    a_lo, a_hi = unpair(sum_attn)
    grad_out = jnp.concatenate([a_lo[:, 128:256], a_hi[:, 128:256]], axis=1).astype(F32).T
    grad_query = jnp.concatenate([a_lo[:, :128], a_hi[:, :128]], axis=1).astype(F32)
    kv_part = jnp.concatenate([a_lo[:, 256:320], a_hi[:, 256:320]], axis=1)
    others = [
        lax.ppermute(kv_part, ("ty", "tc"), [(i, i ^ step) for i in range(4)]) for step in (1, 2, 3)
    ]
    row_here = jnp.where(tc == 0, 0, 1)

    def kv_lines(near, far):
        even = jnp.where(row_here == 0, near, far)
        odd = jnp.where(row_here == 0, far, near)
        return jnp.concatenate([even[:, :64], odd[:, :64], even[:, 64:], odd[:, 64:]], axis=1)

    kv_here, kv_far = kv_lines(kv_part, others[0]), kv_lines(others[1], others[2])
    grad_key = jnp.where(ty == 0, kv_here, kv_far).astype(F32)
    grad_value = jnp.where(ty == 0, kv_far, kv_here).astype(F32)
    gain_out = a_lo[:, 320:328].astype(F32).T
    return (
        output.astype(BF),
        input_grad,
        grad_query,
        grad_key,
        grad_value,
        grad_out,
        grad_gate,
        grad_up,
        grad_down,
        gain_out[0],
        gain_out[4, :gshard],
        gain_out[5, :gshard],
        gain_out[1],
        gain_out[2],
        gain_out[3],
    )


def solution(mesh):
    nf, nt = mesh.shape["fsdp"], mesh.shape["tensor"]
    fine = Mesh(mesh.devices.reshape(nf // 2, 2, nt // 2, 2), ("fo", "fi", "ty", "tc"))
    f_axes, t_axes = ("fo", "fi"), ("ty", "tc")
    rows = P(f_axes + t_axes, None)
    col = P(f_axes, t_axes)
    flat = P(f_axes, None)
    out_w = P(t_axes, f_axes)
    vec = P(f_axes)
    in_specs = (rows, vec, vec, col, flat, flat, out_w, col, col, out_w) + (vec,) * 6 + (rows,)
    out_specs = (rows, rows, col, flat, flat, out_w, col, col, out_w) + (vec,) * 6
    return jax.shard_map(body, mesh=fine, in_specs=in_specs, out_specs=out_specs, check_vma=False)
```

```python
import math
from functools import partial

import jax
import jax.numpy as jnp
from jax import lax
from jax.experimental import pallas as pl
from jax.experimental.pallas import tpu as pltpu
from jax.sharding import Mesh, PartitionSpec as P

HD = 256
WINDOW = 512
PROMPT = 1024
CONT = 8
CLEN = 128


EPS = 1e-06
NEG = -1e30
BASE = 10000.0
HALF = HD // 2
BF = jnp.bfloat16
F32 = jnp.float32


def dot_left_t(left_op, right_op):
    return lax.dot_general(
        left_op, right_op, (((0,), (0,)), ((), ())), preferred_element_type=jnp.float32
    )


def swap(value, axis):
    return lax.ppermute(value, axis, [(0, 1), (1, 0)])


RELS = [(dx, dy, dc) for dx in (0, 1) for dy in (0, 1) for dc in (0, 1)]


def plane_gather(own, cut, side):
    by_x = swap(own, "fi")
    by_y = swap(own, "ty")
    by_c = swap(own, "tc")
    by_x, by_y, side = lax.optimization_barrier((by_x, by_y, side))
    diag_top = swap(by_y[:cut], "fi")
    diag_bot = swap(by_x[cut:], "ty")
    by_xc = swap(by_x, "tc")
    by_yc = swap(by_y, "tc")
    return [
        (own,),
        (by_c,),
        (by_y,),
        (by_yc,),
        (by_x,),
        (by_xc,),
        (diag_top, diag_bot),
        (swap(diag_top, "tc"), swap(diag_bot, "tc")),
    ], side


def core_add(mine, other):
    return mine.astype(F32) + swap(other, "tc").astype(F32)


def far_sum(far, far_c, cut):
    if len(far) == 1:
        far, far_c = (far[0][:cut], far[0][cut:]), (far_c[0][:cut], far_c[0][cut:])
    return core_add(far[0], far_c[0]).astype(BF), core_add(far[1], far_c[1]).astype(BF)


def far_swap(sent):
    return swap(sent[0], "fi"), swap(sent[1], "ty")


def near_first(parts_y, parts_x, cut):
    (near_y, near_yc), (near_x, near_xc) = parts_y, parts_x
    near_x, sib_x = near_x[0], swap(near_xc[0], "tc")
    near_y, sib_y = near_y[0], swap(near_yc[0], "tc")
    x_top = (near_x[:cut].astype(F32) + sib_x[:cut].astype(F32)).astype(BF)
    y_bot = (near_y[cut:].astype(F32) + sib_y[cut:].astype(F32)).astype(BF)
    return (near_x, sib_x, near_y, sib_y), (x_top, y_bot)


def near_second(rest, got, cut):
    near_x, sib_x, near_y, sib_y = rest
    x_bot = near_x[cut:].astype(F32) + sib_x[cut:].astype(F32) + got[1].astype(F32)
    y_top = near_y[:cut].astype(F32) + sib_y[:cut].astype(F32) + got[0].astype(F32)
    return x_bot.astype(BF), y_top.astype(BF)


def near_swap(first):
    return swap(first[0], "fi"), swap(first[1], "ty")


def plane_pieces(parts_o, first, second):
    own, own_c = parts_o
    return own[0], swap(own_c[0], "tc"), first[0], second[0], second[1], first[1]


def piece_sum(pieces):
    own, sib, x_top, x_bot, y_top, y_bot = (piece[...].astype(F32) for piece in pieces)
    cross = jnp.concatenate([x_top + y_top, x_bot + y_bot], axis=0)
    return own + sib + cross


def mix(flag, at_zero, at_one):
    return at_zero * (1.0 - flag) + at_one * flag


def nbytes(shapes):
    return sum(math.prod(shape) * jnp.dtype(dtype).itemsize for shape, dtype in shapes)


def price(us, moved):
    return pl.CostEstimate(flops=int(us * 1.0e9), transcendentals=0, bytes_accessed=moved)


def run(kernel, outs, ins, us, *, grid=(), in_specs=None, out_specs=None, scratch=(), prefetch=0):
    return pl.pallas_call(
        kernel,
        out_shape=[jax.ShapeDtypeStruct(shape, dtype) for shape, dtype in outs],
        grid_spec=pltpu.PrefetchScalarGridSpec(
            num_scalar_prefetch=prefetch,
            grid=grid,
            in_specs=in_specs,
            out_specs=out_specs,
            scratch_shapes=list(scratch),
        ),
        compiler_params=pltpu.CompilerParams(
            vmem_limit_bytes=44 << 20, dimension_semantics=("arbitrary",) * len(grid)
        ),
        cost_estimate=price(us, nbytes(outs) + nbytes([(v.shape, v.dtype) for v in ins])),
    )(*ins)


def whole(shape):
    return pl.BlockSpec(shape, lambda *_: (0,) * len(shape))


def mm(left, right):
    return jnp.dot(left, right, preferred_element_type=F32)


def mm_nt(left, right):
    return lax.dot_general(left, right, (((1,), (1,)), ((), ())), preferred_element_type=F32)


def mm_tn(left, right):
    return lax.dot_general(left, right, (((0,), (0,)), ((), ())), preferred_element_type=F32)


def qkv_kernel(flags, x_ref, place_ref, cos_ref, sin_ref, *refs):
    w_refs, (xin_ref, qrot_ref, qn_ref, kv_ref, kn_ref, fac_ref) = refs[:10], refs[10:16]
    gains_ref, heads_ref = refs[16:]
    fi, ty, tc = (flags[n].astype(F32) for n in range(3))
    gains_ref[...] = w_refs[0][:, 128:256].astype(F32).T[64:72, :]
    line = mm_nt(gains_ref[...].astype(BF), place_ref[...])
    lo, hi = line[:, :128], line[:, 128:]
    heads_ref[...] = jnp.concatenate([mix(fi, lo, hi), mix(fi, hi, lo)], axis=1)
    x = x_ref[...].astype(F32)
    x_factor = lax.rsqrt(jnp.mean(x * x, -1, keepdims=True) + EPS)
    xin = (x * x_factor * gains_ref[0:1, :]).astype(BF)
    xin_ref[...] = xin
    prod = [mm_split(xin, pair) for pair in split_w(w_refs, w_refs[6].shape[0])]
    cos, sin = cos_ref[...], sin_ref[...]
    rows = x.shape[0]
    lane = lax.broadcasted_iota(jnp.int32, (rows, 128), 1)
    factors = jnp.zeros((rows, 128), F32)

    def normed(own, oth, row):
        total = jnp.sum(own * own + oth * oth, -1, keepdims=True)
        factor = lax.rsqrt(total * (1.0 / HD) + EPS)
        own, oth = own * factor, oth * factor
        g_own = own * heads_ref[row : row + 1, :128]
        g_oth = oth * heads_ref[row : row + 1, 128:]
        rot = jnp.concatenate([g_own * cos - g_oth * sin, g_oth * cos + g_own * sin], axis=1)
        return jnp.concatenate([own, oth], axis=1), rot, factor

    for r in range(4):
        norm, rot, factor = normed(prod[r][:, :128], prod[4 + r][:, :128], 4)
        qn_ref[r] = norm.astype(BF)
        qrot_ref[r] = rot.astype(BF)
        factors = jnp.where(lane == r, factor, factors)
    keys, vals = [], []
    for dx in range(2):
        sides = []
        for dy in range(2):
            zero = prod[dx * 4 + dy * 2][:, 128:192]
            one = prod[dx * 4 + dy * 2 + 1][:, 128:192]
            sides.append(jnp.concatenate([mix(tc, zero, one), mix(tc, one, zero)], axis=1))
        keys.append(mix(ty, sides[0], sides[1]))
        vals.append(mix(ty, sides[1], sides[0]))
    norm, rot, factor = normed(keys[0], keys[1], 5)
    kn_ref[...] = norm.astype(BF)
    fac_ref[...] = jnp.where(lane == 4, factor, factors)
    kv_ref[...] = jnp.concatenate([rot, vals[0], vals[1]], axis=1).astype(BF)


def split_w(refs, cut):
    pairs = [(ref[:cut, :], ref[cut:, :]) for ref in refs[:6]]
    return pairs + [(refs[6][...], refs[7][...]), (refs[8][...], refs[9][...])]


def head_w(pairs, r):
    return tuple(jnp.concatenate([pairs[r][n], pairs[4 + r][n]], axis=1) for n in (0, 1))


def mm_split(left, pair):
    cut = pair[0].shape[0]
    return mm(left[:, :cut], pair[0]) + mm(left[:, cut:], pair[1])


def mm_nt_split(left, pair):
    return jnp.concatenate([mm_nt(left, pair[0]), mm_nt(left, pair[1])], axis=1)


def kv_block(refs, kb):
    start = (kb % 2) * 256
    return refs[kb // 2][start : start + 256, :]


def attn_kernel(need, q_ref, k2_ref, kp_ref, ko_ref, bias_ref, o_ref, linv_ref, acc_ref, l_ref):
    i = pl.program_id(0)
    acc_ref[...] = jnp.zeros_like(acc_ref)
    l_ref[...] = jnp.zeros_like(l_ref)
    tile = q_ref.shape[1]
    for kb in range(6):

        @pl.when(need[i * 6 + kb] > 0)
        def _(kb=kb):
            kv = kv_block((k2_ref, kp_ref, ko_ref), kb)
            q = q_ref[...].reshape(4 * tile, HD)
            s = mm_nt(q, kv[:, :HD]).reshape(4, tile, 256) * HD ** (-0.5)
            p = jnp.exp(s + bias_ref[:, kb * 256 : (kb + 1) * 256][None])
            p = p.reshape(4 * tile, 256)
            l_ref[...] += p[:, :128] + p[:, 128:]
            acc_ref[...] += mm(p.astype(BF), kv[:, HD:])

    linv = 1.0 / jnp.sum(l_ref[...], -1, keepdims=True)
    linv_ref[...] = jnp.broadcast_to(linv, (4 * tile, 128)).reshape(4, tile, 128)
    o_ref[...] = (acc_ref[...] * linv).astype(BF).reshape(4, tile, HD)


def out_kernel(o_ref, x_ref, gains_ref, *refs):
    w_refs, (part_ref, hid_ref, ffn_ref) = refs[:10], refs[10:]
    pairs = split_w(w_refs, w_refs[6].shape[0])
    part = jnp.zeros(part_ref.shape, F32)
    for r in range(4):
        part += mm_nt_split(o_ref[r], head_w(pairs, r))
    part_ref[...] = part
    factor = lax.rsqrt(jnp.mean(part * part, -1, keepdims=True) + EPS)
    hidden = x_ref[...].astype(F32) + part * factor * gains_ref[1:2, :]
    hid_ref[...] = hidden
    factor = lax.rsqrt(jnp.mean(hidden * hidden, -1, keepdims=True) + EPS)
    ffn_ref[...] = (hidden * factor * gains_ref[2:3, :]).astype(BF)


def gelu_parts(gate, up):
    c0 = math.sqrt(2.0 / math.pi)
    square = gate * gate
    th = jnp.tanh(gate * (c0 + (0.044715 * c0) * square))
    side = 0.5 + 0.5 * th
    gelu = gate * side
    slope = side + gelu * (1.0 - th) * (c0 + (3.0 * 0.044715 * c0) * square)
    return gelu * up, slope * up, gelu


def ffn_layout(refs, layout):
    at, groups = 0, []
    for block, count in enumerate(layout):
        row = 0
        for ref in refs[at : at + count]:
            groups.append((block, at, row, ref))
            row += ref.shape[0]
            at += 1
    return groups


def ffn_kernel(*refs, layout, base, hpad):
    n_x, blocks = sum(layout), len(layout)
    x_refs, w_ref = refs[:n_x], refs[n_x]
    outs, scr = refs[-(13 + n_x) : -9], refs[-9:]
    all_refs, part_refs = outs[:4], outs[4:]
    xs, act_s, slope_s, gelu_s, part_s, x_sem, out_sem, part_sem, _ = scr
    rows = xs.shape[1]
    stage = (xs, act_s, slope_s, gelu_s)
    loads, started = [[] for _ in range(blocks)], []
    for block, at, row, ref in ffn_layout(x_refs, layout):
        dst = xs.at[block, pl.ds(row, ref.shape[0]), :]
        copy = pltpu.make_async_copy(ref, dst, x_sem.at[at])
        copy.start()
        loads[block].append(copy)

    def stack(block, n):
        dst = all_refs[n].at[pl.ds((base + block) * rows, rows), :]
        copy = pltpu.make_async_copy(stage[n].at[block], dst, out_sem.at[block, n])
        copy.start()
        started.append(copy)

    for block in range(blocks):
        for copy in loads[block]:
            copy.wait()
        stack(block, 0)
        x = xs[block]
        for c in range(0, hpad, 256):
            wide = min(256, hpad - c)
            gate = mm(x, w_ref[:, c : c + wide])
            up = mm(x, w_ref[:, hpad + c : hpad + c + wide])
            act, slope, gelu = gelu_parts(gate, up)
            act_s[block, :, c : c + wide] = act.astype(BF)
            slope_s[block, :, c : c + wide] = slope.astype(BF)
            gelu_s[block, :, c : c + wide] = gelu.astype(BF)
        for n in (1, 2, 3):
            stack(block, n)
        part_s[block] = mm_nt(act_s[block], w_ref[:, 2 * hpad :]).astype(BF)
        for b, at, row, ref in ffn_layout(part_refs, layout):
            if b == block:
                src = part_s.at[block, pl.ds(row, ref.shape[0]), :]
                copy = pltpu.make_async_copy(src, ref, part_sem.at[at])
                copy.start()
                started.append(copy)
    for copy in started:
        copy.wait()


def ffn_back_kernel(*refs, layout, base, hpad):
    n_x, blocks = sum(layout), len(layout)
    x_refs, w_ref, saved_refs = refs[:n_x], refs[n_x], refs[n_x + 1 : n_x + 3]
    outs, scr = refs[-(12 + n_x) : -9], refs[-9:]
    all_refs, part_refs = outs[:3], outs[3:]
    xs, dgu_s, slope_s, gelu_s, part_s, x_sem, out_sem, part_sem, saved_sem = scr
    rows = xs.shape[1]
    stage = (xs, dgu_s.at[:, :, pl.ds(0, hpad)], dgu_s.at[:, :, pl.ds(hpad, hpad)])
    loads, started = [[] for _ in range(blocks)], []

    def saved(block, n):
        src = saved_refs[n].at[pl.ds((base + block) * rows, rows), :]
        dst = (slope_s, gelu_s)[n].at[block]
        copy = pltpu.make_async_copy(src, dst, saved_sem.at[block, n])
        copy.start()
        loads[block].append(copy)

    for block, at, row, ref in ffn_layout(x_refs, layout):
        dst = xs.at[block, pl.ds(row, ref.shape[0]), :]
        copy = pltpu.make_async_copy(ref, dst, x_sem.at[at])
        copy.start()
        loads[block].append(copy)
        if row == 0:
            saved(block, 0)
            saved(block, 1)

    def stack(block, n):
        dst = all_refs[n].at[pl.ds((base + block) * rows, rows), :]
        copy = pltpu.make_async_copy(stage[n].at[block], dst, out_sem.at[block, n])
        copy.start()
        started.append(copy)

    for block in range(blocks):
        for copy in loads[block]:
            copy.wait()
        stack(block, 0)
        dout = xs[block]
        for c in range(0, hpad, 256):
            wide = min(256, hpad - c)
            d_act = mm(dout, w_ref[:, 2 * hpad + c : 2 * hpad + c + wide])
            slope = slope_s[block, :, c : c + wide].astype(F32)
            gelu = gelu_s[block, :, c : c + wide].astype(F32)
            dgu_s[block, :, c : c + wide] = (d_act * slope).astype(BF)
            dgu_s[block, :, hpad + c : hpad + c + wide] = (d_act * gelu).astype(BF)
        stack(block, 1)
        stack(block, 2)
        part_s[block] = mm_nt(dgu_s[block], w_ref[:, : 2 * hpad]).astype(BF)
        for b, at, row, ref in ffn_layout(part_refs, layout):
            if b == block:
                src = part_s.at[block, pl.ds(row, ref.shape[0]), :]
                copy = pltpu.make_async_copy(src, ref, part_sem.at[at])
                copy.start()
                started.append(copy)
    for copy in started:
        copy.wait()


def hold_kernel(src_ref, dst_ref, sem):
    copy = pltpu.make_async_copy(src_ref, dst_ref, sem.at[0])
    copy.start()
    copy.wait()


def hold(value):
    return pl.pallas_call(
        hold_kernel,
        out_shape=pltpu.VMEM(value.shape, value.dtype),
        in_specs=[pl.BlockSpec(memory_space=pltpu.HBM)],
        out_specs=pl.BlockSpec(memory_space=pltpu.VMEM),
        scratch_shapes=[pltpu.SemaphoreType.DMA((1,))],
        compiler_params=pltpu.CompilerParams(vmem_limit_bytes=16 << 20),
        cost_estimate=price(3, 1000000),
    )(in_hbm(value))


def in_hbm(value):
    return pltpu.with_memory_space_constraint(value, pltpu.HBM)


def ffn_call(kernel, blocks, base, saved, w_ffn, bufs):
    pieces = [piece for block in blocks for piece in block]
    layout = tuple(len(block) for block in blocks)
    n, back = len(blocks), bool(saved)
    width, hpad = w_ffn.shape[0], w_ffn.shape[1] // 3
    rows = sum(piece.shape[0] for piece in blocks[0])
    widths = [width, hpad, hpad] if back else [width, hpad, hpad, hpad]
    ins = [in_hbm(v) for v in pieces] + [w_ffn] + [in_hbm(v) for v in saved]
    aliases = {}
    if bufs is not None:
        aliases = {len(ins) + k: k for k in range(len(widths))}
        ins = ins + [in_hbm(v) for v in bufs]
    hbm = pl.BlockSpec(memory_space=pltpu.HBM)
    in_specs = [hbm] * len(ins)
    in_specs[len(pieces)] = pl.BlockSpec(memory_space=pltpu.VMEM)
    shapes = [((8 * rows, w), BF) for w in widths] + [(piece.shape, BF) for piece in pieces]
    mid = [2 * hpad, hpad, hpad] if back else [hpad, hpad, hpad]
    scratch = [pltpu.VMEM((n, rows, w), BF) for w in [width] + mid + [width]]
    scratch += [
        pltpu.SemaphoreType.DMA((len(pieces),)),
        pltpu.SemaphoreType.DMA((n, 4)),
        pltpu.SemaphoreType.DMA((len(pieces),)),
        pltpu.SemaphoreType.DMA((n, 2)),
    ]
    outs = pl.pallas_call(
        partial(kernel, layout=layout, base=base, hpad=hpad),
        out_shape=[pltpu.HBM(shape, dtype) for shape, dtype in shapes],
        in_specs=in_specs,
        out_specs=[hbm] * len(shapes),
        scratch_shapes=scratch,
        input_output_aliases=aliases,
        compiler_params=pltpu.CompilerParams(vmem_limit_bytes=28 << 20),
        cost_estimate=price(6 * n, 1000000 * n),
    )(*ins)
    grouped, at = [], len(widths)
    for count in layout:
        grouped.append(tuple(outs[at : at + count]))
        at += count
    return outs[: len(widths)], grouped


def ffn_mid_kernel(*refs):
    hid_ref, cot_ref, gains_ref, out_ref, dout_ref, gain_ref = refs[6:]
    part = piece_sum(refs[:6])
    gain = gains_ref[3:4, :]
    factor = lax.rsqrt(jnp.mean(part * part, -1, keepdims=True) + EPS)
    out_ref[...] = (hid_ref[...] + part * factor * gain).astype(BF)
    back, gain_grad = norm_back_tile(part, gain, cot_ref[...].astype(F32))
    dout_ref[...] = back.astype(BF)
    gain_ref[0:1, :] = gain_grad


def norm_back_tile(raw, gain, upstream):
    factor = lax.rsqrt(jnp.mean(raw * raw, -1, keepdims=True) + EPS)
    normed = raw * factor
    gain_grad = jnp.sum(upstream * normed, axis=0, keepdims=True)
    scaled = upstream * gain
    back = factor * (scaled - normed * jnp.mean(scaled * normed, -1, keepdims=True))
    return back, gain_grad


def mid_kernel(*refs):
    hid_ref, part_ref, cot_ref, gains_ref = refs[6:10]
    w_refs, (dhid_ref, dpart_ref, dhead_ref, gain_ref) = refs[10:20], refs[20:]
    din = piece_sum(refs[:6])
    extra, gain_ffn = norm_back_tile(hid_ref[...], gains_ref[2:3, :], din)
    dhid = cot_ref[...].astype(F32) + extra
    dhid_ref[...] = dhid
    dpart, gain_post = norm_back_tile(part_ref[...], gains_ref[1:2, :], dhid)
    dpart = dpart.astype(BF)
    dpart_ref[...] = dpart
    gain_ref[0:1, :] = gain_ffn
    gain_ref[1:2, :] = gain_post
    pairs = split_w(w_refs, w_refs[6].shape[0])
    for r in range(4):
        dhead_ref[r] = mm_split(dpart, head_w(pairs, r)).astype(BF)


def attn_back_kernel(
    need,
    q_ref,
    k2_ref,
    kp_ref,
    ko_ref,
    bias_ref,
    o_ref,
    do_ref,
    linv_ref,
    qn_ref,
    fac_ref,
    cos_ref,
    sin_ref,
    gq_ref,
    dq_ref,
    d2_ref,
    dp_ref,
    down_ref,
    gain_ref,
    acc_ref,
    dkv_ref,
):
    i = pl.program_id(0)
    tile = q_ref.shape[1]

    @pl.when(i == 0)
    def _():
        dkv_ref[...] = jnp.zeros_like(dkv_ref)
        gain_ref[...] = jnp.zeros_like(gain_ref)

    acc_ref[...] = jnp.zeros_like(acc_ref)
    q = q_ref[...].reshape(4 * tile, HD)
    do = do_ref[...].reshape(4 * tile, HD)
    linv = linv_ref[...].reshape(4 * tile, 128)[:, 0:1]
    inner = jnp.sum(do.astype(F32) * o_ref[...].reshape(4 * tile, HD).astype(F32), -1, keepdims=True)
    for kb in range(6):

        @pl.when(need[i * 6 + kb] > 0)
        def _(kb=kb):
            kv = kv_block((k2_ref, kp_ref, ko_ref), kb)
            keys, vals = kv[:, :HD], kv[:, HD:]
            s = mm_nt(q, keys).reshape(4, tile, 256) * HD ** (-0.5)
            p = jnp.exp(s + bias_ref[:, kb * 256 : (kb + 1) * 256][None])
            p = p.reshape(4 * tile, 256) * linv
            dp = mm_nt(do, vals)
            ds = (p * (dp - inner)).astype(BF)
            acc_ref[...] += mm(ds, keys)
            span = slice(kb * 256, (kb + 1) * 256)
            dkv_ref[span, :HD] += mm_tn(ds, q)
            dkv_ref[span, HD:] += mm_tn(p.astype(BF), do)

    cos, sin = cos_ref[...], sin_ref[...]
    gain = jnp.zeros((1, HD), F32)
    for r in range(4):
        dq = acc_ref[r * tile : (r + 1) * tile, :] * HD ** (-0.5)
        own, oth = dq[:, :128], dq[:, 128:]
        back = jnp.concatenate([own * cos + oth * sin, oth * cos - own * sin], axis=1)
        norm = qn_ref[r].astype(F32)
        gain += jnp.sum(back * norm, axis=0, keepdims=True)
        scaled = back * gq_ref[4:5, :]
        mean = jnp.mean(scaled * norm, -1, keepdims=True)
        dq_ref[r] = (fac_ref[:, r : r + 1] * (scaled - norm * mean)).astype(BF)
    gain_ref[0:1, :] += gain

    @pl.when(i == pl.num_programs(0) - 1)
    def _():
        rows = d2_ref.shape[0]
        scale = HD ** (-0.5)
        for n, ref in enumerate((d2_ref, dp_ref, down_ref)):
            block = dkv_ref[n * rows : (n + 1) * rows, :]
            ref[:, :HD] = (block[:, :HD] * scale).astype(ref.dtype)
            ref[:, HD:] = block[:, HD:].astype(ref.dtype)


def post_kernel(
    flags,
    dq_ref,
    dkv_ref,
    dp_ref,
    kn_ref,
    fac_ref,
    cos_ref,
    sin_ref,
    gk_ref,
    x_ref,
    gains_ref,
    dhid_ref,
    gq_grad,
    mid_grad,
    post_grad,
    place_ref,
    *refs,
):
    w_refs, din_ref, kvraw_ref, gain_ref = refs[:10], *refs[10:]
    fi, ty, tc = (flags[n].astype(F32) for n in range(3))
    dkv = dkv_ref[...] + dp_ref[...].astype(F32)
    cos, sin = cos_ref[...], sin_ref[...]
    own, oth = dkv[:, :128], dkv[:, 128:256]
    back = jnp.concatenate([own * cos + oth * sin, oth * cos - own * sin], axis=1)
    norm = kn_ref[...].astype(F32)
    gk_grad = jnp.sum(back * norm, axis=0, keepdims=True)
    scaled = back * gk_ref[5:6, :]
    mean = jnp.mean(scaled * norm, -1, keepdims=True)
    dkey = fac_ref[:, 4:5] * (scaled - norm * mean)
    dval = dkv[:, 256:]
    kvraw_ref[...] = jnp.concatenate([dkey, dval], axis=1).astype(BF)
    din = jnp.zeros(din_ref.shape, F32)
    zeros = jnp.zeros((dkv.shape[0], 64), F32)
    pairs = split_w(w_refs, w_refs[6].shape[0])
    rel = 0
    for dx in range(2):
        kh = dkey[:, dx * 128 : (dx + 1) * 128]
        vh = dval[:, dx * 128 : (dx + 1) * 128]
        for dy in range(2):
            half = mix(ty, kh, vh) if dy == 0 else mix(ty, vh, kh)
            for dc in range(2):
                lo, hi = half[:, :64], half[:, 64:]
                part = mix(tc, lo, hi) if dc == 0 else mix(tc, hi, lo)
                side = jnp.concatenate([part, zeros], axis=1).astype(BF)
                dprod = jnp.concatenate(
                    [dq_ref[dy * 2 + dc][:, dx * 128 : (dx + 1) * 128], side], axis=1
                )
                din += mm_nt_split(dprod, pairs[rel])
                rel += 1
    x = x_ref[...].astype(F32)
    extra, gain_pre = norm_back_tile(x, gains_ref[0:1, :], din)
    din_ref[...] = dhid_ref[...] + extra

    def spread(grad):
        own, oth = grad[:, :128], grad[:, 128:]
        whole_row = jnp.concatenate([mix(fi, own, oth), mix(fi, oth, own)], axis=1)
        return mm(jnp.broadcast_to(whole_row.astype(BF), (8, HD)), place_ref[...])[0:1, :]

    gain_ref[...] = jnp.zeros_like(gain_ref)
    gain_ref[0:1, :] = gain_pre
    gain_ref[1:2, :] = mid_grad[1:2, :]
    gain_ref[2:3, :] = mid_grad[0:1, :]
    gain_ref[3:4, :] = post_grad[0:1, :]
    gain_ref[4:5, :] = spread(gq_grad[0:1, :])
    gain_ref[5:6, :] = spread(gk_grad)


def store_rows(refs, value):
    cut = refs[0].shape[0]
    refs[0][...] = value[:cut, :]
    refs[1][...] = value[cut:, :]


def qo_grad_kernel(xin, xin_c, dq, dq_c, dpart, dpart_c, head, head_c, *outs):
    xt, xt_c, dt, dt_c = (ref[...].T for ref in (xin, xin_c, dpart, dpart_c))
    for dy in range(2):
        gq = (mm(xt, dq[2 * dy]) + mm(xt_c, dq_c[dy])).astype(BF)
        go = (mm(dt, head[2 * dy]) + mm(dt_c, head_c[dy])).astype(BF)
        for dx in range(2):
            half = slice(dx * 128, (dx + 1) * 128)
            at = 4 * dx + 2 * dy
            store_rows(outs[at : at + 2], jnp.concatenate([gq[:, half], go[:, half]], axis=1))


def kv_grad_kernel(flags, xin, xin_c, kv, kv_c, gain, gain_c, *refs):
    outs, rows_ref = refs[:8], refs[8]
    ty, tc = flags[1].astype(F32), flags[2].astype(F32)
    rows_ref[...] = jnp.zeros_like(rows_ref)
    rows_ref[64:72, :] = gain[...] + gain_c[...]
    gain_cols = rows_ref[...].T
    xt, xt_c = xin[...].T, xin_c[...].T

    def sides(ref):
        block = ref[...].astype(F32)
        picked = []
        for dy in range(2):
            for dx in range(2):
                kh = block[:, dx * 128 : (dx + 1) * 128]
                vh = block[:, 256 + dx * 128 : 256 + (dx + 1) * 128]
                half = mix(ty, kh, vh) if dy == 0 else mix(ty, vh, kh)
                picked.append(mix(tc, half[:, :64], half[:, 64:]))
        return jnp.concatenate(picked, axis=1).astype(BF)

    grad = mm(xt, sides(kv)) + mm(xt_c, sides(kv_c))
    zeros = jnp.zeros((grad.shape[0], 64), F32)
    for dy in range(2):
        for dx in range(2):
            at = 4 * dx + 2 * dy
            col = (2 * dy + dx) * 64
            part = jnp.concatenate([grad[:, col : col + 64], zeros], axis=1) + gain_cols
            store_rows(outs[at : at + 2], part.astype(BF))


def chip_reduce(parts):
    own, near_y, near_x, far = (parts[n : n + 2] for n in (0, 2, 4, 6))
    from_x, from_y = swap(far[0], "fi"), swap(far[1], "ty")
    got_x_top, got_y_bot = swap(near_x[0], "fi"), swap(near_y[1], "ty")
    x_bot = (near_x[1].astype(F32) + from_y.astype(F32)).astype(BF)
    y_top = (near_y[0].astype(F32) + from_x.astype(F32)).astype(BF)
    return (*own, got_x_top, swap(x_bot, "fi"), swap(y_top, "ty"), got_y_bot)


def gather_sum_kernel(*refs):
    out_ref = refs[12]
    for n, cols in ((0, slice(0, 256)), (6, slice(256, 384))):
        own_top, own_bot, x_top, x_bot, y_top, y_bot = (ref[...].astype(F32) for ref in refs[n : n + 6])
        cut = own_top.shape[0]
        out_ref[:cut, cols] = (own_top + x_top + y_top).astype(BF)
        out_ref[cut:, cols] = (own_bot + x_bot + y_bot).astype(BF)


def pad_cols(value, width):
    return jnp.pad(value, ((0, 0), (0, width - value.shape[1])))


def body(
    tokens,
    positions,
    segments,
    w_query,
    w_key,
    w_value,
    w_out,
    w_gate,
    w_up,
    w_down,
    gain_attn_pre,
    gain_query,
    gain_key,
    gain_attn_post,
    gain_ffn_pre,
    gain_ffn_post,
    cotangent,
):
    fi = lax.axis_index("fi")
    ty = lax.axis_index("ty")
    tc = lax.axis_index("tc")
    t_idx = ty * 2 + tc
    me = fi * 4 + t_idx
    first = fi == 0
    rows = tokens.shape[0]
    width = tokens.shape[1]
    shard = w_query.shape[0]
    nf = width // shard
    hid = w_gate.shape[1] // 2
    hpad = -(-hid // 128) * 128
    gshard = gain_query.shape[0]

    def pair_rows(keep, recv):
        return jnp.where(
            first,
            jnp.concatenate([keep, recv], axis=0),
            jnp.concatenate([recv, keep], axis=0),
        )

    kv_mine = jnp.where(ty == 0, w_key, w_value)
    out_t = w_out.T
    gains = pad_cols(
        jnp.stack(
            [
                gain_attn_pre,
                gain_attn_post,
                gain_ffn_pre,
                gain_ffn_post,
                jnp.pad(gain_query, (0, shard - gshard)),
                jnp.pad(gain_key, (0, shard - gshard)),
            ],
            axis=1,
        ),
        64,
    )

    def piece(h):
        kv_half = kv_mine[:, h * 128 : (h + 1) * 128]
        kv_part = jnp.where(tc == 0, kv_half[:, :64], kv_half[:, 64:])
        return jnp.concatenate(
            [
                w_query[:, h * 128 : (h + 1) * 128],
                kv_part,
                gains,
                out_t[:, h * 128 : (h + 1) * 128],
            ],
            axis=1,
        )

    piece0, piece1 = piece(0), piece(1)
    keep = jnp.where(first, piece0, piece1)
    recv = swap(jnp.where(first, piece1, piece0), "fi")

    down_t = w_down.T

    def halves(weight):
        lo, hi = pad_cols(weight[:, :hid], hpad), pad_cols(weight[:, hid:], hpad)
        return jnp.where(first, lo, hi), jnp.where(first, hi, lo)

    gate_keep, gate_send = halves(w_gate)
    up_keep, up_send = halves(w_up)
    down_keep, down_send = halves(down_t)
    ffn_keep = jnp.concatenate([gate_keep, up_keep, down_keep], axis=1)
    ffn_send = jnp.concatenate([gate_send, up_send, down_send], axis=1)
    ffn_send, ffn_keep, recv = lax.optimization_barrier((ffn_send, ffn_keep, recv))
    ffn_recv = swap(ffn_send, "fi")
    attn_col = lax.all_gather(pair_rows(keep, recv), "fo", axis=0, tiled=True)
    attn_col, ffn_pair = lax.optimization_barrier((attn_col, pair_rows(ffn_keep, ffn_recv)))
    w_ffn = lax.all_gather(ffn_pair, "fo", axis=0, tiled=True)

    elem = lax.broadcasted_iota(jnp.int32, (HD, width), 0)
    spot = lax.broadcasted_iota(jnp.int32, (HD, width), 1)
    place = (spot == (elem // gshard) * shard + elem % gshard).astype(BF)
    cut = width // 256 * 128
    row_start = t_idx * rows
    pos_local = lax.dynamic_slice_in_dim(positions, row_start, rows)
    seg_local = lax.dynamic_slice_in_dim(segments, row_start, rows)

    def block_of(meta, back):
        return lax.dynamic_slice_in_dim(meta, ((t_idx - back) % 4) * rows, rows)

    k_pos = jnp.concatenate([block_of(positions, 2), block_of(positions, 1), pos_local])
    k_seg = jnp.concatenate(
        [
            jnp.where(t_idx == 3, block_of(segments, 2), -1),
            jnp.where(t_idx >= 1, block_of(segments, 1), -1),
            seg_local,
        ]
    )
    allowed = (
        ((k_seg[None, :] == 0) | (k_seg[None, :] == seg_local[:, None]))
        & (k_pos[None, :] <= pos_local[:, None])
        & (pos_local[:, None] - k_pos[None, :] < WINDOW)
    )
    bias = jnp.where(allowed, 0.0, NEG).astype(F32)
    need = jnp.any(allowed.reshape(4, rows // 4, 6, rows // 2), axis=(1, 3))
    need = need.astype(jnp.int32).reshape(24)
    frequency = jnp.exp(-math.log(BASE) * jnp.arange(HALF).astype(F32) / HALF)
    angles = pos_local.astype(F32)[:, None] * frequency
    cosine = jnp.cos(angles)
    sine = jnp.sin(angles) * jnp.where(first, 1.0, -1.0)

    w_parts, (bias, need, cosine, sine, place) = plane_gather(
        attn_col, cut, (bias, need, cosine, sine, place)
    )
    w_parts = [in_hbm(piece) for pieces in w_parts for piece in pieces]
    flags = jnp.stack([fi, ty, tc]).astype(jnp.int32)
    qkv_spec = [pl.BlockSpec((part.shape[0], 256), lambda *_: (0, 0)) for part in w_parts]
    wo_spec = [pl.BlockSpec((part.shape[0], 128), lambda *_: (0, 2)) for part in w_parts]
    full, gains8 = whole((rows, width)), whole((8, width))
    heads = whole((4, rows, HD))
    lanes = whole((rows, 128))
    kv_full = whole((rows, 2 * HD))
    attn_in, q_rot, q_norm, kv_own, k_norm, factors, gain_rows, head_gains = run(
        qkv_kernel,
        [
            ((rows, width), BF),
            ((4, rows, HD), BF),
            ((4, rows, HD), BF),
            ((rows, 2 * HD), BF),
            ((rows, HD), BF),
            ((rows, 128), F32),
            ((8, width), F32),
            ((8, HD), F32),
        ],
        (flags, tokens, place, cosine, sine, *w_parts),
        9,
        grid=(1,),
        in_specs=[full, whole((HD, width)), lanes, lanes] + qkv_spec,
        out_specs=[full, heads, heads, kv_full, whole((rows, HD)), lanes, gains8, whole((8, HD))],
        prefetch=1,
    )
    kv_prev = lax.ppermute(kv_own, ("ty", "tc"), [(i, (i + 1) % 4) for i in range(4)])
    kv_two = swap(kv_prev, "tc")
    tile = rows // 4
    q_tile = pl.BlockSpec((4, tile, HD), lambda i, *_: (0, i, 0))
    l_tile = pl.BlockSpec((4, tile, 128), lambda i, *_: (0, i, 0))
    bias_tile = pl.BlockSpec((tile, 3 * rows), lambda i, *_: (i, 0))
    head_out, linv = run(
        attn_kernel,
        [((4, rows, HD), BF), ((4, rows, 128), F32)],
        (need, q_rot, kv_two, kv_prev, kv_own, bias),
        8,
        grid=(4,),
        in_specs=[q_tile, kv_full, kv_full, kv_full, bias_tile],
        out_specs=[q_tile, l_tile],
        scratch=[pltpu.VMEM((4 * tile, HD), F32), pltpu.VMEM((4 * tile, 128), F32)],
        prefetch=1,
    )
    attn_part, hidden, ffn_local = run(
        out_kernel,
        [((rows, width), F32), ((rows, width), F32), ((rows, width), BF)],
        (head_out, tokens, gain_rows, *w_parts),
        6,
        grid=(1,),
        in_specs=[heads, full, gains8] + wo_spec,
        out_specs=[full, full, full],
    )

    half = rows // 2
    def far_pieces(top, bot, after):
        top, bot, after = lax.optimization_barrier((top, bot, after))
        return [(top, bot), (swap(top, "tc"), swap(bot, "tc"))], after

    by_x, by_y, by_c = swap(ffn_local, "fi"), swap(ffn_local, "ty"), swap(ffn_local, "tc")
    top, bot = swap(by_y[:half], "fi"), swap(by_x[half:], "ty")
    by_xc, by_yc = swap(by_x, "tc"), swap(by_y, "tc")
    w_ffn = hold(w_ffn)
    top_c, bot_c = swap(top, "tc"), swap(bot, "tc")
    far = [(top, bot), (top_c, bot_c)]
    bufs, parts_f = ffn_call(ffn_kernel, far, 6, [], w_ffn, None)
    got = far_swap(far_sum(*parts_f, half))
    bufs, parts_x = ffn_call(ffn_kernel, [(by_x,), (by_xc,)], 2, [], w_ffn, bufs)
    by_y, by_yc, got = lax.optimization_barrier((by_y, by_yc, got))
    bufs, parts_y = ffn_call(ffn_kernel, [(by_y,), (by_yc,)], 4, [], w_ffn, bufs)
    rest, first_out = near_first(parts_y, parts_x, half)
    first_in = near_swap(first_out)
    second_out = near_second(rest, got, half)
    first_in, second_out = lax.optimization_barrier((first_in, second_out))
    second_in = near_swap(second_out)
    (x_all, act_all, slope_all, gelu_all), parts_o = ffn_call(
        ffn_kernel, [(ffn_local,), (by_c,)], 0, [], w_ffn, bufs
    )
    pieces = plane_pieces(parts_o, first_in, second_in)
    quarter = whole((half, width))
    piece_spec = [full, full] + [quarter] * 4

    other = swap(jnp.stack([head_out[1], head_out[3]]), "tc"), swap(attn_in, "tc")
    pieces, (head_out_c, attn_in_c) = lax.optimization_barrier((pieces, other))
    output, d_local, ffn_post_grad = run(
        ffn_mid_kernel,
        [((rows, width), BF), ((rows, width), BF), ((8, width), F32)],
        (*pieces, hidden, cotangent, gain_rows),
        6,
        grid=(1,),
        in_specs=piece_spec + [full, full, gains8],
        out_specs=[full, full, gains8],
    )
    by_x, by_y, by_c = swap(d_local, "fi"), swap(d_local, "ty"), swap(d_local, "tc")
    saved = [slope_all, gelu_all]
    bufs, parts_o = ffn_call(ffn_back_kernel, [(d_local,), (by_c,)], 0, saved, w_ffn, None)
    by_x, by_y, parts_o = lax.optimization_barrier((by_x, by_y, parts_o))
    top, bot = swap(by_y[:half], "fi"), swap(by_x[half:], "ty")
    by_xc, by_yc = swap(by_x, "tc"), swap(by_y, "tc")
    bufs, parts_x = ffn_call(ffn_back_kernel, [(by_x,), (by_xc,)], 2, saved, w_ffn, bufs)
    far, parts_x = far_pieces(top, bot, parts_x)
    bufs, parts_f = ffn_call(ffn_back_kernel, far, 6, saved, w_ffn, bufs)
    (d_all, dgate_all, dup_all), parts_y = ffn_call(
        ffn_back_kernel, [(by_y,), (by_yc,)], 4, saved, w_ffn, bufs
    )
    sent = far_sum(*parts_f, half)
    rest, first_out = near_first(parts_y, parts_x, half)
    d_all, sent, first_out = lax.optimization_barrier((d_all, sent, first_out))
    got, first_in = far_swap(sent), near_swap(first_out)
    grad_dt = dot_left_t(d_all, act_all).astype(BF)
    dgate_all, grad_dt, got = lax.optimization_barrier((dgate_all, grad_dt, got))
    second_out = near_second(rest, got, half)
    first_in, second_out = lax.optimization_barrier((first_in, second_out))
    second_in = near_swap(second_out)
    grad_gate = dot_left_t(x_all, dgate_all).astype(BF)
    pieces = plane_pieces(parts_o, first_in, second_in)
    pieces, grad_gate = lax.optimization_barrier((pieces, grad_gate))
    sum_dt = lax.psum_scatter(grad_dt, "fo", scatter_dimension=0, tiled=True)
    sum_gate = lax.psum_scatter(grad_gate, "fo", scatter_dimension=0, tiled=True)

    def unpair(summed):
        top_rows, bot_rows = summed[:shard], summed[shard:]
        mine = jnp.where(first, top_rows, bot_rows)
        theirs = swap(jnp.where(first, bot_rows, top_rows), "fi")
        return jnp.where(first, mine, theirs), jnp.where(first, theirs, mine)

    def join(lo, hi):
        return jnp.concatenate([lo[:, :hid], hi[:, :hid]], axis=1).astype(F32)

    hidden_grad, attn_part_grad, head_grad, mid_gains = run(
        mid_kernel,
        [((rows, width), F32), ((rows, width), BF), ((4, rows, HD), BF), ((8, width), F32)],
        (*pieces, hidden, attn_part, cotangent, gain_rows, *w_parts),
        10,
        grid=(1,),
        in_specs=piece_spec + [full, full, full, gains8] + wo_spec,
        out_specs=[full, full, heads, whole((8, width))],
    )
    fac_tile = pl.BlockSpec((tile, 128), lambda i, *_: (i, 0))
    line = whole((8, HD))
    q_raw_grad, kv_grad_two, kv_grad_prev, kv_grad_own, gain_q = run(
        attn_back_kernel,
        [
            ((4, rows, HD), BF),
            ((rows, 2 * HD), BF),
            ((rows, 2 * HD), BF),
            ((rows, 2 * HD), F32),
            ((8, HD), F32),
        ],
        (
            need,
            q_rot,
            kv_two,
            kv_prev,
            kv_own,
            bias,
            head_out,
            head_grad,
            linv,
            q_norm,
            factors,
            cosine,
            sine,
            head_gains,
        ),
        12,
        grid=(4,),
        in_specs=[
            q_tile,
            kv_full,
            kv_full,
            kv_full,
            bias_tile,
            q_tile,
            q_tile,
            l_tile,
            q_tile,
            fac_tile,
            fac_tile,
            fac_tile,
            line,
        ],
        out_specs=[q_tile, kv_full, kv_full, kv_full, whole((8, HD))],
        scratch=[pltpu.VMEM((4 * tile, HD), F32), pltpu.VMEM((3 * rows, 2 * HD), F32)],
        prefetch=1,
    )
    back_two = kv_grad_prev.astype(F32) + swap(kv_grad_two, "tc").astype(F32)
    q_raw_grad, dup_all, back_two = lax.optimization_barrier(
        (q_raw_grad, dup_all, back_two.astype(BF))
    )
    grad_up = dot_left_t(x_all, dup_all).astype(BF)
    back_prev = lax.ppermute(back_two, ("ty", "tc"), [(i, (i + 3) % 4) for i in range(4)])
    def row_pieces(cols):
        return [((n, cols), BF) for n in (cut, width - cut)] * 4

    other_heads = lambda value: swap(jnp.stack([value[1], value[3]]), "tc")
    two_heads = whole((2, rows, HD))
    qo_grads = run(
        qo_grad_kernel,
        row_pieces(256),
        (
            attn_in,
            attn_in_c,
            q_raw_grad,
            other_heads(q_raw_grad),
            attn_part_grad,
            swap(attn_part_grad, "tc"),
            head_out,
            head_out_c,
        ),
        5,
        grid=(1,),
        in_specs=[full, full, heads, two_heads, full, full, heads, two_heads],
        out_specs=[whole(shape) for shape, _ in row_pieces(256)],
    )
    back_prev, sum_dt, grad_up = lax.optimization_barrier((back_prev, sum_dt, grad_up))
    sum_up = lax.psum_scatter(grad_up, "fo", scatter_dimension=0, tiled=True)
    qo_pieces = chip_reduce(qo_grads)
    input_grad, kv_raw_grad, gain_grads = run(
        post_kernel,
        [((rows, width), F32), ((rows, 2 * HD), BF), ((8, width), F32)],
        (
            flags,
            q_raw_grad,
            kv_grad_own,
            back_prev,
            k_norm,
            factors,
            cosine,
            sine,
            head_gains,
            tokens,
            gain_rows,
            hidden_grad,
            gain_q,
            mid_gains,
            ffn_post_grad,
            place,
            *w_parts,
        ),
        9,
        grid=(1,),
        in_specs=[heads, kv_full, kv_full, whole((rows, HD)), lanes, lanes, lanes, line]
        + [full, gains8, full, whole((8, HD)), gains8, gains8]
        + [whole((HD, width))]
        + qkv_spec,
        out_specs=[full, kv_full, gains8],
        prefetch=1,
    )
    kv_grads = run(
        kv_grad_kernel,
        row_pieces(128),
        (
            flags,
            attn_in,
            attn_in_c,
            kv_raw_grad,
            swap(kv_raw_grad, "tc"),
            gain_grads,
            swap(gain_grads, "tc"),
        ),
        3,
        grid=(1,),
        in_specs=[full, full, kv_full, kv_full, gains8, gains8],
        out_specs=[whole(shape) for shape, _ in row_pieces(128)],
        scratch=[pltpu.VMEM((128, width), F32)],
        prefetch=1,
    )
    kv_pieces = chip_reduce(kv_grads)
    qo_pieces, kv_pieces, sum_gate, sum_up = lax.optimization_barrier(
        (qo_pieces, kv_pieces, sum_gate, sum_up)
    )
    (attn_grads,) = run(
        gather_sum_kernel,
        [((width, 384), BF)],
        (*qo_pieces, *kv_pieces),
        2,
        grid=(1,),
        in_specs=[whole(piece.shape) for piece in (*qo_pieces, *kv_pieces)],
        out_specs=[whole((width, 384))],
    )
    sum_attn = lax.psum_scatter(attn_grads, "fo", scatter_dimension=0, tiled=True)
    dt_lo, dt_hi = unpair(sum_dt)
    grad_gate = join(*unpair(sum_gate))
    grad_up = join(*unpair(sum_up))
    grad_down = join(dt_lo, dt_hi).T

    a_lo, a_hi = unpair(sum_attn)
    grad_out = jnp.concatenate([a_lo[:, 128:256], a_hi[:, 128:256]], axis=1).astype(F32).T
    grad_query = jnp.concatenate([a_lo[:, :128], a_hi[:, :128]], axis=1).astype(F32)
    kv_part = jnp.concatenate([a_lo[:, 256:320], a_hi[:, 256:320]], axis=1)
    others = [
        lax.ppermute(kv_part, ("ty", "tc"), [(i, i ^ step) for i in range(4)]) for step in (1, 2, 3)
    ]
    row_here = jnp.where(tc == 0, 0, 1)

    def kv_lines(near, far):
        even = jnp.where(row_here == 0, near, far)
        odd = jnp.where(row_here == 0, far, near)
        return jnp.concatenate([even[:, :64], odd[:, :64], even[:, 64:], odd[:, 64:]], axis=1)

    kv_here, kv_far = kv_lines(kv_part, others[0]), kv_lines(others[1], others[2])
    grad_key = jnp.where(ty == 0, kv_here, kv_far).astype(F32)
    grad_value = jnp.where(ty == 0, kv_far, kv_here).astype(F32)
    gain_out = a_lo[:, 320:328].astype(F32).T
    return (
        output.astype(BF),
        input_grad,
        grad_query,
        grad_key,
        grad_value,
        grad_out,
        grad_gate,
        grad_up,
        grad_down,
        gain_out[0],
        gain_out[4, :gshard],
        gain_out[5, :gshard],
        gain_out[1],
        gain_out[2],
        gain_out[3],
    )


def solution(mesh):
    nf, nt = mesh.shape["fsdp"], mesh.shape["tensor"]
    fine = Mesh(mesh.devices.reshape(nf // 2, 2, nt // 2, 2), ("fo", "fi", "ty", "tc"))
    f_axes, t_axes = ("fo", "fi"), ("ty", "tc")
    rows = P(f_axes + t_axes, None)
    col = P(f_axes, t_axes)
    flat = P(f_axes, None)
    out_w = P(t_axes, f_axes)
    vec = P(f_axes)
    in_specs = (rows, vec, vec, col, flat, flat, out_w, col, col, out_w) + (vec,) * 6 + (rows,)
    out_specs = (rows, rows, col, flat, flat, out_w, col, col, out_w) + (vec,) * 6
    return jax.shard_map(body, mesh=fine, in_specs=in_specs, out_specs=out_specs, check_vma=False)
```

```python
import math
from functools import partial

import jax
import jax.numpy as jnp
from jax import lax
from jax.experimental import pallas as pl
from jax.experimental.pallas import tpu as pltpu
from jax.sharding import Mesh, PartitionSpec as P

HD = 256
WINDOW = 512
PROMPT = 1024
CONT = 8
CLEN = 128


EPS = 1e-06
NEG = -1e30
BASE = 10000.0
HALF = HD // 2
BF = jnp.bfloat16
F32 = jnp.float32


def dot_left_t(left_op, right_op):
    return lax.dot_general(
        left_op, right_op, (((0,), (0,)), ((), ())), preferred_element_type=jnp.float32
    )


def swap(value, axis):
    return lax.ppermute(value, axis, [(0, 1), (1, 0)])


RELS = [(dx, dy, dc) for dx in (0, 1) for dy in (0, 1) for dc in (0, 1)]


def plane_gather(own, cut, side):
    by_x = swap(own, "fi")
    by_y = swap(own, "ty")
    by_c = swap(own, "tc")
    by_x, by_y, side = lax.optimization_barrier((by_x, by_y, side))
    diag_top = swap(by_y[:cut], "fi")
    diag_bot = swap(by_x[cut:], "ty")
    by_xc = swap(by_x, "tc")
    by_yc = swap(by_y, "tc")
    return [
        (own,),
        (by_c,),
        (by_y,),
        (by_yc,),
        (by_x,),
        (by_xc,),
        (diag_top, diag_bot),
        (swap(diag_top, "tc"), swap(diag_bot, "tc")),
    ], side


def core_add(mine, other):
    return mine.astype(F32) + swap(other, "tc").astype(F32)


def far_sum(far, far_c, cut):
    if len(far) == 1:
        far, far_c = (far[0][:cut], far[0][cut:]), (far_c[0][:cut], far_c[0][cut:])
    return core_add(far[0], far_c[0]).astype(BF), core_add(far[1], far_c[1]).astype(BF)


def far_swap(sent):
    return swap(sent[0], "fi"), swap(sent[1], "ty")


def near_first(parts):
    (x_top, y_bot), (x_top_c, y_bot_c) = parts
    return core_add(x_top, x_top_c).astype(BF), core_add(y_bot, y_bot_c).astype(BF)


def near_second(parts, got):
    (x_bot, y_top), (x_bot_c, y_top_c) = parts
    x_bot = core_add(x_bot, x_bot_c) + got[1].astype(F32)
    y_top = core_add(y_top, y_top_c) + got[0].astype(F32)
    return x_bot.astype(BF), y_top.astype(BF)


def near_swap(first):
    return swap(first[0], "fi"), swap(first[1], "ty")


def plane_pieces(parts_o, first, second):
    own, own_c = parts_o
    return own[0], swap(own_c[0], "tc"), first[0], second[0], second[1], first[1]


def piece_sum(pieces):
    own, sib, x_top, x_bot, y_top, y_bot = (piece[...].astype(F32) for piece in pieces)
    cross = jnp.concatenate([x_top + y_top, x_bot + y_bot], axis=0)
    return own + sib + cross


def mix(flag, at_zero, at_one):
    return at_zero * (1.0 - flag) + at_one * flag


def nbytes(shapes):
    return sum(math.prod(shape) * jnp.dtype(dtype).itemsize for shape, dtype in shapes)


def price(us, moved):
    return pl.CostEstimate(flops=int(us * 1.0e9), transcendentals=0, bytes_accessed=moved)


def run(kernel, outs, ins, us, *, grid=(), in_specs=None, out_specs=None, scratch=(), prefetch=0):
    return pl.pallas_call(
        kernel,
        out_shape=[jax.ShapeDtypeStruct(shape, dtype) for shape, dtype in outs],
        grid_spec=pltpu.PrefetchScalarGridSpec(
            num_scalar_prefetch=prefetch,
            grid=grid,
            in_specs=in_specs,
            out_specs=out_specs,
            scratch_shapes=list(scratch),
        ),
        compiler_params=pltpu.CompilerParams(
            vmem_limit_bytes=44 << 20, dimension_semantics=("arbitrary",) * len(grid)
        ),
        cost_estimate=price(us, nbytes(outs) + nbytes([(v.shape, v.dtype) for v in ins])),
    )(*ins)


def whole(shape):
    return pl.BlockSpec(shape, lambda *_: (0,) * len(shape))


def mm(left, right):
    return jnp.dot(left, right, preferred_element_type=F32)


def mm_nt(left, right):
    return lax.dot_general(left, right, (((1,), (1,)), ((), ())), preferred_element_type=F32)


def mm_tn(left, right):
    return lax.dot_general(left, right, (((0,), (0,)), ((), ())), preferred_element_type=F32)


def qkv_kernel(flags, x_ref, place_ref, cos_ref, sin_ref, *refs):
    w_refs, (xin_ref, qrot_ref, qn_ref, kv_ref, kn_ref, fac_ref) = refs[:10], refs[10:16]
    gains_ref, heads_ref = refs[16:]
    fi, ty, tc = (flags[n].astype(F32) for n in range(3))
    gains_ref[...] = w_refs[0][:, 128:256].astype(F32).T[64:72, :]
    line = mm_nt(gains_ref[...].astype(BF), place_ref[...])
    lo, hi = line[:, :128], line[:, 128:]
    heads_ref[...] = jnp.concatenate([mix(fi, lo, hi), mix(fi, hi, lo)], axis=1)
    x = x_ref[...].astype(F32)
    x_factor = lax.rsqrt(jnp.mean(x * x, -1, keepdims=True) + EPS)
    xin = (x * x_factor * gains_ref[0:1, :]).astype(BF)
    xin_ref[...] = xin
    prod = [mm_split(xin, pair) for pair in split_w(w_refs, w_refs[6].shape[0])]
    cos, sin = cos_ref[...], sin_ref[...]
    rows = x.shape[0]
    lane = lax.broadcasted_iota(jnp.int32, (rows, 128), 1)
    factors = jnp.zeros((rows, 128), F32)

    def normed(own, oth, row):
        total = jnp.sum(own * own + oth * oth, -1, keepdims=True)
        factor = lax.rsqrt(total * (1.0 / HD) + EPS)
        own, oth = own * factor, oth * factor
        g_own = own * heads_ref[row : row + 1, :128]
        g_oth = oth * heads_ref[row : row + 1, 128:]
        rot = jnp.concatenate([g_own * cos - g_oth * sin, g_oth * cos + g_own * sin], axis=1)
        return jnp.concatenate([own, oth], axis=1), rot, factor

    for r in range(4):
        norm, rot, factor = normed(prod[r][:, :128], prod[4 + r][:, :128], 4)
        qn_ref[r] = norm.astype(BF)
        qrot_ref[r] = rot.astype(BF)
        factors = jnp.where(lane == r, factor, factors)
    keys, vals = [], []
    for dx in range(2):
        sides = []
        for dy in range(2):
            zero = prod[dx * 4 + dy * 2][:, 128:192]
            one = prod[dx * 4 + dy * 2 + 1][:, 128:192]
            sides.append(jnp.concatenate([mix(tc, zero, one), mix(tc, one, zero)], axis=1))
        keys.append(mix(ty, sides[0], sides[1]))
        vals.append(mix(ty, sides[1], sides[0]))
    norm, rot, factor = normed(keys[0], keys[1], 5)
    kn_ref[...] = norm.astype(BF)
    fac_ref[...] = jnp.where(lane == 4, factor, factors)
    kv_ref[...] = jnp.concatenate([rot, vals[0], vals[1]], axis=1).astype(BF)


def split_w(refs, cut):
    pairs = [(ref[:cut, :], ref[cut:, :]) for ref in refs[:6]]
    return pairs + [(refs[6][...], refs[7][...]), (refs[8][...], refs[9][...])]


def head_w(pairs, r):
    return tuple(jnp.concatenate([pairs[r][n], pairs[4 + r][n]], axis=1) for n in (0, 1))


def mm_split(left, pair):
    cut = pair[0].shape[0]
    return mm(left[:, :cut], pair[0]) + mm(left[:, cut:], pair[1])


def mm_nt_split(left, pair):
    return jnp.concatenate([mm_nt(left, pair[0]), mm_nt(left, pair[1])], axis=1)


def kv_block(refs, kb):
    start = (kb % 2) * 256
    return refs[kb // 2][start : start + 256, :]


def attn_kernel(need, q_ref, k2_ref, kp_ref, ko_ref, bias_ref, o_ref, linv_ref, acc_ref, l_ref):
    i = pl.program_id(0)
    acc_ref[...] = jnp.zeros_like(acc_ref)
    l_ref[...] = jnp.zeros_like(l_ref)
    tile = q_ref.shape[1]
    for kb in range(6):

        @pl.when(need[i * 6 + kb] > 0)
        def _(kb=kb):
            kv = kv_block((k2_ref, kp_ref, ko_ref), kb)
            q = q_ref[...].reshape(4 * tile, HD)
            s = mm_nt(q, kv[:, :HD]).reshape(4, tile, 256) * HD ** (-0.5)
            p = jnp.exp(s + bias_ref[:, kb * 256 : (kb + 1) * 256][None])
            p = p.reshape(4 * tile, 256)
            l_ref[...] += p[:, :128] + p[:, 128:]
            acc_ref[...] += mm(p.astype(BF), kv[:, HD:])

    linv = 1.0 / jnp.sum(l_ref[...], -1, keepdims=True)
    linv_ref[...] = jnp.broadcast_to(linv, (4 * tile, 128)).reshape(4, tile, 128)
    o_ref[...] = (acc_ref[...] * linv).astype(BF).reshape(4, tile, HD)


def out_kernel(o_ref, x_ref, gains_ref, *refs):
    w_refs, (part_ref, hid_ref, ffn_ref) = refs[:10], refs[10:]
    pairs = split_w(w_refs, w_refs[6].shape[0])
    part = jnp.zeros(part_ref.shape, F32)
    for r in range(4):
        part += mm_nt_split(o_ref[r], head_w(pairs, r))
    part_ref[...] = part
    factor = lax.rsqrt(jnp.mean(part * part, -1, keepdims=True) + EPS)
    hidden = x_ref[...].astype(F32) + part * factor * gains_ref[1:2, :]
    hid_ref[...] = hidden
    factor = lax.rsqrt(jnp.mean(hidden * hidden, -1, keepdims=True) + EPS)
    ffn_ref[...] = (hidden * factor * gains_ref[2:3, :]).astype(BF)


def gelu_parts(gate, up):
    c0 = math.sqrt(2.0 / math.pi)
    square = gate * gate
    th = jnp.tanh(gate * (c0 + (0.044715 * c0) * square))
    side = 0.5 + 0.5 * th
    gelu = gate * side
    slope = side + gelu * (1.0 - th) * (c0 + (3.0 * 0.044715 * c0) * square)
    return gelu * up, slope * up, gelu


def ffn_layout(refs, layout):
    at, groups = 0, []
    for block, spans in enumerate(layout):
        row = 0
        for start, count in spans:
            groups.append((block, at, pl.ds(row, count), pl.ds(start, count), refs[at]))
            row += count
            at += 1
    return groups


def ffn_kernel(*refs, layout, base, hpad):
    n_x, blocks = sum(len(spans) for spans in layout), len(layout)
    x_refs, w_ref = refs[:n_x], refs[n_x]
    outs, scr = refs[-(13 + n_x) : -9], refs[-9:]
    all_refs, part_refs = outs[:4], outs[4:]
    xs, act_s, slope_s, gelu_s, part_s, x_sem, out_sem, part_sem, _ = scr
    rows = xs.shape[1]
    stage = (xs, act_s, slope_s, gelu_s)
    loads = [[] for _ in range(blocks)]
    for block, at, row, span, ref in ffn_layout(x_refs, layout):
        copy = pltpu.make_async_copy(ref.at[span, :], xs.at[block, row, :], x_sem.at[at])
        copy.start()
        loads[block].append(copy)

    def stack(block, n):
        dst = all_refs[n].at[pl.ds((base + block) * rows, rows), :]
        return pltpu.make_async_copy(stage[n].at[block], dst, out_sem.at[block, n])

    def part_copies(block):
        groups = [group for group in ffn_layout(part_refs, layout) if group[0] == block]
        return [
            pltpu.make_async_copy(part_s.at[block, row, :], ref, part_sem.at[at])
            for _, at, row, _, ref in groups
        ]

    def one_block(i, carry):
        per_block(i, blocks, lambda block: [copy.wait() for copy in loads[block]])
        stack(i, 0).start()
        x = xs[i]
        for c in range(0, hpad, 256):
            wide = min(256, hpad - c)
            gate = mm(x, w_ref[:, c : c + wide])
            up = mm(x, w_ref[:, hpad + c : hpad + c + wide])
            act, slope, gelu = gelu_parts(gate, up)
            act_s[i, :, c : c + wide] = act.astype(BF)
            slope_s[i, :, c : c + wide] = slope.astype(BF)
            gelu_s[i, :, c : c + wide] = gelu.astype(BF)
        for n in (1, 2, 3):
            stack(i, n).start()
        part_s[i] = mm_nt(act_s[i], w_ref[:, 2 * hpad :]).astype(BF)
        per_block(i, blocks, lambda block: [copy.start() for copy in part_copies(block)])
        return carry

    lax.fori_loop(0, blocks, one_block, 0)
    for block in range(blocks):
        for n in range(4):
            stack(block, n).wait()
        for copy in part_copies(block):
            copy.wait()


def per_block(i, blocks, act):
    for block in range(blocks):

        @pl.when(i == block)
        def _(block=block):
            act(block)


def ffn_back_kernel(*refs, layout, base, hpad):
    n_x, blocks = sum(len(spans) for spans in layout), len(layout)
    x_refs, w_ref, saved_refs = refs[:n_x], refs[n_x], refs[n_x + 1 : n_x + 3]
    outs, scr = refs[-(12 + n_x) : -9], refs[-9:]
    all_refs, part_refs = outs[:3], outs[3:]
    xs, dgu_s, slope_s, gelu_s, part_s, x_sem, out_sem, part_sem, saved_sem = scr
    rows = xs.shape[1]
    stage = (xs, dgu_s.at[:, :, pl.ds(0, hpad)], dgu_s.at[:, :, pl.ds(hpad, hpad)])
    loads = [[] for _ in range(blocks)]

    def saved(block, n):
        src = saved_refs[n].at[pl.ds((base + block) * rows, rows), :]
        dst = (slope_s, gelu_s)[n].at[block]
        copy = pltpu.make_async_copy(src, dst, saved_sem.at[block, n])
        copy.start()
        loads[block].append(copy)

    for block, at, row, span, ref in ffn_layout(x_refs, layout):
        copy = pltpu.make_async_copy(ref.at[span, :], xs.at[block, row, :], x_sem.at[at])
        copy.start()
        loads[block].append(copy)

    for block in range(blocks):
        saved(block, 0)
        saved(block, 1)

    def stack(block, n):
        dst = all_refs[n].at[pl.ds((base + block) * rows, rows), :]
        return pltpu.make_async_copy(stage[n].at[block], dst, out_sem.at[block, n])

    def part_copies(block):
        groups = [group for group in ffn_layout(part_refs, layout) if group[0] == block]
        return [
            pltpu.make_async_copy(part_s.at[block, row, :], ref, part_sem.at[at])
            for _, at, row, _, ref in groups
        ]

    def one_block(i, carry):
        per_block(i, blocks, lambda block: [copy.wait() for copy in loads[block]])
        stack(i, 0).start()
        dout = xs[i]
        for c in range(0, hpad, 256):
            wide = min(256, hpad - c)
            d_act = mm(dout, w_ref[:, 2 * hpad + c : 2 * hpad + c + wide])
            slope = slope_s[i, :, c : c + wide].astype(F32)
            gelu = gelu_s[i, :, c : c + wide].astype(F32)
            dgu_s[i, :, c : c + wide] = (d_act * slope).astype(BF)
            dgu_s[i, :, hpad + c : hpad + c + wide] = (d_act * gelu).astype(BF)
        stack(i, 1).start()
        stack(i, 2).start()
        part_s[i] = mm_nt(dgu_s[i], w_ref[:, : 2 * hpad]).astype(BF)
        per_block(i, blocks, lambda block: [copy.start() for copy in part_copies(block)])
        return carry

    lax.fori_loop(0, blocks, one_block, 0)
    for block in range(blocks):
        for n in range(3):
            stack(block, n).wait()
        for copy in part_copies(block):
            copy.wait()


def hold_kernel(src_ref, dst_ref, sem):
    copy = pltpu.make_async_copy(src_ref, dst_ref, sem.at[0])
    copy.start()
    copy.wait()


def hold(value):
    return pl.pallas_call(
        hold_kernel,
        out_shape=pltpu.VMEM(value.shape, value.dtype),
        in_specs=[pl.BlockSpec(memory_space=pltpu.HBM)],
        out_specs=pl.BlockSpec(memory_space=pltpu.VMEM),
        scratch_shapes=[pltpu.SemaphoreType.DMA((1,))],
        compiler_params=pltpu.CompilerParams(vmem_limit_bytes=16 << 20),
        cost_estimate=price(3, 1000000),
    )(in_hbm(value))


def in_hbm(value):
    return pltpu.with_memory_space_constraint(value, pltpu.HBM)


def ffn_call(kernel, blocks, base, saved, w_ffn, bufs):
    pieces = [value for block in blocks for value, _, _ in block]
    layout = tuple(tuple((start, count) for _, start, count in block) for block in blocks)
    n, back = len(blocks), bool(saved)
    width, hpad = w_ffn.shape[0], w_ffn.shape[1] // 3
    rows = sum(count for _, count in layout[0])
    widths = [width, hpad, hpad] if back else [width, hpad, hpad, hpad]
    ins = [in_hbm(v) for v in pieces] + [w_ffn] + [in_hbm(v) for v in saved]
    aliases = {}
    if bufs is not None:
        aliases = {len(ins) + k: k for k in range(len(widths))}
        ins = ins + [in_hbm(v) for v in bufs]
    hbm = pl.BlockSpec(memory_space=pltpu.HBM)
    in_specs = [hbm] * len(ins)
    in_specs[len(pieces)] = pl.BlockSpec(memory_space=pltpu.VMEM)
    counts = [count for spans in layout for _, count in spans]
    shapes = [((8 * rows, w), BF) for w in widths] + [((count, width), BF) for count in counts]
    mid = [2 * hpad, hpad, hpad] if back else [hpad, hpad, hpad]
    scratch = [pltpu.VMEM((n, rows, w), BF) for w in [width] + mid + [width]]
    scratch += [
        pltpu.SemaphoreType.DMA((len(pieces),)),
        pltpu.SemaphoreType.DMA((n, 4)),
        pltpu.SemaphoreType.DMA((len(pieces),)),
        pltpu.SemaphoreType.DMA((n, 2)),
    ]
    outs = pl.pallas_call(
        partial(kernel, layout=layout, base=base, hpad=hpad),
        out_shape=[pltpu.HBM(shape, dtype) for shape, dtype in shapes],
        in_specs=in_specs,
        out_specs=[hbm] * len(shapes),
        scratch_shapes=scratch,
        input_output_aliases=aliases,
        compiler_params=pltpu.CompilerParams(vmem_limit_bytes=28 << 20),
        cost_estimate=price(6 * n, 1000000 * n),
    )(*ins)
    grouped, at = [], len(widths)
    for spans in layout:
        grouped.append(tuple(outs[at : at + len(spans)]))
        at += len(spans)
    return outs[: len(widths)], grouped


def ffn_mid_kernel(*refs):
    hid_ref, cot_ref, gains_ref, out_ref, dout_ref, gain_ref = refs[6:]
    part = piece_sum(refs[:6])
    gain = gains_ref[3:4, :]
    factor = lax.rsqrt(jnp.mean(part * part, -1, keepdims=True) + EPS)
    out_ref[...] = (hid_ref[...] + part * factor * gain).astype(BF)
    back, gain_grad = norm_back_tile(part, gain, cot_ref[...].astype(F32))
    dout_ref[...] = back.astype(BF)
    gain_ref[0:1, :] = gain_grad


def norm_back_tile(raw, gain, upstream):
    factor = lax.rsqrt(jnp.mean(raw * raw, -1, keepdims=True) + EPS)
    normed = raw * factor
    gain_grad = jnp.sum(upstream * normed, axis=0, keepdims=True)
    scaled = upstream * gain
    back = factor * (scaled - normed * jnp.mean(scaled * normed, -1, keepdims=True))
    return back, gain_grad


def mid_kernel(*refs):
    hid_ref, part_ref, cot_ref, gains_ref = refs[6:10]
    w_refs, (dhid_ref, dpart_ref, dhead_ref, gain_ref) = refs[10:20], refs[20:]
    din = piece_sum(refs[:6])
    extra, gain_ffn = norm_back_tile(hid_ref[...], gains_ref[2:3, :], din)
    dhid = cot_ref[...].astype(F32) + extra
    dhid_ref[...] = dhid
    dpart, gain_post = norm_back_tile(part_ref[...], gains_ref[1:2, :], dhid)
    dpart = dpart.astype(BF)
    dpart_ref[...] = dpart
    gain_ref[0:1, :] = gain_ffn
    gain_ref[1:2, :] = gain_post
    pairs = split_w(w_refs, w_refs[6].shape[0])
    for r in range(4):
        dhead_ref[r] = mm_split(dpart, head_w(pairs, r)).astype(BF)


def attn_back_kernel(
    need,
    q_ref,
    k2_ref,
    kp_ref,
    ko_ref,
    bias_ref,
    o_ref,
    do_ref,
    linv_ref,
    qn_ref,
    fac_ref,
    cos_ref,
    sin_ref,
    gq_ref,
    dq_ref,
    d2_ref,
    dp_ref,
    down_ref,
    gain_ref,
    acc_ref,
    dkv_ref,
):
    i = pl.program_id(0)
    tile = q_ref.shape[1]

    @pl.when(i == 0)
    def _():
        dkv_ref[...] = jnp.zeros_like(dkv_ref)
        gain_ref[...] = jnp.zeros_like(gain_ref)

    acc_ref[...] = jnp.zeros_like(acc_ref)
    q = q_ref[...].reshape(4 * tile, HD)
    do = do_ref[...].reshape(4 * tile, HD)
    linv = linv_ref[...].reshape(4 * tile, 128)[:, 0:1]
    inner = jnp.sum(do.astype(F32) * o_ref[...].reshape(4 * tile, HD).astype(F32), -1, keepdims=True)
    for kb in range(6):

        @pl.when(need[i * 6 + kb] > 0)
        def _(kb=kb):
            kv = kv_block((k2_ref, kp_ref, ko_ref), kb)
            keys, vals = kv[:, :HD], kv[:, HD:]
            s = mm_nt(q, keys).reshape(4, tile, 256) * HD ** (-0.5)
            p = jnp.exp(s + bias_ref[:, kb * 256 : (kb + 1) * 256][None])
            p = p.reshape(4 * tile, 256) * linv
            dp = mm_nt(do, vals)
            ds = (p * (dp - inner)).astype(BF)
            acc_ref[...] += mm(ds, keys)
            span = slice(kb * 256, (kb + 1) * 256)
            dkv_ref[span, :HD] += mm_tn(ds, q)
            dkv_ref[span, HD:] += mm_tn(p.astype(BF), do)

    cos, sin = cos_ref[...], sin_ref[...]
    gain = jnp.zeros((1, HD), F32)
    for r in range(4):
        dq = acc_ref[r * tile : (r + 1) * tile, :] * HD ** (-0.5)
        own, oth = dq[:, :128], dq[:, 128:]
        back = jnp.concatenate([own * cos + oth * sin, oth * cos - own * sin], axis=1)
        norm = qn_ref[r].astype(F32)
        gain += jnp.sum(back * norm, axis=0, keepdims=True)
        scaled = back * gq_ref[4:5, :]
        mean = jnp.mean(scaled * norm, -1, keepdims=True)
        dq_ref[r] = (fac_ref[:, r : r + 1] * (scaled - norm * mean)).astype(BF)
    gain_ref[0:1, :] += gain

    @pl.when(i == pl.num_programs(0) - 1)
    def _():
        rows = d2_ref.shape[0]
        scale = HD ** (-0.5)
        for n, ref in enumerate((d2_ref, dp_ref, down_ref)):
            block = dkv_ref[n * rows : (n + 1) * rows, :]
            ref[:, :HD] = (block[:, :HD] * scale).astype(ref.dtype)
            ref[:, HD:] = block[:, HD:].astype(ref.dtype)


def post_kernel(
    flags,
    dq_ref,
    dkv_ref,
    dp_ref,
    kn_ref,
    fac_ref,
    cos_ref,
    sin_ref,
    gk_ref,
    x_ref,
    gains_ref,
    dhid_ref,
    gq_grad,
    mid_grad,
    post_grad,
    place_ref,
    *refs,
):
    w_refs, din_ref, kvraw_ref, gain_ref = refs[:10], *refs[10:]
    fi, ty, tc = (flags[n].astype(F32) for n in range(3))
    dkv = dkv_ref[...] + dp_ref[...].astype(F32)
    cos, sin = cos_ref[...], sin_ref[...]
    own, oth = dkv[:, :128], dkv[:, 128:256]
    back = jnp.concatenate([own * cos + oth * sin, oth * cos - own * sin], axis=1)
    norm = kn_ref[...].astype(F32)
    gk_grad = jnp.sum(back * norm, axis=0, keepdims=True)
    scaled = back * gk_ref[5:6, :]
    mean = jnp.mean(scaled * norm, -1, keepdims=True)
    dkey = fac_ref[:, 4:5] * (scaled - norm * mean)
    dval = dkv[:, 256:]
    kvraw_ref[...] = jnp.concatenate([dkey, dval], axis=1).astype(BF)
    din = jnp.zeros(din_ref.shape, F32)
    zeros = jnp.zeros((dkv.shape[0], 64), F32)
    pairs = split_w(w_refs, w_refs[6].shape[0])
    rel = 0
    for dx in range(2):
        kh = dkey[:, dx * 128 : (dx + 1) * 128]
        vh = dval[:, dx * 128 : (dx + 1) * 128]
        for dy in range(2):
            half = mix(ty, kh, vh) if dy == 0 else mix(ty, vh, kh)
            for dc in range(2):
                lo, hi = half[:, :64], half[:, 64:]
                part = mix(tc, lo, hi) if dc == 0 else mix(tc, hi, lo)
                side = jnp.concatenate([part, zeros], axis=1).astype(BF)
                dprod = jnp.concatenate(
                    [dq_ref[dy * 2 + dc][:, dx * 128 : (dx + 1) * 128], side], axis=1
                )
                din += mm_nt_split(dprod, pairs[rel])
                rel += 1
    x = x_ref[...].astype(F32)
    extra, gain_pre = norm_back_tile(x, gains_ref[0:1, :], din)
    din_ref[...] = dhid_ref[...] + extra

    def spread(grad):
        own, oth = grad[:, :128], grad[:, 128:]
        whole_row = jnp.concatenate([mix(fi, own, oth), mix(fi, oth, own)], axis=1)
        return mm(jnp.broadcast_to(whole_row.astype(BF), (8, HD)), place_ref[...])[0:1, :]

    gain_ref[...] = jnp.zeros_like(gain_ref)
    gain_ref[0:1, :] = gain_pre
    gain_ref[1:2, :] = mid_grad[1:2, :]
    gain_ref[2:3, :] = mid_grad[0:1, :]
    gain_ref[3:4, :] = post_grad[0:1, :]
    gain_ref[4:5, :] = spread(gq_grad[0:1, :])
    gain_ref[5:6, :] = spread(gk_grad)


def store_rows(refs, value):
    cut = refs[0].shape[0]
    refs[0][...] = value[:cut, :]
    refs[1][...] = value[cut:, :]


def qo_grad_kernel(xin, xin_c, dq, dq_c, dpart, dpart_c, head, head_c, *outs):
    xt, xt_c, dt, dt_c = (ref[...].T for ref in (xin, xin_c, dpart, dpart_c))
    for dy in range(2):
        gq = (mm(xt, dq[2 * dy]) + mm(xt_c, dq_c[dy])).astype(BF)
        go = (mm(dt, head[2 * dy]) + mm(dt_c, head_c[dy])).astype(BF)
        for dx in range(2):
            half = slice(dx * 128, (dx + 1) * 128)
            at = 4 * dx + 2 * dy
            store_rows(outs[at : at + 2], jnp.concatenate([gq[:, half], go[:, half]], axis=1))


def kv_grad_kernel(flags, xin, xin_c, kv, kv_c, gain, gain_c, *refs):
    outs, rows_ref = refs[:8], refs[8]
    ty, tc = flags[1].astype(F32), flags[2].astype(F32)
    rows_ref[...] = jnp.zeros_like(rows_ref)
    rows_ref[64:72, :] = gain[...] + gain_c[...]
    gain_cols = rows_ref[...].T
    xt, xt_c = xin[...].T, xin_c[...].T

    def sides(ref):
        block = ref[...].astype(F32)
        picked = []
        for dy in range(2):
            for dx in range(2):
                kh = block[:, dx * 128 : (dx + 1) * 128]
                vh = block[:, 256 + dx * 128 : 256 + (dx + 1) * 128]
                half = mix(ty, kh, vh) if dy == 0 else mix(ty, vh, kh)
                picked.append(mix(tc, half[:, :64], half[:, 64:]))
        return jnp.concatenate(picked, axis=1).astype(BF)

    grad = mm(xt, sides(kv)) + mm(xt_c, sides(kv_c))
    zeros = jnp.zeros((grad.shape[0], 64), F32)
    for dy in range(2):
        for dx in range(2):
            at = 4 * dx + 2 * dy
            col = (2 * dy + dx) * 64
            part = jnp.concatenate([grad[:, col : col + 64], zeros], axis=1) + gain_cols
            store_rows(outs[at : at + 2], part.astype(BF))


def chip_reduce(parts):
    own, near_y, near_x, far = (parts[n : n + 2] for n in (0, 2, 4, 6))
    from_x, from_y = swap(far[0], "fi"), swap(far[1], "ty")
    got_x_top, got_y_bot = swap(near_x[0], "fi"), swap(near_y[1], "ty")
    x_bot = (near_x[1].astype(F32) + from_y.astype(F32)).astype(BF)
    y_top = (near_y[0].astype(F32) + from_x.astype(F32)).astype(BF)
    return (*own, got_x_top, swap(x_bot, "fi"), swap(y_top, "ty"), got_y_bot)


def gather_sum_kernel(*refs):
    out_ref = refs[12]
    for n, cols in ((0, slice(0, 256)), (6, slice(256, 384))):
        own_top, own_bot, x_top, x_bot, y_top, y_bot = (ref[...].astype(F32) for ref in refs[n : n + 6])
        cut = own_top.shape[0]
        out_ref[:cut, cols] = (own_top + x_top + y_top).astype(BF)
        out_ref[cut:, cols] = (own_bot + x_bot + y_bot).astype(BF)


def pad_cols(value, width):
    return jnp.pad(value, ((0, 0), (0, width - value.shape[1])))


def body(
    tokens,
    positions,
    segments,
    w_query,
    w_key,
    w_value,
    w_out,
    w_gate,
    w_up,
    w_down,
    gain_attn_pre,
    gain_query,
    gain_key,
    gain_attn_post,
    gain_ffn_pre,
    gain_ffn_post,
    cotangent,
):
    fi = lax.axis_index("fi")
    ty = lax.axis_index("ty")
    tc = lax.axis_index("tc")
    t_idx = ty * 2 + tc
    me = fi * 4 + t_idx
    first = fi == 0
    rows = tokens.shape[0]
    width = tokens.shape[1]
    shard = w_query.shape[0]
    nf = width // shard
    hid = w_gate.shape[1] // 2
    hpad = -(-hid // 128) * 128
    gshard = gain_query.shape[0]

    def pair_rows(keep, recv):
        return jnp.where(
            first,
            jnp.concatenate([keep, recv], axis=0),
            jnp.concatenate([recv, keep], axis=0),
        )

    kv_mine = jnp.where(ty == 0, w_key, w_value)
    out_t = w_out.T
    gains = pad_cols(
        jnp.stack(
            [
                gain_attn_pre,
                gain_attn_post,
                gain_ffn_pre,
                gain_ffn_post,
                jnp.pad(gain_query, (0, shard - gshard)),
                jnp.pad(gain_key, (0, shard - gshard)),
            ],
            axis=1,
        ),
        64,
    )

    def piece(h):
        kv_half = kv_mine[:, h * 128 : (h + 1) * 128]
        kv_part = jnp.where(tc == 0, kv_half[:, :64], kv_half[:, 64:])
        return jnp.concatenate(
            [
                w_query[:, h * 128 : (h + 1) * 128],
                kv_part,
                gains,
                out_t[:, h * 128 : (h + 1) * 128],
            ],
            axis=1,
        )

    piece0, piece1 = piece(0), piece(1)
    keep = jnp.where(first, piece0, piece1)
    recv = swap(jnp.where(first, piece1, piece0), "fi")

    down_t = w_down.T

    def halves(weight):
        lo, hi = pad_cols(weight[:, :hid], hpad), pad_cols(weight[:, hid:], hpad)
        return jnp.where(first, lo, hi), jnp.where(first, hi, lo)

    gate_keep, gate_send = halves(w_gate)
    up_keep, up_send = halves(w_up)
    down_keep, down_send = halves(down_t)
    ffn_keep = jnp.concatenate([gate_keep, up_keep, down_keep], axis=1)
    ffn_send = jnp.concatenate([gate_send, up_send, down_send], axis=1)
    ffn_send, ffn_keep, recv = lax.optimization_barrier((ffn_send, ffn_keep, recv))
    ffn_recv = swap(ffn_send, "fi")
    attn_col = lax.all_gather(pair_rows(keep, recv), "fo", axis=0, tiled=True)
    attn_col, ffn_pair = lax.optimization_barrier((attn_col, pair_rows(ffn_keep, ffn_recv)))
    w_ffn = lax.all_gather(ffn_pair, "fo", axis=0, tiled=True)

    elem = lax.broadcasted_iota(jnp.int32, (HD, width), 0)
    spot = lax.broadcasted_iota(jnp.int32, (HD, width), 1)
    place = (spot == (elem // gshard) * shard + elem % gshard).astype(BF)
    cut = width // 256 * 128
    row_start = t_idx * rows
    pos_local = lax.dynamic_slice_in_dim(positions, row_start, rows)
    seg_local = lax.dynamic_slice_in_dim(segments, row_start, rows)

    def block_of(meta, back):
        return lax.dynamic_slice_in_dim(meta, ((t_idx - back) % 4) * rows, rows)

    k_pos = jnp.concatenate([block_of(positions, 2), block_of(positions, 1), pos_local])
    k_seg = jnp.concatenate(
        [
            jnp.where(t_idx == 3, block_of(segments, 2), -1),
            jnp.where(t_idx >= 1, block_of(segments, 1), -1),
            seg_local,
        ]
    )
    allowed = (
        ((k_seg[None, :] == 0) | (k_seg[None, :] == seg_local[:, None]))
        & (k_pos[None, :] <= pos_local[:, None])
        & (pos_local[:, None] - k_pos[None, :] < WINDOW)
    )
    bias = jnp.where(allowed, 0.0, NEG).astype(F32)
    need = jnp.any(allowed.reshape(4, rows // 4, 6, rows // 2), axis=(1, 3))
    need = need.astype(jnp.int32).reshape(24)
    frequency = jnp.exp(-math.log(BASE) * jnp.arange(HALF).astype(F32) / HALF)
    angles = pos_local.astype(F32)[:, None] * frequency
    cosine = jnp.cos(angles)
    sine = jnp.sin(angles) * jnp.where(first, 1.0, -1.0)

    w_parts, (bias, need, cosine, sine, place) = plane_gather(
        attn_col, cut, (bias, need, cosine, sine, place)
    )
    w_parts = [in_hbm(piece) for pieces in w_parts for piece in pieces]
    flags = jnp.stack([fi, ty, tc]).astype(jnp.int32)
    qkv_spec = [pl.BlockSpec((part.shape[0], 256), lambda *_: (0, 0)) for part in w_parts]
    wo_spec = [pl.BlockSpec((part.shape[0], 128), lambda *_: (0, 2)) for part in w_parts]
    full, gains8 = whole((rows, width)), whole((8, width))
    heads = whole((4, rows, HD))
    lanes = whole((rows, 128))
    kv_full = whole((rows, 2 * HD))
    attn_in, q_rot, q_norm, kv_own, k_norm, factors, gain_rows, head_gains = run(
        qkv_kernel,
        [
            ((rows, width), BF),
            ((4, rows, HD), BF),
            ((4, rows, HD), BF),
            ((rows, 2 * HD), BF),
            ((rows, HD), BF),
            ((rows, 128), F32),
            ((8, width), F32),
            ((8, HD), F32),
        ],
        (flags, tokens, place, cosine, sine, *w_parts),
        9,
        grid=(1,),
        in_specs=[full, whole((HD, width)), lanes, lanes] + qkv_spec,
        out_specs=[full, heads, heads, kv_full, whole((rows, HD)), lanes, gains8, whole((8, HD))],
        prefetch=1,
    )
    kv_prev = lax.ppermute(kv_own, ("ty", "tc"), [(i, (i + 1) % 4) for i in range(4)])
    kv_two = swap(kv_prev, "tc")
    tile = rows // 4
    q_tile = pl.BlockSpec((4, tile, HD), lambda i, *_: (0, i, 0))
    l_tile = pl.BlockSpec((4, tile, 128), lambda i, *_: (0, i, 0))
    bias_tile = pl.BlockSpec((tile, 3 * rows), lambda i, *_: (i, 0))
    head_out, linv = run(
        attn_kernel,
        [((4, rows, HD), BF), ((4, rows, 128), F32)],
        (need, q_rot, kv_two, kv_prev, kv_own, bias),
        8,
        grid=(4,),
        in_specs=[q_tile, kv_full, kv_full, kv_full, bias_tile],
        out_specs=[q_tile, l_tile],
        scratch=[pltpu.VMEM((4 * tile, HD), F32), pltpu.VMEM((4 * tile, 128), F32)],
        prefetch=1,
    )
    attn_part, hidden, ffn_local = run(
        out_kernel,
        [((rows, width), F32), ((rows, width), F32), ((rows, width), BF)],
        (head_out, tokens, gain_rows, *w_parts),
        6,
        grid=(1,),
        in_specs=[heads, full, gains8] + wo_spec,
        out_specs=[full, full, full],
    )

    half = rows // 2
    def far_pieces(top, bot, after):
        top, bot, after = lax.optimization_barrier((top, bot, after))
        return (top, bot), (swap(top, "tc"), swap(bot, "tc")), after

    by_x, by_y, by_c = swap(ffn_local, "fi"), swap(ffn_local, "ty"), swap(ffn_local, "tc")
    top, bot = swap(by_y[:half], "fi"), swap(by_x[half:], "ty")
    by_xc, by_yc = swap(by_x, "tc"), swap(by_y, "tc")
    w_ffn = hold(w_ffn)
    top, bot, w_ffn = lax.optimization_barrier((top, bot, w_ffn))
    top_c, bot_c = swap(top, "tc"), swap(bot, "tc")
    whole_of = lambda value: [(value, 0, rows)]
    halves_of = lambda low, high: [(low, 0, half), (high, half, half)]
    both_of = lambda top, bot: [(top, 0, half), (bot, 0, half)]
    far = [both_of(top, bot), both_of(top_c, bot_c)]
    bufs, parts_f = ffn_call(ffn_kernel, far, 6, [], w_ffn, None)
    sent = far_sum(*parts_f, half)
    by_x, by_y, by_xc, by_yc, sent = lax.optimization_barrier((by_x, by_y, by_xc, by_yc, sent))
    got = far_swap(sent)
    first_rows = [halves_of(by_x, by_y), halves_of(by_xc, by_yc)]
    bufs, parts_1 = ffn_call(ffn_kernel, first_rows, 2, [], w_ffn, bufs)
    by_x, by_y, by_xc, by_yc, got = lax.optimization_barrier((by_x, by_y, by_xc, by_yc, got))
    second_rows = [
        [(by_x, half, half), (by_y, 0, half)],
        [(by_xc, half, half), (by_yc, 0, half)],
    ]
    bufs, parts_2 = ffn_call(ffn_kernel, second_rows, 4, [], w_ffn, bufs)
    first_in = near_swap(near_first(parts_1))
    second_out = near_second(parts_2, got)
    first_in, second_out = lax.optimization_barrier((first_in, second_out))
    second_in = near_swap(second_out)
    (x_all, act_all, slope_all, gelu_all), parts_o = ffn_call(
        ffn_kernel, [whole_of(ffn_local), whole_of(by_c)], 0, [], w_ffn, bufs
    )
    pieces = plane_pieces(parts_o, first_in, second_in)
    quarter = whole((half, width))
    piece_spec = [full, full] + [quarter] * 4

    other = swap(jnp.stack([head_out[1], head_out[3]]), "tc"), swap(attn_in, "tc")
    pieces, (head_out_c, attn_in_c) = lax.optimization_barrier((pieces, other))
    output, d_local, ffn_post_grad = run(
        ffn_mid_kernel,
        [((rows, width), BF), ((rows, width), BF), ((8, width), F32)],
        (*pieces, hidden, cotangent, gain_rows),
        6,
        grid=(1,),
        in_specs=piece_spec + [full, full, gains8],
        out_specs=[full, full, gains8],
    )
    by_x, by_y, by_c = swap(d_local, "fi"), swap(d_local, "ty"), swap(d_local, "tc")
    saved = [slope_all, gelu_all]
    own_rows = [whole_of(d_local), whole_of(by_c)]
    bufs, parts_o = ffn_call(ffn_back_kernel, own_rows, 0, saved, w_ffn, None)
    by_x, by_y, parts_o = lax.optimization_barrier((by_x, by_y, parts_o))
    top, bot = swap(by_y[:half], "fi"), swap(by_x[half:], "ty")
    by_xc, by_yc = swap(by_x, "tc"), swap(by_y, "tc")
    first_rows = [halves_of(by_x, by_y), halves_of(by_xc, by_yc)]
    bufs, parts_1 = ffn_call(ffn_back_kernel, first_rows, 2, saved, w_ffn, bufs)
    (top, bot), (top_c, bot_c), parts_1 = far_pieces(top, bot, parts_1)
    first_in = near_swap(near_first(parts_1))
    far = [both_of(top, bot), both_of(top_c, bot_c)]
    bufs, parts_f = ffn_call(ffn_back_kernel, far, 6, saved, w_ffn, bufs)
    second_rows = [
        [(by_x, half, half), (by_y, 0, half)],
        [(by_xc, half, half), (by_yc, 0, half)],
    ]
    (d_all, dgate_all, dup_all), parts_2 = ffn_call(
        ffn_back_kernel, second_rows, 4, saved, w_ffn, bufs
    )
    sent = far_sum(*parts_f, half)
    d_all, sent, first_in = lax.optimization_barrier((d_all, sent, first_in))
    got = far_swap(sent)
    grad_dt = dot_left_t(d_all, act_all).astype(BF)
    dgate_all, grad_dt, got = lax.optimization_barrier((dgate_all, grad_dt, got))
    second_in = near_swap(near_second(parts_2, got))
    grad_gate = dot_left_t(x_all, dgate_all).astype(BF)
    pieces = plane_pieces(parts_o, first_in, second_in)
    pieces, grad_gate = lax.optimization_barrier((pieces, grad_gate))
    sum_dt = lax.psum_scatter(grad_dt, "fo", scatter_dimension=0, tiled=True)
    sum_gate = lax.psum_scatter(grad_gate, "fo", scatter_dimension=0, tiled=True)

    def unpair(summed):
        top_rows, bot_rows = summed[:shard], summed[shard:]
        mine = jnp.where(first, top_rows, bot_rows)
        theirs = swap(jnp.where(first, bot_rows, top_rows), "fi")
        return jnp.where(first, mine, theirs), jnp.where(first, theirs, mine)

    def join(lo, hi):
        return jnp.concatenate([lo[:, :hid], hi[:, :hid]], axis=1).astype(F32)

    hidden_grad, attn_part_grad, head_grad, mid_gains = run(
        mid_kernel,
        [((rows, width), F32), ((rows, width), BF), ((4, rows, HD), BF), ((8, width), F32)],
        (*pieces, hidden, attn_part, cotangent, gain_rows, *w_parts),
        10,
        grid=(1,),
        in_specs=piece_spec + [full, full, full, gains8] + wo_spec,
        out_specs=[full, full, heads, whole((8, width))],
    )
    fac_tile = pl.BlockSpec((tile, 128), lambda i, *_: (i, 0))
    line = whole((8, HD))
    q_raw_grad, kv_grad_two, kv_grad_prev, kv_grad_own, gain_q = run(
        attn_back_kernel,
        [
            ((4, rows, HD), BF),
            ((rows, 2 * HD), BF),
            ((rows, 2 * HD), BF),
            ((rows, 2 * HD), F32),
            ((8, HD), F32),
        ],
        (
            need,
            q_rot,
            kv_two,
            kv_prev,
            kv_own,
            bias,
            head_out,
            head_grad,
            linv,
            q_norm,
            factors,
            cosine,
            sine,
            head_gains,
        ),
        12,
        grid=(4,),
        in_specs=[
            q_tile,
            kv_full,
            kv_full,
            kv_full,
            bias_tile,
            q_tile,
            q_tile,
            l_tile,
            q_tile,
            fac_tile,
            fac_tile,
            fac_tile,
            line,
        ],
        out_specs=[q_tile, kv_full, kv_full, kv_full, whole((8, HD))],
        scratch=[pltpu.VMEM((4 * tile, HD), F32), pltpu.VMEM((3 * rows, 2 * HD), F32)],
        prefetch=1,
    )
    back_two = kv_grad_prev.astype(F32) + swap(kv_grad_two, "tc").astype(F32)
    q_raw_grad, dup_all, back_two = lax.optimization_barrier(
        (q_raw_grad, dup_all, back_two.astype(BF))
    )
    grad_up = dot_left_t(x_all, dup_all).astype(BF)
    back_prev = lax.ppermute(back_two, ("ty", "tc"), [(i, (i + 3) % 4) for i in range(4)])
    def row_pieces(cols):
        return [((n, cols), BF) for n in (cut, width - cut)] * 4

    other_heads = lambda value: swap(jnp.stack([value[1], value[3]]), "tc")
    two_heads = whole((2, rows, HD))
    qo_grads = run(
        qo_grad_kernel,
        row_pieces(256),
        (
            attn_in,
            attn_in_c,
            q_raw_grad,
            other_heads(q_raw_grad),
            attn_part_grad,
            swap(attn_part_grad, "tc"),
            head_out,
            head_out_c,
        ),
        5,
        grid=(1,),
        in_specs=[full, full, heads, two_heads, full, full, heads, two_heads],
        out_specs=[whole(shape) for shape, _ in row_pieces(256)],
    )
    back_prev, sum_dt, grad_up = lax.optimization_barrier((back_prev, sum_dt, grad_up))
    sum_up = lax.psum_scatter(grad_up, "fo", scatter_dimension=0, tiled=True)
    qo_pieces = chip_reduce(qo_grads)
    input_grad, kv_raw_grad, gain_grads = run(
        post_kernel,
        [((rows, width), F32), ((rows, 2 * HD), BF), ((8, width), F32)],
        (
            flags,
            q_raw_grad,
            kv_grad_own,
            back_prev,
            k_norm,
            factors,
            cosine,
            sine,
            head_gains,
            tokens,
            gain_rows,
            hidden_grad,
            gain_q,
            mid_gains,
            ffn_post_grad,
            place,
            *w_parts,
        ),
        9,
        grid=(1,),
        in_specs=[heads, kv_full, kv_full, whole((rows, HD)), lanes, lanes, lanes, line]
        + [full, gains8, full, whole((8, HD)), gains8, gains8]
        + [whole((HD, width))]
        + qkv_spec,
        out_specs=[full, kv_full, gains8],
        prefetch=1,
    )
    kv_grads = run(
        kv_grad_kernel,
        row_pieces(128),
        (
            flags,
            attn_in,
            attn_in_c,
            kv_raw_grad,
            swap(kv_raw_grad, "tc"),
            gain_grads,
            swap(gain_grads, "tc"),
        ),
        3,
        grid=(1,),
        in_specs=[full, full, kv_full, kv_full, gains8, gains8],
        out_specs=[whole(shape) for shape, _ in row_pieces(128)],
        scratch=[pltpu.VMEM((128, width), F32)],
        prefetch=1,
    )
    kv_pieces = chip_reduce(kv_grads)
    qo_pieces, kv_pieces, sum_gate, sum_up = lax.optimization_barrier(
        (qo_pieces, kv_pieces, sum_gate, sum_up)
    )
    (attn_grads,) = run(
        gather_sum_kernel,
        [((width, 384), BF)],
        (*qo_pieces, *kv_pieces),
        2,
        grid=(1,),
        in_specs=[whole(piece.shape) for piece in (*qo_pieces, *kv_pieces)],
        out_specs=[whole((width, 384))],
    )
    sum_attn = lax.psum_scatter(attn_grads, "fo", scatter_dimension=0, tiled=True)
    dt_lo, dt_hi = unpair(sum_dt)
    grad_gate = join(*unpair(sum_gate))
    grad_up = join(*unpair(sum_up))
    grad_down = join(dt_lo, dt_hi).T

    a_lo, a_hi = unpair(sum_attn)
    grad_out = jnp.concatenate([a_lo[:, 128:256], a_hi[:, 128:256]], axis=1).astype(F32).T
    grad_query = jnp.concatenate([a_lo[:, :128], a_hi[:, :128]], axis=1).astype(F32)
    kv_part = jnp.concatenate([a_lo[:, 256:320], a_hi[:, 256:320]], axis=1)
    others = [
        lax.ppermute(kv_part, ("ty", "tc"), [(i, i ^ step) for i in range(4)]) for step in (1, 2, 3)
    ]
    row_here = jnp.where(tc == 0, 0, 1)

    def kv_lines(near, far):
        even = jnp.where(row_here == 0, near, far)
        odd = jnp.where(row_here == 0, far, near)
        return jnp.concatenate([even[:, :64], odd[:, :64], even[:, 64:], odd[:, 64:]], axis=1)

    kv_here, kv_far = kv_lines(kv_part, others[0]), kv_lines(others[1], others[2])
    grad_key = jnp.where(ty == 0, kv_here, kv_far).astype(F32)
    grad_value = jnp.where(ty == 0, kv_far, kv_here).astype(F32)
    gain_out = a_lo[:, 320:328].astype(F32).T
    return (
        output.astype(BF),
        input_grad,
        grad_query,
        grad_key,
        grad_value,
        grad_out,
        grad_gate,
        grad_up,
        grad_down,
        gain_out[0],
        gain_out[4, :gshard],
        gain_out[5, :gshard],
        gain_out[1],
        gain_out[2],
        gain_out[3],
    )


def solution(mesh):
    nf, nt = mesh.shape["fsdp"], mesh.shape["tensor"]
    fine = Mesh(mesh.devices.reshape(nf // 2, 2, nt // 2, 2), ("fo", "fi", "ty", "tc"))
    f_axes, t_axes = ("fo", "fi"), ("ty", "tc")
    rows = P(f_axes + t_axes, None)
    col = P(f_axes, t_axes)
    flat = P(f_axes, None)
    out_w = P(t_axes, f_axes)
    vec = P(f_axes)
    in_specs = (rows, vec, vec, col, flat, flat, out_w, col, col, out_w) + (vec,) * 6 + (rows,)
    out_specs = (rows, rows, col, flat, flat, out_w, col, col, out_w) + (vec,) * 6
    return jax.shard_map(body, mesh=fine, in_specs=in_specs, out_specs=out_specs, check_vma=False)
```

```python
import math
from functools import partial

import jax
import jax.numpy as jnp
from jax import lax
from jax.experimental import pallas as pl
from jax.experimental.pallas import tpu as pltpu
from jax.sharding import Mesh, PartitionSpec as P

HD = 256
WINDOW = 512
PROMPT = 1024
CONT = 8
CLEN = 128


EPS = 1e-06
NEG = -1e30
BASE = 10000.0
HALF = HD // 2
BF = jnp.bfloat16
F32 = jnp.float32


def dot_left_t(left_op, right_op):
    return lax.dot_general(
        left_op, right_op, (((0,), (0,)), ((), ())), preferred_element_type=jnp.float32
    )


def swap(value, axis):
    return lax.ppermute(value, axis, [(0, 1), (1, 0)])


RELS = [(dx, dy, dc) for dx in (0, 1) for dy in (0, 1) for dc in (0, 1)]


def plane_gather(own, cut, side):
    by_x = swap(own, "fi")
    by_y = swap(own, "ty")
    by_c = swap(own, "tc")
    by_x, by_y, side = lax.optimization_barrier((by_x, by_y, side))
    diag_top = swap(by_y[:cut], "fi")
    diag_bot = swap(by_x[cut:], "ty")
    by_xc = swap(by_x, "tc")
    by_yc = swap(by_y, "tc")
    return [
        (own,),
        (by_c,),
        (by_y,),
        (by_yc,),
        (by_x,),
        (by_xc,),
        (diag_top, diag_bot),
        (swap(diag_top, "tc"), swap(diag_bot, "tc")),
    ], side


def core_add(mine, other):
    return mine.astype(F32) + swap(other, "tc").astype(F32)


def far_sum(far, far_c, cut):
    if len(far) == 1:
        far, far_c = (far[0][:cut], far[0][cut:]), (far_c[0][:cut], far_c[0][cut:])
    return core_add(far[0], far_c[0]).astype(BF), core_add(far[1], far_c[1]).astype(BF)


def far_swap(sent):
    return swap(sent[0], "fi"), swap(sent[1], "ty")


def near_first(parts):
    (x_top, y_bot), (x_top_c, y_bot_c) = parts
    return core_add(x_top, x_top_c).astype(BF), core_add(y_bot, y_bot_c).astype(BF)


def near_second(parts, got):
    (x_bot, y_top), (x_bot_c, y_top_c) = parts
    x_bot = core_add(x_bot, x_bot_c) + got[1].astype(F32)
    y_top = core_add(y_top, y_top_c) + got[0].astype(F32)
    return x_bot.astype(BF), y_top.astype(BF)


def near_swap(first):
    return swap(first[0], "fi"), swap(first[1], "ty")


def plane_pieces(parts_o, first, second):
    own, own_c = parts_o
    return own[0], swap(own_c[0], "tc"), first[0], second[0], second[1], first[1]


def piece_sum(pieces):
    own, sib, x_top, x_bot, y_top, y_bot = (piece[...].astype(F32) for piece in pieces)
    cross = jnp.concatenate([x_top + y_top, x_bot + y_bot], axis=0)
    return own + sib + cross


def mix(flag, at_zero, at_one):
    return at_zero * (1.0 - flag) + at_one * flag


def nbytes(shapes):
    return sum(math.prod(shape) * jnp.dtype(dtype).itemsize for shape, dtype in shapes)


def price(us, moved):
    return pl.CostEstimate(flops=int(us * 1.0e9), transcendentals=0, bytes_accessed=moved)


def run(kernel, outs, ins, us, *, grid=(), in_specs=None, out_specs=None, scratch=(), prefetch=0):
    return pl.pallas_call(
        kernel,
        out_shape=[jax.ShapeDtypeStruct(shape, dtype) for shape, dtype in outs],
        grid_spec=pltpu.PrefetchScalarGridSpec(
            num_scalar_prefetch=prefetch,
            grid=grid,
            in_specs=in_specs,
            out_specs=out_specs,
            scratch_shapes=list(scratch),
        ),
        compiler_params=pltpu.CompilerParams(
            vmem_limit_bytes=44 << 20, dimension_semantics=("arbitrary",) * len(grid)
        ),
        cost_estimate=price(us, nbytes(outs) + nbytes([(v.shape, v.dtype) for v in ins])),
    )(*ins)


def whole(shape):
    return pl.BlockSpec(shape, lambda *_: (0,) * len(shape))


def mm(left, right):
    return jnp.dot(left, right, preferred_element_type=F32)


def mm_nt(left, right):
    return lax.dot_general(left, right, (((1,), (1,)), ((), ())), preferred_element_type=F32)


def mm_tn(left, right):
    return lax.dot_general(left, right, (((0,), (0,)), ((), ())), preferred_element_type=F32)


def qkv_kernel(flags, x_ref, place_ref, cos_ref, sin_ref, *refs):
    w_refs, (xin_ref, qrot_ref, qn_ref, kv_ref, kn_ref, fac_ref) = refs[:10], refs[10:16]
    gains_ref, heads_ref = refs[16:]
    fi, ty, tc = (flags[n].astype(F32) for n in range(3))
    gains_ref[...] = w_refs[0][:, 128:256].astype(F32).T[64:72, :]
    line = mm_nt(gains_ref[...].astype(BF), place_ref[...])
    lo, hi = line[:, :128], line[:, 128:]
    heads_ref[...] = jnp.concatenate([mix(fi, lo, hi), mix(fi, hi, lo)], axis=1)
    x = x_ref[...].astype(F32)
    x_factor = lax.rsqrt(jnp.mean(x * x, -1, keepdims=True) + EPS)
    xin = (x * x_factor * gains_ref[0:1, :]).astype(BF)
    xin_ref[...] = xin
    prod = [mm_split(xin, pair) for pair in split_w(w_refs, w_refs[6].shape[0])]
    cos, sin = cos_ref[...], sin_ref[...]
    rows = x.shape[0]
    lane = lax.broadcasted_iota(jnp.int32, (rows, 128), 1)
    factors = jnp.zeros((rows, 128), F32)

    def normed(own, oth, row):
        total = jnp.sum(own * own + oth * oth, -1, keepdims=True)
        factor = lax.rsqrt(total * (1.0 / HD) + EPS)
        own, oth = own * factor, oth * factor
        g_own = own * heads_ref[row : row + 1, :128]
        g_oth = oth * heads_ref[row : row + 1, 128:]
        rot = jnp.concatenate([g_own * cos - g_oth * sin, g_oth * cos + g_own * sin], axis=1)
        return jnp.concatenate([own, oth], axis=1), rot, factor

    for r in range(4):
        norm, rot, factor = normed(prod[r][:, :128], prod[4 + r][:, :128], 4)
        qn_ref[r] = norm.astype(BF)
        qrot_ref[r] = rot.astype(BF)
        factors = jnp.where(lane == r, factor, factors)
    keys, vals = [], []
    for dx in range(2):
        sides = []
        for dy in range(2):
            zero = prod[dx * 4 + dy * 2][:, 128:192]
            one = prod[dx * 4 + dy * 2 + 1][:, 128:192]
            sides.append(jnp.concatenate([mix(tc, zero, one), mix(tc, one, zero)], axis=1))
        keys.append(mix(ty, sides[0], sides[1]))
        vals.append(mix(ty, sides[1], sides[0]))
    norm, rot, factor = normed(keys[0], keys[1], 5)
    kn_ref[...] = norm.astype(BF)
    fac_ref[...] = jnp.where(lane == 4, factor, factors)
    kv_ref[...] = jnp.concatenate([rot, vals[0], vals[1]], axis=1).astype(BF)


def split_w(refs, cut):
    pairs = [(ref[:cut, :], ref[cut:, :]) for ref in refs[:6]]
    return pairs + [(refs[6][...], refs[7][...]), (refs[8][...], refs[9][...])]


def head_w(pairs, r):
    return tuple(jnp.concatenate([pairs[r][n], pairs[4 + r][n]], axis=1) for n in (0, 1))


def mm_split(left, pair):
    cut = pair[0].shape[0]
    return mm(left[:, :cut], pair[0]) + mm(left[:, cut:], pair[1])


def mm_nt_split(left, pair):
    return jnp.concatenate([mm_nt(left, pair[0]), mm_nt(left, pair[1])], axis=1)


def kv_block(refs, kb):
    start = (kb % 2) * 256
    return refs[kb // 2][start : start + 256, :]


def attn_kernel(need, q_ref, k2_ref, kp_ref, ko_ref, bias_ref, o_ref, linv_ref, acc_ref, l_ref):
    i = pl.program_id(0)
    acc_ref[...] = jnp.zeros_like(acc_ref)
    l_ref[...] = jnp.zeros_like(l_ref)
    tile = q_ref.shape[1]
    for kb in range(6):

        @pl.when(need[i * 6 + kb] > 0)
        def _(kb=kb):
            kv = kv_block((k2_ref, kp_ref, ko_ref), kb)
            q = q_ref[...].reshape(4 * tile, HD)
            s = mm_nt(q, kv[:, :HD]).reshape(4, tile, 256) * HD ** (-0.5)
            p = jnp.exp(s + bias_ref[:, kb * 256 : (kb + 1) * 256][None])
            p = p.reshape(4 * tile, 256)
            l_ref[...] += p[:, :128] + p[:, 128:]
            acc_ref[...] += mm(p.astype(BF), kv[:, HD:])

    linv = 1.0 / jnp.sum(l_ref[...], -1, keepdims=True)
    linv_ref[...] = jnp.broadcast_to(linv, (4 * tile, 128)).reshape(4, tile, 128)
    o_ref[...] = (acc_ref[...] * linv).astype(BF).reshape(4, tile, HD)


def out_kernel(o_ref, x_ref, gains_ref, *refs):
    w_refs, (part_ref, hid_ref, ffn_ref) = refs[:10], refs[10:]
    pairs = split_w(w_refs, w_refs[6].shape[0])
    part = jnp.zeros(part_ref.shape, F32)
    for r in range(4):
        part += mm_nt_split(o_ref[r], head_w(pairs, r))
    part_ref[...] = part
    factor = lax.rsqrt(jnp.mean(part * part, -1, keepdims=True) + EPS)
    hidden = x_ref[...].astype(F32) + part * factor * gains_ref[1:2, :]
    hid_ref[...] = hidden
    factor = lax.rsqrt(jnp.mean(hidden * hidden, -1, keepdims=True) + EPS)
    ffn_ref[...] = (hidden * factor * gains_ref[2:3, :]).astype(BF)


def gelu_parts(gate, up):
    c0 = math.sqrt(2.0 / math.pi)
    square = gate * gate
    th = jnp.tanh(gate * (c0 + (0.044715 * c0) * square))
    side = 0.5 + 0.5 * th
    gelu = gate * side
    slope = side + gelu * (1.0 - th) * (c0 + (3.0 * 0.044715 * c0) * square)
    return gelu * up, slope * up, gelu


def ffn_layout(refs, layout):
    at, groups = 0, []
    for block, spans in enumerate(layout):
        row = 0
        for start, count in spans:
            groups.append((block, at, pl.ds(row, count), pl.ds(start, count), refs[at]))
            row += count
            at += 1
    return groups


def ffn_kernel(*refs, layout, base, hpad):
    n_x, blocks = sum(len(spans) for spans in layout), len(layout)
    x_refs, w_ref = refs[:n_x], refs[n_x]
    outs, scr = refs[-(13 + n_x) : -9], refs[-9:]
    all_refs, part_refs = outs[:4], outs[4:]
    xs, act_s, slope_s, gelu_s, part_s, x_sem, out_sem, part_sem, _ = scr
    rows = xs.shape[1]
    stage = (xs, act_s, slope_s, gelu_s)
    loads = [[] for _ in range(blocks)]
    for block, at, row, span, ref in ffn_layout(x_refs, layout):
        copy = pltpu.make_async_copy(ref.at[span, :], xs.at[block, row, :], x_sem.at[at])
        copy.start()
        loads[block].append(copy)

    def stack(block, n):
        dst = all_refs[n].at[pl.ds((base + block) * rows, rows), :]
        return pltpu.make_async_copy(stage[n].at[block], dst, out_sem.at[block, n])

    def part_copies(block):
        groups = [group for group in ffn_layout(part_refs, layout) if group[0] == block]
        return [
            pltpu.make_async_copy(part_s.at[block, row, :], ref, part_sem.at[at])
            for _, at, row, _, ref in groups
        ]

    def one_block(i, carry):
        per_block(i, blocks, lambda block: [copy.wait() for copy in loads[block]])
        stack(i, 0).start()
        x = xs[i]
        for c in range(0, hpad, 256):
            wide = min(256, hpad - c)
            gate = mm(x, w_ref[:, c : c + wide])
            up = mm(x, w_ref[:, hpad + c : hpad + c + wide])
            act, slope, gelu = gelu_parts(gate, up)
            act_s[i, :, c : c + wide] = act.astype(BF)
            slope_s[i, :, c : c + wide] = slope.astype(BF)
            gelu_s[i, :, c : c + wide] = gelu.astype(BF)
        for n in (1, 2, 3):
            stack(i, n).start()
        part_s[i] = mm_nt(act_s[i], w_ref[:, 2 * hpad :]).astype(BF)
        per_block(i, blocks, lambda block: [copy.start() for copy in part_copies(block)])
        return carry

    lax.fori_loop(0, blocks, one_block, 0)
    for block in range(blocks):
        for n in range(4):
            stack(block, n).wait()
        for copy in part_copies(block):
            copy.wait()


def per_block(i, blocks, act):
    for block in range(blocks):

        @pl.when(i == block)
        def _(block=block):
            act(block)


def ffn_back_kernel(*refs, layout, base, hpad):
    n_x, blocks = sum(len(spans) for spans in layout), len(layout)
    x_refs, w_ref, saved_refs = refs[:n_x], refs[n_x], refs[n_x + 1 : n_x + 3]
    outs, scr = refs[-(11 + n_x) : -9], refs[-9:]
    all_refs, part_refs = outs[:2], outs[2:]
    xs, dgu_s, slope_s, gelu_s, part_s, x_sem, out_sem, part_sem, saved_sem = scr
    rows = xs.shape[1]
    stage = (xs, dgu_s)
    loads = [[] for _ in range(blocks)]

    def saved(block, n):
        src = saved_refs[n].at[pl.ds((base + block) * rows, rows), :]
        dst = (slope_s, gelu_s)[n].at[block]
        copy = pltpu.make_async_copy(src, dst, saved_sem.at[block, n])
        copy.start()
        loads[block].append(copy)

    for block, at, row, span, ref in ffn_layout(x_refs, layout):
        copy = pltpu.make_async_copy(ref.at[span, :], xs.at[block, row, :], x_sem.at[at])
        copy.start()
        loads[block].append(copy)

    for block in range(blocks):
        saved(block, 0)
        saved(block, 1)

    def stack(block, n):
        dst = all_refs[n].at[pl.ds((base + block) * rows, rows), :]
        return pltpu.make_async_copy(stage[n].at[block], dst, out_sem.at[block, n])

    def part_copies(block):
        groups = [group for group in ffn_layout(part_refs, layout) if group[0] == block]
        return [
            pltpu.make_async_copy(part_s.at[block, row, :], ref, part_sem.at[at])
            for _, at, row, _, ref in groups
        ]

    def one_block(i, carry):
        per_block(i, blocks, lambda block: [copy.wait() for copy in loads[block]])
        stack(i, 0).start()
        dout = xs[i]
        for c in range(0, hpad, 256):
            wide = min(256, hpad - c)
            d_act = mm(dout, w_ref[:, 2 * hpad + c : 2 * hpad + c + wide])
            slope = slope_s[i, :, c : c + wide].astype(F32)
            gelu = gelu_s[i, :, c : c + wide].astype(F32)
            dgu_s[i, :, c : c + wide] = (d_act * slope).astype(BF)
            dgu_s[i, :, hpad + c : hpad + c + wide] = (d_act * gelu).astype(BF)
        stack(i, 1).start()
        part_s[i] = mm_nt(dgu_s[i], w_ref[:, : 2 * hpad]).astype(BF)
        per_block(i, blocks, lambda block: [copy.start() for copy in part_copies(block)])
        return carry

    lax.fori_loop(0, blocks, one_block, 0)
    for block in range(blocks):
        for n in range(2):
            stack(block, n).wait()
        for copy in part_copies(block):
            copy.wait()


def hold_kernel(src_ref, dst_ref, sem):
    copy = pltpu.make_async_copy(src_ref, dst_ref, sem.at[0])
    copy.start()
    copy.wait()


def hold(value):
    return pl.pallas_call(
        hold_kernel,
        out_shape=pltpu.VMEM(value.shape, value.dtype),
        in_specs=[pl.BlockSpec(memory_space=pltpu.HBM)],
        out_specs=pl.BlockSpec(memory_space=pltpu.VMEM),
        scratch_shapes=[pltpu.SemaphoreType.DMA((1,))],
        compiler_params=pltpu.CompilerParams(vmem_limit_bytes=16 << 20),
        cost_estimate=price(3, 1000000),
    )(in_hbm(value))


def in_hbm(value):
    return pltpu.with_memory_space_constraint(value, pltpu.HBM)


def ffn_call(kernel, blocks, base, saved, w_ffn, bufs):
    pieces = [value for block in blocks for value, _, _ in block]
    layout = tuple(tuple((start, count) for _, start, count in block) for block in blocks)
    n, back = len(blocks), bool(saved)
    width, hpad = w_ffn.shape[0], w_ffn.shape[1] // 3
    rows = sum(count for _, count in layout[0])
    widths = [width, 2 * hpad] if back else [width, hpad, hpad, hpad]
    ins = [in_hbm(v) for v in pieces] + [w_ffn] + [in_hbm(v) for v in saved]
    aliases = {}
    if bufs is not None:
        aliases = {len(ins) + k: k for k in range(len(widths))}
        ins = ins + [in_hbm(v) for v in bufs]
    hbm = pl.BlockSpec(memory_space=pltpu.HBM)
    in_specs = [hbm] * len(ins)
    in_specs[len(pieces)] = pl.BlockSpec(memory_space=pltpu.VMEM)
    counts = [count for spans in layout for _, count in spans]
    shapes = [((8 * rows, w), BF) for w in widths] + [((count, width), BF) for count in counts]
    mid = [2 * hpad, hpad, hpad] if back else [hpad, hpad, hpad]
    scratch = [pltpu.VMEM((n, rows, w), BF) for w in [width] + mid + [width]]
    scratch += [
        pltpu.SemaphoreType.DMA((len(pieces),)),
        pltpu.SemaphoreType.DMA((n, 4)),
        pltpu.SemaphoreType.DMA((len(pieces),)),
        pltpu.SemaphoreType.DMA((n, 2)),
    ]
    outs = pl.pallas_call(
        partial(kernel, layout=layout, base=base, hpad=hpad),
        out_shape=[pltpu.HBM(shape, dtype) for shape, dtype in shapes],
        in_specs=in_specs,
        out_specs=[hbm] * len(shapes),
        scratch_shapes=scratch,
        input_output_aliases=aliases,
        compiler_params=pltpu.CompilerParams(vmem_limit_bytes=28 << 20),
        cost_estimate=price(6 * n, 1000000 * n),
    )(*ins)
    grouped, at = [], len(widths)
    for spans in layout:
        grouped.append(tuple(outs[at : at + len(spans)]))
        at += len(spans)
    return outs[: len(widths)], grouped


def ffn_mid_kernel(*refs):
    hid_ref, cot_ref, gains_ref, out_ref, dout_ref, gain_ref = refs[6:]
    part = piece_sum(refs[:6])
    gain = gains_ref[3:4, :]
    factor = lax.rsqrt(jnp.mean(part * part, -1, keepdims=True) + EPS)
    out_ref[...] = (hid_ref[...] + part * factor * gain).astype(BF)
    back, gain_grad = norm_back_tile(part, gain, cot_ref[...].astype(F32))
    dout_ref[...] = back.astype(BF)
    gain_ref[0:1, :] = gain_grad


def norm_back_tile(raw, gain, upstream):
    factor = lax.rsqrt(jnp.mean(raw * raw, -1, keepdims=True) + EPS)
    normed = raw * factor
    gain_grad = jnp.sum(upstream * normed, axis=0, keepdims=True)
    scaled = upstream * gain
    back = factor * (scaled - normed * jnp.mean(scaled * normed, -1, keepdims=True))
    return back, gain_grad


def mid_kernel(*refs):
    hid_ref, part_ref, cot_ref, gains_ref = refs[6:10]
    w_refs, (dhid_ref, dpart_ref, dhead_ref, gain_ref) = refs[10:20], refs[20:]
    din = piece_sum(refs[:6])
    extra, gain_ffn = norm_back_tile(hid_ref[...], gains_ref[2:3, :], din)
    dhid = cot_ref[...].astype(F32) + extra
    dhid_ref[...] = dhid
    dpart, gain_post = norm_back_tile(part_ref[...], gains_ref[1:2, :], dhid)
    dpart = dpart.astype(BF)
    dpart_ref[...] = dpart
    gain_ref[0:1, :] = gain_ffn
    gain_ref[1:2, :] = gain_post
    pairs = split_w(w_refs, w_refs[6].shape[0])
    for r in range(4):
        dhead_ref[r] = mm_split(dpart, head_w(pairs, r)).astype(BF)


def attn_back_kernel(
    need,
    q_ref,
    k2_ref,
    kp_ref,
    ko_ref,
    bias_ref,
    o_ref,
    do_ref,
    linv_ref,
    qn_ref,
    fac_ref,
    cos_ref,
    sin_ref,
    gq_ref,
    dq_ref,
    d2_ref,
    dp_ref,
    down_ref,
    gain_ref,
    acc_ref,
    dkv_ref,
):
    i = pl.program_id(0)
    tile = q_ref.shape[1]

    @pl.when(i == 0)
    def _():
        dkv_ref[...] = jnp.zeros_like(dkv_ref)
        gain_ref[...] = jnp.zeros_like(gain_ref)

    acc_ref[...] = jnp.zeros_like(acc_ref)
    q = q_ref[...].reshape(4 * tile, HD)
    do = do_ref[...].reshape(4 * tile, HD)
    linv = linv_ref[...].reshape(4 * tile, 128)[:, 0:1]
    inner = jnp.sum(do.astype(F32) * o_ref[...].reshape(4 * tile, HD).astype(F32), -1, keepdims=True)
    for kb in range(6):

        @pl.when(need[i * 6 + kb] > 0)
        def _(kb=kb):
            kv = kv_block((k2_ref, kp_ref, ko_ref), kb)
            keys, vals = kv[:, :HD], kv[:, HD:]
            s = mm_nt(q, keys).reshape(4, tile, 256) * HD ** (-0.5)
            p = jnp.exp(s + bias_ref[:, kb * 256 : (kb + 1) * 256][None])
            p = p.reshape(4 * tile, 256) * linv
            dp = mm_nt(do, vals)
            ds = (p * (dp - inner)).astype(BF)
            acc_ref[...] += mm(ds, keys)
            span = slice(kb * 256, (kb + 1) * 256)
            dkv_ref[span, :HD] += mm_tn(ds, q)
            dkv_ref[span, HD:] += mm_tn(p.astype(BF), do)

    cos, sin = cos_ref[...], sin_ref[...]
    gain = jnp.zeros((1, HD), F32)
    for r in range(4):
        dq = acc_ref[r * tile : (r + 1) * tile, :] * HD ** (-0.5)
        own, oth = dq[:, :128], dq[:, 128:]
        back = jnp.concatenate([own * cos + oth * sin, oth * cos - own * sin], axis=1)
        norm = qn_ref[r].astype(F32)
        gain += jnp.sum(back * norm, axis=0, keepdims=True)
        scaled = back * gq_ref[4:5, :]
        mean = jnp.mean(scaled * norm, -1, keepdims=True)
        dq_ref[r] = (fac_ref[:, r : r + 1] * (scaled - norm * mean)).astype(BF)
    gain_ref[0:1, :] += gain

    @pl.when(i == pl.num_programs(0) - 1)
    def _():
        rows = d2_ref.shape[0]
        scale = HD ** (-0.5)
        for n, ref in enumerate((d2_ref, dp_ref, down_ref)):
            block = dkv_ref[n * rows : (n + 1) * rows, :]
            ref[:, :HD] = (block[:, :HD] * scale).astype(ref.dtype)
            ref[:, HD:] = block[:, HD:].astype(ref.dtype)


def post_kernel(
    flags,
    dq_ref,
    dkv_ref,
    dp_ref,
    kn_ref,
    fac_ref,
    cos_ref,
    sin_ref,
    gk_ref,
    x_ref,
    gains_ref,
    dhid_ref,
    gq_grad,
    mid_grad,
    post_grad,
    place_ref,
    *refs,
):
    w_refs, din_ref, kvraw_ref, gain_ref = refs[:10], *refs[10:]
    fi, ty, tc = (flags[n].astype(F32) for n in range(3))
    dkv = dkv_ref[...] + dp_ref[...].astype(F32)
    cos, sin = cos_ref[...], sin_ref[...]
    own, oth = dkv[:, :128], dkv[:, 128:256]
    back = jnp.concatenate([own * cos + oth * sin, oth * cos - own * sin], axis=1)
    norm = kn_ref[...].astype(F32)
    gk_grad = jnp.sum(back * norm, axis=0, keepdims=True)
    scaled = back * gk_ref[5:6, :]
    mean = jnp.mean(scaled * norm, -1, keepdims=True)
    dkey = fac_ref[:, 4:5] * (scaled - norm * mean)
    dval = dkv[:, 256:]
    kvraw_ref[...] = jnp.concatenate([dkey, dval], axis=1).astype(BF)
    din = jnp.zeros(din_ref.shape, F32)
    zeros = jnp.zeros((dkv.shape[0], 64), F32)
    pairs = split_w(w_refs, w_refs[6].shape[0])
    rel = 0
    for dx in range(2):
        kh = dkey[:, dx * 128 : (dx + 1) * 128]
        vh = dval[:, dx * 128 : (dx + 1) * 128]
        for dy in range(2):
            half = mix(ty, kh, vh) if dy == 0 else mix(ty, vh, kh)
            for dc in range(2):
                lo, hi = half[:, :64], half[:, 64:]
                part = mix(tc, lo, hi) if dc == 0 else mix(tc, hi, lo)
                side = jnp.concatenate([part, zeros], axis=1).astype(BF)
                dprod = jnp.concatenate(
                    [dq_ref[dy * 2 + dc][:, dx * 128 : (dx + 1) * 128], side], axis=1
                )
                din += mm_nt_split(dprod, pairs[rel])
                rel += 1
    x = x_ref[...].astype(F32)
    extra, gain_pre = norm_back_tile(x, gains_ref[0:1, :], din)
    din_ref[...] = dhid_ref[...] + extra

    def spread(grad):
        own, oth = grad[:, :128], grad[:, 128:]
        whole_row = jnp.concatenate([mix(fi, own, oth), mix(fi, oth, own)], axis=1)
        return mm(jnp.broadcast_to(whole_row.astype(BF), (8, HD)), place_ref[...])[0:1, :]

    gain_ref[...] = jnp.zeros_like(gain_ref)
    gain_ref[0:1, :] = gain_pre
    gain_ref[1:2, :] = mid_grad[1:2, :]
    gain_ref[2:3, :] = mid_grad[0:1, :]
    gain_ref[3:4, :] = post_grad[0:1, :]
    gain_ref[4:5, :] = spread(gq_grad[0:1, :])
    gain_ref[5:6, :] = spread(gk_grad)


def store_rows(refs, value):
    cut = refs[0].shape[0]
    refs[0][...] = value[:cut, :]
    refs[1][...] = value[cut:, :]


def qo_grad_kernel(xin, xin_c, dq, dq_c, dpart, dpart_c, head, head_c, *outs):
    xt, xt_c, dt, dt_c = (ref[...].T for ref in (xin, xin_c, dpart, dpart_c))
    for dy in range(2):
        gq = (mm(xt, dq[2 * dy]) + mm(xt_c, dq_c[dy])).astype(BF)
        go = (mm(dt, head[2 * dy]) + mm(dt_c, head_c[dy])).astype(BF)
        for dx in range(2):
            half = slice(dx * 128, (dx + 1) * 128)
            at = 4 * dx + 2 * dy
            store_rows(outs[at : at + 2], jnp.concatenate([gq[:, half], go[:, half]], axis=1))


def kv_grad_kernel(flags, xin, xin_c, kv, kv_c, gain, gain_c, *refs):
    outs, rows_ref = refs[:8], refs[8]
    ty, tc = flags[1].astype(F32), flags[2].astype(F32)
    rows_ref[...] = jnp.zeros_like(rows_ref)
    rows_ref[64:72, :] = gain[...] + gain_c[...]
    gain_cols = rows_ref[...].T
    xt, xt_c = xin[...].T, xin_c[...].T

    def sides(ref):
        block = ref[...].astype(F32)
        picked = []
        for dy in range(2):
            for dx in range(2):
                kh = block[:, dx * 128 : (dx + 1) * 128]
                vh = block[:, 256 + dx * 128 : 256 + (dx + 1) * 128]
                half = mix(ty, kh, vh) if dy == 0 else mix(ty, vh, kh)
                picked.append(mix(tc, half[:, :64], half[:, 64:]))
        return jnp.concatenate(picked, axis=1).astype(BF)

    grad = mm(xt, sides(kv)) + mm(xt_c, sides(kv_c))
    zeros = jnp.zeros((grad.shape[0], 64), F32)
    for dy in range(2):
        for dx in range(2):
            at = 4 * dx + 2 * dy
            col = (2 * dy + dx) * 64
            part = jnp.concatenate([grad[:, col : col + 64], zeros], axis=1) + gain_cols
            store_rows(outs[at : at + 2], part.astype(BF))


def chip_reduce(parts):
    own, near_y, near_x, far = (parts[n : n + 2] for n in (0, 2, 4, 6))
    from_x, from_y = swap(far[0], "fi"), swap(far[1], "ty")
    got_x_top, got_y_bot = swap(near_x[0], "fi"), swap(near_y[1], "ty")
    x_bot = (near_x[1].astype(F32) + from_y.astype(F32)).astype(BF)
    y_top = (near_y[0].astype(F32) + from_x.astype(F32)).astype(BF)
    return (*own, got_x_top, swap(x_bot, "fi"), swap(y_top, "ty"), got_y_bot)


def gather_sum_kernel(*refs):
    out_ref = refs[12]
    for n, cols in ((0, slice(0, 256)), (6, slice(256, 384))):
        own_top, own_bot, x_top, x_bot, y_top, y_bot = (ref[...].astype(F32) for ref in refs[n : n + 6])
        cut = own_top.shape[0]
        out_ref[:cut, cols] = (own_top + x_top + y_top).astype(BF)
        out_ref[cut:, cols] = (own_bot + x_bot + y_bot).astype(BF)


def pad_cols(value, width):
    return jnp.pad(value, ((0, 0), (0, width - value.shape[1])))


def body(
    tokens,
    positions,
    segments,
    w_query,
    w_key,
    w_value,
    w_out,
    w_gate,
    w_up,
    w_down,
    gain_attn_pre,
    gain_query,
    gain_key,
    gain_attn_post,
    gain_ffn_pre,
    gain_ffn_post,
    cotangent,
):
    fi = lax.axis_index("fi")
    ty = lax.axis_index("ty")
    tc = lax.axis_index("tc")
    t_idx = ty * 2 + tc
    me = fi * 4 + t_idx
    first = fi == 0
    rows = tokens.shape[0]
    width = tokens.shape[1]
    shard = w_query.shape[0]
    nf = width // shard
    hid = w_gate.shape[1] // 2
    hpad = -(-hid // 128) * 128
    gshard = gain_query.shape[0]

    def pair_rows(keep, recv):
        return jnp.where(
            first,
            jnp.concatenate([keep, recv], axis=0),
            jnp.concatenate([recv, keep], axis=0),
        )

    kv_mine = jnp.where(ty == 0, w_key, w_value)
    out_t = w_out.T
    gains = pad_cols(
        jnp.stack(
            [
                gain_attn_pre,
                gain_attn_post,
                gain_ffn_pre,
                gain_ffn_post,
                jnp.pad(gain_query, (0, shard - gshard)),
                jnp.pad(gain_key, (0, shard - gshard)),
            ],
            axis=1,
        ),
        64,
    )

    def piece(h):
        kv_half = kv_mine[:, h * 128 : (h + 1) * 128]
        kv_part = jnp.where(tc == 0, kv_half[:, :64], kv_half[:, 64:])
        return jnp.concatenate(
            [
                w_query[:, h * 128 : (h + 1) * 128],
                kv_part,
                gains,
                out_t[:, h * 128 : (h + 1) * 128],
            ],
            axis=1,
        )

    piece0, piece1 = piece(0), piece(1)
    keep = jnp.where(first, piece0, piece1)
    recv = swap(jnp.where(first, piece1, piece0), "fi")

    down_t = w_down.T

    def halves(weight):
        lo, hi = pad_cols(weight[:, :hid], hpad), pad_cols(weight[:, hid:], hpad)
        return jnp.where(first, lo, hi), jnp.where(first, hi, lo)

    gate_keep, gate_send = halves(w_gate)
    up_keep, up_send = halves(w_up)
    down_keep, down_send = halves(down_t)
    ffn_keep = jnp.concatenate([gate_keep, up_keep, down_keep], axis=1)
    ffn_send = jnp.concatenate([gate_send, up_send, down_send], axis=1)
    ffn_send, ffn_keep, recv = lax.optimization_barrier((ffn_send, ffn_keep, recv))
    ffn_recv = swap(ffn_send, "fi")
    attn_col = lax.all_gather(pair_rows(keep, recv), "fo", axis=0, tiled=True)
    attn_col, ffn_pair = lax.optimization_barrier((attn_col, pair_rows(ffn_keep, ffn_recv)))
    w_ffn = lax.all_gather(ffn_pair, "fo", axis=0, tiled=True)

    elem = lax.broadcasted_iota(jnp.int32, (HD, width), 0)
    spot = lax.broadcasted_iota(jnp.int32, (HD, width), 1)
    place = (spot == (elem // gshard) * shard + elem % gshard).astype(BF)
    cut = width // 256 * 128
    row_start = t_idx * rows
    pos_local = lax.dynamic_slice_in_dim(positions, row_start, rows)
    seg_local = lax.dynamic_slice_in_dim(segments, row_start, rows)

    def block_of(meta, back):
        return lax.dynamic_slice_in_dim(meta, ((t_idx - back) % 4) * rows, rows)

    k_pos = jnp.concatenate([block_of(positions, 2), block_of(positions, 1), pos_local])
    k_seg = jnp.concatenate(
        [
            jnp.where(t_idx == 3, block_of(segments, 2), -1),
            jnp.where(t_idx >= 1, block_of(segments, 1), -1),
            seg_local,
        ]
    )
    allowed = (
        ((k_seg[None, :] == 0) | (k_seg[None, :] == seg_local[:, None]))
        & (k_pos[None, :] <= pos_local[:, None])
        & (pos_local[:, None] - k_pos[None, :] < WINDOW)
    )
    bias = jnp.where(allowed, 0.0, NEG).astype(F32)
    need = jnp.any(allowed.reshape(4, rows // 4, 6, rows // 2), axis=(1, 3))
    need = need.astype(jnp.int32).reshape(24)
    frequency = jnp.exp(-math.log(BASE) * jnp.arange(HALF).astype(F32) / HALF)
    angles = pos_local.astype(F32)[:, None] * frequency
    cosine = jnp.cos(angles)
    sine = jnp.sin(angles) * jnp.where(first, 1.0, -1.0)

    w_parts, (bias, need, cosine, sine, place) = plane_gather(
        attn_col, cut, (bias, need, cosine, sine, place)
    )
    w_parts = [in_hbm(piece) for pieces in w_parts for piece in pieces]
    flags = jnp.stack([fi, ty, tc]).astype(jnp.int32)
    qkv_spec = [pl.BlockSpec((part.shape[0], 256), lambda *_: (0, 0)) for part in w_parts]
    wo_spec = [pl.BlockSpec((part.shape[0], 128), lambda *_: (0, 2)) for part in w_parts]
    full, gains8 = whole((rows, width)), whole((8, width))
    heads = whole((4, rows, HD))
    lanes = whole((rows, 128))
    kv_full = whole((rows, 2 * HD))
    attn_in, q_rot, q_norm, kv_own, k_norm, factors, gain_rows, head_gains = run(
        qkv_kernel,
        [
            ((rows, width), BF),
            ((4, rows, HD), BF),
            ((4, rows, HD), BF),
            ((rows, 2 * HD), BF),
            ((rows, HD), BF),
            ((rows, 128), F32),
            ((8, width), F32),
            ((8, HD), F32),
        ],
        (flags, tokens, place, cosine, sine, *w_parts),
        9,
        grid=(1,),
        in_specs=[full, whole((HD, width)), lanes, lanes] + qkv_spec,
        out_specs=[full, heads, heads, kv_full, whole((rows, HD)), lanes, gains8, whole((8, HD))],
        prefetch=1,
    )
    kv_prev = lax.ppermute(kv_own, ("ty", "tc"), [(i, (i + 1) % 4) for i in range(4)])
    kv_two = swap(kv_prev, "tc")
    tile = rows // 4
    q_tile = pl.BlockSpec((4, tile, HD), lambda i, *_: (0, i, 0))
    l_tile = pl.BlockSpec((4, tile, 128), lambda i, *_: (0, i, 0))
    bias_tile = pl.BlockSpec((tile, 3 * rows), lambda i, *_: (i, 0))
    head_out, linv = run(
        attn_kernel,
        [((4, rows, HD), BF), ((4, rows, 128), F32)],
        (need, q_rot, kv_two, kv_prev, kv_own, bias),
        8,
        grid=(4,),
        in_specs=[q_tile, kv_full, kv_full, kv_full, bias_tile],
        out_specs=[q_tile, l_tile],
        scratch=[pltpu.VMEM((4 * tile, HD), F32), pltpu.VMEM((4 * tile, 128), F32)],
        prefetch=1,
    )
    attn_part, hidden, ffn_local = run(
        out_kernel,
        [((rows, width), F32), ((rows, width), F32), ((rows, width), BF)],
        (head_out, tokens, gain_rows, *w_parts),
        6,
        grid=(1,),
        in_specs=[heads, full, gains8] + wo_spec,
        out_specs=[full, full, full],
    )

    half = rows // 2
    def far_pieces(top, bot, after):
        top, bot, after = lax.optimization_barrier((top, bot, after))
        return (top, bot), (swap(top, "tc"), swap(bot, "tc")), after

    by_x, by_y, by_c = swap(ffn_local, "fi"), swap(ffn_local, "ty"), swap(ffn_local, "tc")
    top, bot = swap(by_y[:half], "fi"), swap(by_x[half:], "ty")
    by_xc, by_yc = swap(by_x, "tc"), swap(by_y, "tc")
    w_ffn = hold(w_ffn)
    top, bot, w_ffn = lax.optimization_barrier((top, bot, w_ffn))
    top_c, bot_c = swap(top, "tc"), swap(bot, "tc")
    whole_of = lambda value: [(value, 0, rows)]
    halves_of = lambda low, high: [(low, 0, half), (high, half, half)]
    both_of = lambda top, bot: [(top, 0, half), (bot, 0, half)]
    far = [both_of(top, bot), both_of(top_c, bot_c)]
    bufs, parts_f = ffn_call(ffn_kernel, far, 6, [], w_ffn, None)
    sent = far_sum(*parts_f, half)
    by_x, by_y, by_xc, by_yc, sent = lax.optimization_barrier((by_x, by_y, by_xc, by_yc, sent))
    got = far_swap(sent)
    first_rows = [halves_of(by_x, by_y), halves_of(by_xc, by_yc)]
    bufs, parts_1 = ffn_call(ffn_kernel, first_rows, 2, [], w_ffn, bufs)
    by_x, by_y, by_xc, by_yc, got = lax.optimization_barrier((by_x, by_y, by_xc, by_yc, got))
    second_rows = [
        [(by_x, half, half), (by_y, 0, half)],
        [(by_xc, half, half), (by_yc, 0, half)],
    ]
    bufs, parts_2 = ffn_call(ffn_kernel, second_rows, 4, [], w_ffn, bufs)
    first_in = near_swap(near_first(parts_1))
    second_out = near_second(parts_2, got)
    first_in, second_out = lax.optimization_barrier((first_in, second_out))
    second_in = near_swap(second_out)
    (x_all, act_all, slope_all, gelu_all), parts_o = ffn_call(
        ffn_kernel, [whole_of(ffn_local), whole_of(by_c)], 0, [], w_ffn, bufs
    )
    pieces = plane_pieces(parts_o, first_in, second_in)
    quarter = whole((half, width))
    piece_spec = [full, full] + [quarter] * 4

    other = swap(jnp.stack([head_out[1], head_out[3]]), "tc"), swap(attn_in, "tc")
    pieces, (head_out_c, attn_in_c) = lax.optimization_barrier((pieces, other))
    output, d_local, ffn_post_grad = run(
        ffn_mid_kernel,
        [((rows, width), BF), ((rows, width), BF), ((8, width), F32)],
        (*pieces, hidden, cotangent, gain_rows),
        6,
        grid=(1,),
        in_specs=piece_spec + [full, full, gains8],
        out_specs=[full, full, gains8],
    )
    by_x, by_y, by_c = swap(d_local, "fi"), swap(d_local, "ty"), swap(d_local, "tc")
    saved = [slope_all, gelu_all]
    own_rows = [whole_of(d_local), whole_of(by_c)]
    bufs, parts_o = ffn_call(ffn_back_kernel, own_rows, 0, saved, w_ffn, None)
    by_x, by_y, parts_o = lax.optimization_barrier((by_x, by_y, parts_o))
    top, bot = swap(by_y[:half], "fi"), swap(by_x[half:], "ty")
    by_xc, by_yc = swap(by_x, "tc"), swap(by_y, "tc")
    first_rows = [halves_of(by_x, by_y), halves_of(by_xc, by_yc)]
    bufs, parts_1 = ffn_call(ffn_back_kernel, first_rows, 2, saved, w_ffn, bufs)
    (top, bot), (top_c, bot_c), parts_1 = far_pieces(top, bot, parts_1)
    first_in = near_swap(near_first(parts_1))
    far = [both_of(top, bot), both_of(top_c, bot_c)]
    bufs, parts_f = ffn_call(ffn_back_kernel, far, 6, saved, w_ffn, bufs)
    second_rows = [
        [(by_x, half, half), (by_y, 0, half)],
        [(by_xc, half, half), (by_yc, 0, half)],
    ]
    (d_all, dgu_all), parts_2 = ffn_call(
        ffn_back_kernel, second_rows, 4, saved, w_ffn, bufs
    )
    sent = far_sum(*parts_f, half)
    d_all, sent, first_in = lax.optimization_barrier((d_all, sent, first_in))
    got = far_swap(sent)
    grad_dt = dot_left_t(d_all, act_all).astype(BF)
    dgu_all, grad_dt, got = lax.optimization_barrier((dgu_all, grad_dt, got))
    second_in = near_swap(near_second(parts_2, got))
    grad_gu = dot_left_t(x_all, dgu_all).astype(BF)
    pieces = plane_pieces(parts_o, first_in, second_in)
    pieces, grad_gu = lax.optimization_barrier((pieces, grad_gu))
    sum_dt = lax.psum_scatter(grad_dt, "fo", scatter_dimension=0, tiled=True)
    sum_gu = lax.psum_scatter(grad_gu, "fo", scatter_dimension=0, tiled=True)

    def unpair(summed):
        top_rows, bot_rows = summed[:shard], summed[shard:]
        mine = jnp.where(first, top_rows, bot_rows)
        theirs = swap(jnp.where(first, bot_rows, top_rows), "fi")
        return jnp.where(first, mine, theirs), jnp.where(first, theirs, mine)

    def join(lo, hi):
        return jnp.concatenate([lo[:, :hid], hi[:, :hid]], axis=1).astype(F32)

    hidden_grad, attn_part_grad, head_grad, mid_gains = run(
        mid_kernel,
        [((rows, width), F32), ((rows, width), BF), ((4, rows, HD), BF), ((8, width), F32)],
        (
            *map(in_hbm, (*pieces, hidden, attn_part, cotangent)),
            gain_rows,
            *w_parts,
        ),
        10,
        grid=(1,),
        in_specs=piece_spec + [full, full, full, gains8] + wo_spec,
        out_specs=[full, full, heads, whole((8, width))],
    )
    fac_tile = pl.BlockSpec((tile, 128), lambda i, *_: (i, 0))
    line = whole((8, HD))
    q_raw_grad, kv_grad_two, kv_grad_prev, kv_grad_own, gain_q = run(
        attn_back_kernel,
        [
            ((4, rows, HD), BF),
            ((rows, 2 * HD), BF),
            ((rows, 2 * HD), BF),
            ((rows, 2 * HD), F32),
            ((8, HD), F32),
        ],
        (
            need,
            q_rot,
            kv_two,
            kv_prev,
            kv_own,
            bias,
            head_out,
            head_grad,
            linv,
            q_norm,
            factors,
            cosine,
            sine,
            head_gains,
        ),
        12,
        grid=(4,),
        in_specs=[
            q_tile,
            kv_full,
            kv_full,
            kv_full,
            bias_tile,
            q_tile,
            q_tile,
            l_tile,
            q_tile,
            fac_tile,
            fac_tile,
            fac_tile,
            line,
        ],
        out_specs=[q_tile, kv_full, kv_full, kv_full, whole((8, HD))],
        scratch=[pltpu.VMEM((4 * tile, HD), F32), pltpu.VMEM((3 * rows, 2 * HD), F32)],
        prefetch=1,
    )
    back_two = kv_grad_prev.astype(F32) + swap(kv_grad_two, "tc").astype(F32)
    q_raw_grad, back_two = lax.optimization_barrier((q_raw_grad, back_two.astype(BF)))
    back_prev = lax.ppermute(back_two, ("ty", "tc"), [(i, (i + 3) % 4) for i in range(4)])
    def row_pieces(cols):
        return [((n, cols), BF) for n in (cut, width - cut)] * 4

    other_heads = lambda value: swap(jnp.stack([value[1], value[3]]), "tc")
    two_heads = whole((2, rows, HD))
    qo_grads = run(
        qo_grad_kernel,
        row_pieces(256),
        (
            attn_in,
            attn_in_c,
            q_raw_grad,
            other_heads(q_raw_grad),
            attn_part_grad,
            swap(attn_part_grad, "tc"),
            head_out,
            head_out_c,
        ),
        5,
        grid=(1,),
        in_specs=[full, full, heads, two_heads, full, full, heads, two_heads],
        out_specs=[whole(shape) for shape, _ in row_pieces(256)],
    )
    back_prev, sum_dt = lax.optimization_barrier((back_prev, sum_dt))
    qo_pieces = chip_reduce(qo_grads)
    input_grad, kv_raw_grad, gain_grads = run(
        post_kernel,
        [((rows, width), F32), ((rows, 2 * HD), BF), ((8, width), F32)],
        (
            flags,
            q_raw_grad,
            in_hbm(kv_grad_own),
            back_prev,
            k_norm,
            factors,
            cosine,
            sine,
            head_gains,
            in_hbm(tokens),
            gain_rows,
            in_hbm(hidden_grad),
            gain_q,
            mid_gains,
            ffn_post_grad,
            place,
            *w_parts,
        ),
        9,
        grid=(1,),
        in_specs=[heads, kv_full, kv_full, whole((rows, HD)), lanes, lanes, lanes, line]
        + [full, gains8, full, whole((8, HD)), gains8, gains8]
        + [whole((HD, width))]
        + qkv_spec,
        out_specs=[full, kv_full, gains8],
        prefetch=1,
    )
    kv_grads = run(
        kv_grad_kernel,
        row_pieces(128),
        (
            flags,
            attn_in,
            attn_in_c,
            kv_raw_grad,
            swap(kv_raw_grad, "tc"),
            gain_grads,
            swap(gain_grads, "tc"),
        ),
        3,
        grid=(1,),
        in_specs=[full, full, kv_full, kv_full, gains8, gains8],
        out_specs=[whole(shape) for shape, _ in row_pieces(128)],
        scratch=[pltpu.VMEM((128, width), F32)],
        prefetch=1,
    )
    kv_pieces = chip_reduce(kv_grads)
    qo_pieces, kv_pieces, sum_gu = lax.optimization_barrier((qo_pieces, kv_pieces, sum_gu))
    (attn_grads,) = run(
        gather_sum_kernel,
        [((width, 384), BF)],
        (*qo_pieces, *kv_pieces),
        2,
        grid=(1,),
        in_specs=[whole(piece.shape) for piece in (*qo_pieces, *kv_pieces)],
        out_specs=[whole((width, 384))],
    )
    sum_attn = lax.psum_scatter(attn_grads, "fo", scatter_dimension=0, tiled=True)
    dt_lo, dt_hi = unpair(sum_dt)
    gu_lo, gu_hi = unpair(sum_gu)
    grad_gate = join(gu_lo[:, :hpad], gu_hi[:, :hpad])
    grad_up = join(gu_lo[:, hpad:], gu_hi[:, hpad:])
    grad_down = join(dt_lo, dt_hi).T

    a_lo, a_hi = unpair(sum_attn)
    grad_out = jnp.concatenate([a_lo[:, 128:256], a_hi[:, 128:256]], axis=1).astype(F32).T
    grad_query = jnp.concatenate([a_lo[:, :128], a_hi[:, :128]], axis=1).astype(F32)
    kv_part = jnp.concatenate([a_lo[:, 256:320], a_hi[:, 256:320]], axis=1)
    others = [
        lax.ppermute(kv_part, ("ty", "tc"), [(i, i ^ step) for i in range(4)]) for step in (1, 2, 3)
    ]
    row_here = jnp.where(tc == 0, 0, 1)

    def kv_lines(near, far):
        even = jnp.where(row_here == 0, near, far)
        odd = jnp.where(row_here == 0, far, near)
        return jnp.concatenate([even[:, :64], odd[:, :64], even[:, 64:], odd[:, 64:]], axis=1)

    kv_here, kv_far = kv_lines(kv_part, others[0]), kv_lines(others[1], others[2])
    grad_key = jnp.where(ty == 0, kv_here, kv_far).astype(F32)
    grad_value = jnp.where(ty == 0, kv_far, kv_here).astype(F32)
    gain_out = a_lo[:, 320:328].astype(F32).T
    return (
        output.astype(BF),
        input_grad,
        grad_query,
        grad_key,
        grad_value,
        grad_out,
        grad_gate,
        grad_up,
        grad_down,
        gain_out[0],
        gain_out[4, :gshard],
        gain_out[5, :gshard],
        gain_out[1],
        gain_out[2],
        gain_out[3],
    )


def solution(mesh):
    nf, nt = mesh.shape["fsdp"], mesh.shape["tensor"]
    fine = Mesh(mesh.devices.reshape(nf // 2, 2, nt // 2, 2), ("fo", "fi", "ty", "tc"))
    f_axes, t_axes = ("fo", "fi"), ("ty", "tc")
    rows = P(f_axes + t_axes, None)
    col = P(f_axes, t_axes)
    flat = P(f_axes, None)
    out_w = P(t_axes, f_axes)
    vec = P(f_axes)
    in_specs = (rows, vec, vec, col, flat, flat, out_w, col, col, out_w) + (vec,) * 6 + (rows,)
    out_specs = (rows, rows, col, flat, flat, out_w, col, col, out_w) + (vec,) * 6
    return jax.shard_map(body, mesh=fine, in_specs=in_specs, out_specs=out_specs, check_vma=False)
```

```python
import math
from functools import partial

import jax
import jax.numpy as jnp
from jax import lax
from jax.experimental import pallas as pl
from jax.experimental.pallas import tpu as pltpu
from jax.sharding import Mesh, PartitionSpec as P

HD = 256
WINDOW = 512
PROMPT = 1024
CONT = 8
CLEN = 128


EPS = 1e-06
NEG = -1e30
BASE = 10000.0
HALF = HD // 2
BF = jnp.bfloat16
F32 = jnp.float32


def dot_left_t(left_op, right_op):
    return lax.dot_general(
        left_op, right_op, (((0,), (0,)), ((), ())), preferred_element_type=jnp.float32
    )


def swap(value, axis):
    return lax.ppermute(value, axis, [(0, 1), (1, 0)])


RELS = [(dx, dy, dc) for dx in (0, 1) for dy in (0, 1) for dc in (0, 1)]


def plane_gather(own, cut, side):
    by_x = swap(own, "fi")
    by_y = swap(own, "ty")
    by_c = swap(own, "tc")
    by_x, by_y, side = lax.optimization_barrier((by_x, by_y, side))
    diag_top = swap(by_y[:cut], "fi")
    diag_bot = swap(by_x[cut:], "ty")
    by_xc = swap(by_x, "tc")
    by_yc = swap(by_y, "tc")
    return [
        (own,),
        (by_c,),
        (by_y,),
        (by_yc,),
        (by_x,),
        (by_xc,),
        (diag_top, diag_bot),
        (swap(diag_top, "tc"), swap(diag_bot, "tc")),
    ], side


def core_add(mine, other):
    return mine.astype(F32) + swap(other, "tc").astype(F32)


def far_sum(far, far_c, cut):
    if len(far) == 1:
        far, far_c = (far[0][:cut], far[0][cut:]), (far_c[0][:cut], far_c[0][cut:])
    return core_add(far[0], far_c[0]).astype(BF), core_add(far[1], far_c[1]).astype(BF)


def far_swap(sent):
    return swap(sent[0], "fi"), swap(sent[1], "ty")


def near_first(parts):
    (x_top, y_bot), (x_top_c, y_bot_c) = parts
    return core_add(x_top, x_top_c).astype(BF), core_add(y_bot, y_bot_c).astype(BF)


def near_second(parts, got):
    (x_bot, y_top), (x_bot_c, y_top_c) = parts
    x_bot = core_add(x_bot, x_bot_c) + got[1].astype(F32)
    y_top = core_add(y_top, y_top_c) + got[0].astype(F32)
    return x_bot.astype(BF), y_top.astype(BF)


def near_swap(first):
    return swap(first[0], "fi"), swap(first[1], "ty")


def plane_pieces(parts_o, first, second):
    own, own_c = parts_o
    return own[0], swap(own_c[0], "tc"), first[0], second[0], second[1], first[1]


def piece_sum(pieces):
    own, sib, x_top, x_bot, y_top, y_bot = (piece[...].astype(F32) for piece in pieces)
    cross = jnp.concatenate([x_top + y_top, x_bot + y_bot], axis=0)
    return own + sib + cross


def mix(flag, at_zero, at_one):
    return at_zero * (1.0 - flag) + at_one * flag


def nbytes(shapes):
    return sum(math.prod(shape) * jnp.dtype(dtype).itemsize for shape, dtype in shapes)


def price(us, moved):
    return pl.CostEstimate(flops=int(us * 1.0e9), transcendentals=0, bytes_accessed=moved)


def run(kernel, outs, ins, us, *, grid=(), in_specs=None, out_specs=None, scratch=(), prefetch=0):
    return pl.pallas_call(
        kernel,
        out_shape=[jax.ShapeDtypeStruct(shape, dtype) for shape, dtype in outs],
        grid_spec=pltpu.PrefetchScalarGridSpec(
            num_scalar_prefetch=prefetch,
            grid=grid,
            in_specs=in_specs,
            out_specs=out_specs,
            scratch_shapes=list(scratch),
        ),
        compiler_params=pltpu.CompilerParams(
            vmem_limit_bytes=44 << 20, dimension_semantics=("arbitrary",) * len(grid)
        ),
        cost_estimate=price(us, nbytes(outs) + nbytes([(v.shape, v.dtype) for v in ins])),
    )(*ins)


def whole(shape):
    return pl.BlockSpec(shape, lambda *_: (0,) * len(shape))


def mm(left, right):
    return jnp.dot(left, right, preferred_element_type=F32)


def mm_nt(left, right):
    return lax.dot_general(left, right, (((1,), (1,)), ((), ())), preferred_element_type=F32)


def mm_tn(left, right):
    return lax.dot_general(left, right, (((0,), (0,)), ((), ())), preferred_element_type=F32)


def qkv_kernel(flags, x_ref, place_ref, cos_ref, sin_ref, *refs):
    w_refs, (xin_ref, qrot_ref, qn_ref, kv_ref, kn_ref, fac_ref) = refs[:10], refs[10:16]
    gains_ref, heads_ref = refs[16:]
    fi, ty, tc = (flags[n].astype(F32) for n in range(3))
    gains_ref[...] = w_refs[0][:, 128:256].astype(F32).T[64:72, :]
    line = mm_nt(gains_ref[...].astype(BF), place_ref[...])
    lo, hi = line[:, :128], line[:, 128:]
    heads_ref[...] = jnp.concatenate([mix(fi, lo, hi), mix(fi, hi, lo)], axis=1)
    x = x_ref[...].astype(F32)
    x_factor = lax.rsqrt(jnp.mean(x * x, -1, keepdims=True) + EPS)
    xin = (x * x_factor * gains_ref[0:1, :]).astype(BF)
    xin_ref[...] = xin
    prod = [mm_split(xin, pair) for pair in split_w(w_refs, w_refs[6].shape[0])]
    cos, sin = cos_ref[...], sin_ref[...]
    rows = x.shape[0]
    lane = lax.broadcasted_iota(jnp.int32, (rows, 128), 1)
    factors = jnp.zeros((rows, 128), F32)

    def normed(own, oth, row):
        total = jnp.sum(own * own + oth * oth, -1, keepdims=True)
        factor = lax.rsqrt(total * (1.0 / HD) + EPS)
        own, oth = own * factor, oth * factor
        g_own = own * heads_ref[row : row + 1, :128]
        g_oth = oth * heads_ref[row : row + 1, 128:]
        rot = jnp.concatenate([g_own * cos - g_oth * sin, g_oth * cos + g_own * sin], axis=1)
        return jnp.concatenate([own, oth], axis=1), rot, factor

    for r in range(4):
        norm, rot, factor = normed(prod[r][:, :128], prod[4 + r][:, :128], 4)
        qn_ref[r] = norm.astype(BF)
        qrot_ref[r] = rot.astype(BF)
        factors = jnp.where(lane == r, factor, factors)
    keys, vals = [], []
    for dx in range(2):
        sides = []
        for dy in range(2):
            zero = prod[dx * 4 + dy * 2][:, 128:192]
            one = prod[dx * 4 + dy * 2 + 1][:, 128:192]
            sides.append(jnp.concatenate([mix(tc, zero, one), mix(tc, one, zero)], axis=1))
        keys.append(mix(ty, sides[0], sides[1]))
        vals.append(mix(ty, sides[1], sides[0]))
    norm, rot, factor = normed(keys[0], keys[1], 5)
    kn_ref[...] = norm.astype(BF)
    fac_ref[...] = jnp.where(lane == 4, factor, factors)
    kv_ref[...] = jnp.concatenate([rot, vals[0], vals[1]], axis=1).astype(BF)


def split_w(refs, cut):
    pairs = [(ref[:cut, :], ref[cut:, :]) for ref in refs[:6]]
    return pairs + [(refs[6][...], refs[7][...]), (refs[8][...], refs[9][...])]


def head_w(pairs, r):
    return tuple(jnp.concatenate([pairs[r][n], pairs[4 + r][n]], axis=1) for n in (0, 1))


def mm_split(left, pair):
    cut = pair[0].shape[0]
    return mm(left[:, :cut], pair[0]) + mm(left[:, cut:], pair[1])


def mm_nt_split(left, pair):
    return jnp.concatenate([mm_nt(left, pair[0]), mm_nt(left, pair[1])], axis=1)


def kv_block(refs, kb):
    start = (kb % 2) * 256
    return refs[kb // 2][start : start + 256, :]


def attn_kernel(need, q_ref, k2_ref, kp_ref, ko_ref, bias_ref, o_ref, linv_ref, acc_ref, l_ref):
    i = pl.program_id(0)
    acc_ref[...] = jnp.zeros_like(acc_ref)
    l_ref[...] = jnp.zeros_like(l_ref)
    tile = q_ref.shape[1]
    for kb in range(6):

        @pl.when(need[i * 6 + kb] > 0)
        def _(kb=kb):
            kv = kv_block((k2_ref, kp_ref, ko_ref), kb)
            q = q_ref[...].reshape(4 * tile, HD)
            s = mm_nt(q, kv[:, :HD]).reshape(4, tile, 256) * HD ** (-0.5)
            p = jnp.exp(s + bias_ref[:, kb * 256 : (kb + 1) * 256][None])
            p = p.reshape(4 * tile, 256)
            l_ref[...] += p[:, :128] + p[:, 128:]
            acc_ref[...] += mm(p.astype(BF), kv[:, HD:])

    linv = 1.0 / jnp.sum(l_ref[...], -1, keepdims=True)
    linv_ref[...] = jnp.broadcast_to(linv, (4 * tile, 128)).reshape(4, tile, 128)
    o_ref[...] = (acc_ref[...] * linv).astype(BF).reshape(4, tile, HD)


def out_kernel(o_ref, x_ref, gains_ref, *refs):
    w_refs, (part_ref, hid_ref, ffn_ref) = refs[:10], refs[10:]
    pairs = split_w(w_refs, w_refs[6].shape[0])
    part = jnp.zeros(part_ref.shape, F32)
    for r in range(4):
        part += mm_nt_split(o_ref[r], head_w(pairs, r))
    part_ref[...] = part
    factor = lax.rsqrt(jnp.mean(part * part, -1, keepdims=True) + EPS)
    hidden = x_ref[...].astype(F32) + part * factor * gains_ref[1:2, :]
    hid_ref[...] = hidden
    factor = lax.rsqrt(jnp.mean(hidden * hidden, -1, keepdims=True) + EPS)
    ffn_ref[...] = (hidden * factor * gains_ref[2:3, :]).astype(BF)


def gelu_parts(gate, up):
    c0 = math.sqrt(2.0 / math.pi)
    square = gate * gate
    th = jnp.tanh(gate * (c0 + (0.044715 * c0) * square))
    side = 0.5 + 0.5 * th
    gelu = gate * side
    slope = side + gelu * (1.0 - th) * (c0 + (3.0 * 0.044715 * c0) * square)
    return gelu * up, slope * up, gelu


def ffn_layout(refs, layout):
    at, groups = 0, []
    for block, spans in enumerate(layout):
        row = 0
        for start, count in spans:
            groups.append((block, at, pl.ds(row, count), pl.ds(start, count), refs[at]))
            row += count
            at += 1
    return groups


def ffn_kernel(*refs, layout, base, hpad):
    n_x, blocks = sum(len(spans) for spans in layout), len(layout)
    x_refs, w_ref = refs[:n_x], refs[n_x]
    outs, scr = refs[-(13 + n_x) : -9], refs[-9:]
    all_refs, part_refs = outs[:4], outs[4:]
    xs, act_s, slope_s, gelu_s, part_s, x_sem, out_sem, part_sem, _ = scr
    rows = xs.shape[1]
    stage = (xs, act_s, slope_s, gelu_s)
    loads = [[] for _ in range(blocks)]
    for block, at, row, span, ref in ffn_layout(x_refs, layout):
        copy = pltpu.make_async_copy(ref.at[span, :], xs.at[block, row, :], x_sem.at[at])
        copy.start()
        loads[block].append(copy)

    def stack(block, n):
        dst = all_refs[n].at[pl.ds((base + block) * rows, rows), :]
        return pltpu.make_async_copy(stage[n].at[block], dst, out_sem.at[block, n])

    def part_copies(block):
        groups = [group for group in ffn_layout(part_refs, layout) if group[0] == block]
        return [
            pltpu.make_async_copy(part_s.at[block, row, :], ref, part_sem.at[at])
            for _, at, row, _, ref in groups
        ]

    def one_block(i, carry):
        per_block(i, blocks, lambda block: [copy.wait() for copy in loads[block]])
        stack(i, 0).start()
        x = xs[i]
        for c in range(0, hpad, 256):
            wide = min(256, hpad - c)
            gate = mm(x, w_ref[:, c : c + wide])
            up = mm(x, w_ref[:, hpad + c : hpad + c + wide])
            act, slope, gelu = gelu_parts(gate, up)
            act_s[i, :, c : c + wide] = act.astype(BF)
            slope_s[i, :, c : c + wide] = slope.astype(BF)
            gelu_s[i, :, c : c + wide] = gelu.astype(BF)
        for n in (1, 2, 3):
            stack(i, n).start()
        part_s[i] = mm_nt(act_s[i], w_ref[:, 2 * hpad :]).astype(BF)
        per_block(i, blocks, lambda block: [copy.start() for copy in part_copies(block)])
        return carry

    lax.fori_loop(0, blocks, one_block, 0)
    for block in range(blocks):
        for n in range(4):
            stack(block, n).wait()
        for copy in part_copies(block):
            copy.wait()


def per_block(i, blocks, act):
    for block in range(blocks):

        @pl.when(i == block)
        def _(block=block):
            act(block)


def ffn_back_kernel(*refs, layout, base, hpad):
    n_x, blocks = sum(len(spans) for spans in layout), len(layout)
    x_refs, w_ref, saved_refs = refs[:n_x], refs[n_x], refs[n_x + 1 : n_x + 3]
    outs, scr = refs[-(11 + n_x) : -9], refs[-9:]
    all_refs, part_refs = outs[:2], outs[2:]
    xs, dgu_s, slope_s, gelu_s, part_s, x_sem, out_sem, part_sem, saved_sem = scr
    rows = xs.shape[1]
    stage = (xs, dgu_s)
    loads = [[] for _ in range(blocks)]

    def saved(block, n):
        src = saved_refs[n].at[pl.ds((base + block) * rows, rows), :]
        dst = (slope_s, gelu_s)[n].at[block]
        copy = pltpu.make_async_copy(src, dst, saved_sem.at[block, n])
        copy.start()
        loads[block].append(copy)

    for block, at, row, span, ref in ffn_layout(x_refs, layout):
        copy = pltpu.make_async_copy(ref.at[span, :], xs.at[block, row, :], x_sem.at[at])
        copy.start()
        loads[block].append(copy)

    for block in range(blocks):
        saved(block, 0)
        saved(block, 1)

    def stack(block, n):
        dst = all_refs[n].at[pl.ds((base + block) * rows, rows), :]
        return pltpu.make_async_copy(stage[n].at[block], dst, out_sem.at[block, n])

    def part_copies(block):
        groups = [group for group in ffn_layout(part_refs, layout) if group[0] == block]
        return [
            pltpu.make_async_copy(part_s.at[block, row, :], ref, part_sem.at[at])
            for _, at, row, _, ref in groups
        ]

    def one_block(i, carry):
        per_block(i, blocks, lambda block: [copy.wait() for copy in loads[block]])
        stack(i, 0).start()
        dout = xs[i]
        for c in range(0, hpad, 256):
            wide = min(256, hpad - c)
            d_act = mm(dout, w_ref[:, 2 * hpad + c : 2 * hpad + c + wide])
            slope = slope_s[i, :, c : c + wide].astype(F32)
            gelu = gelu_s[i, :, c : c + wide].astype(F32)
            dgu_s[i, :, c : c + wide] = (d_act * slope).astype(BF)
            dgu_s[i, :, hpad + c : hpad + c + wide] = (d_act * gelu).astype(BF)
        stack(i, 1).start()
        part_s[i] = mm_nt(dgu_s[i], w_ref[:, : 2 * hpad]).astype(BF)
        per_block(i, blocks, lambda block: [copy.start() for copy in part_copies(block)])
        return carry

    lax.fori_loop(0, blocks, one_block, 0)
    for block in range(blocks):
        for n in range(2):
            stack(block, n).wait()
        for copy in part_copies(block):
            copy.wait()


def hold_kernel(src_ref, dst_ref, sem):
    copy = pltpu.make_async_copy(src_ref, dst_ref, sem.at[0])
    copy.start()
    copy.wait()


def hold(value):
    return pl.pallas_call(
        hold_kernel,
        out_shape=pltpu.VMEM(value.shape, value.dtype),
        in_specs=[pl.BlockSpec(memory_space=pltpu.HBM)],
        out_specs=pl.BlockSpec(memory_space=pltpu.VMEM),
        scratch_shapes=[pltpu.SemaphoreType.DMA((1,))],
        compiler_params=pltpu.CompilerParams(vmem_limit_bytes=16 << 20),
        cost_estimate=price(3, 1000000),
    )(in_hbm(value))


def in_hbm(value):
    return pltpu.with_memory_space_constraint(value, pltpu.HBM)


def ffn_call(kernel, blocks, base, saved, w_ffn, bufs):
    pieces = [value for block in blocks for value, _, _ in block]
    layout = tuple(tuple((start, count) for _, start, count in block) for block in blocks)
    n, back = len(blocks), bool(saved)
    width, hpad = w_ffn.shape[0], w_ffn.shape[1] // 3
    rows = sum(count for _, count in layout[0])
    widths = [width, 2 * hpad] if back else [width, hpad, hpad, hpad]
    ins = [in_hbm(v) for v in pieces] + [w_ffn] + [in_hbm(v) for v in saved]
    aliases = {}
    if bufs is not None:
        aliases = {len(ins) + k: k for k in range(len(widths))}
        ins = ins + [in_hbm(v) for v in bufs]
    hbm = pl.BlockSpec(memory_space=pltpu.HBM)
    in_specs = [hbm] * len(ins)
    in_specs[len(pieces)] = pl.BlockSpec(memory_space=pltpu.VMEM)
    counts = [count for spans in layout for _, count in spans]
    shapes = [((8 * rows, w), BF) for w in widths] + [((count, width), BF) for count in counts]
    mid = [2 * hpad, hpad, hpad] if back else [hpad, hpad, hpad]
    scratch = [pltpu.VMEM((n, rows, w), BF) for w in [width] + mid + [width]]
    scratch += [
        pltpu.SemaphoreType.DMA((len(pieces),)),
        pltpu.SemaphoreType.DMA((n, 4)),
        pltpu.SemaphoreType.DMA((len(pieces),)),
        pltpu.SemaphoreType.DMA((n, 2)),
    ]
    outs = pl.pallas_call(
        partial(kernel, layout=layout, base=base, hpad=hpad),
        out_shape=[pltpu.HBM(shape, dtype) for shape, dtype in shapes],
        in_specs=in_specs,
        out_specs=[hbm] * len(shapes),
        scratch_shapes=scratch,
        input_output_aliases=aliases,
        compiler_params=pltpu.CompilerParams(vmem_limit_bytes=28 << 20),
        cost_estimate=price(6 * n, 1000000 * n),
    )(*ins)
    grouped, at = [], len(widths)
    for spans in layout:
        grouped.append(tuple(outs[at : at + len(spans)]))
        at += len(spans)
    return outs[: len(widths)], grouped


def ffn_mid_kernel(*refs):
    hid_ref, cot_ref, gains_ref, out_ref, dout_ref, gain_ref = refs[6:]
    part = piece_sum(refs[:6])
    gain = gains_ref[3:4, :]
    factor = lax.rsqrt(jnp.mean(part * part, -1, keepdims=True) + EPS)
    out_ref[...] = (hid_ref[...] + part * factor * gain).astype(BF)
    back, gain_grad = norm_back_tile(part, gain, cot_ref[...].astype(F32))
    dout_ref[...] = back.astype(BF)
    gain_ref[0:1, :] = gain_grad


def norm_back_tile(raw, gain, upstream):
    factor = lax.rsqrt(jnp.mean(raw * raw, -1, keepdims=True) + EPS)
    normed = raw * factor
    gain_grad = jnp.sum(upstream * normed, axis=0, keepdims=True)
    scaled = upstream * gain
    back = factor * (scaled - normed * jnp.mean(scaled * normed, -1, keepdims=True))
    return back, gain_grad


def mid_kernel(*refs):
    hid_ref, part_ref, cot_ref, gains_ref = refs[6:10]
    w_refs, (dhid_ref, dpart_ref, dhead_ref, gain_ref) = refs[10:20], refs[20:]
    din = piece_sum(refs[:6])
    extra, gain_ffn = norm_back_tile(hid_ref[...], gains_ref[2:3, :], din)
    dhid = cot_ref[...].astype(F32) + extra
    dhid_ref[...] = dhid
    dpart, gain_post = norm_back_tile(part_ref[...], gains_ref[1:2, :], dhid)
    dpart = dpart.astype(BF)
    dpart_ref[...] = dpart
    gain_ref[0:1, :] = gain_ffn
    gain_ref[1:2, :] = gain_post
    pairs = split_w(w_refs, w_refs[6].shape[0])
    for r in range(4):
        dhead_ref[r] = mm_split(dpart, head_w(pairs, r)).astype(BF)


def attn_back_kernel(
    need,
    q_ref,
    k2_ref,
    kp_ref,
    ko_ref,
    bias_ref,
    o_ref,
    do_ref,
    linv_ref,
    qn_ref,
    fac_ref,
    cos_ref,
    sin_ref,
    gq_ref,
    dq_ref,
    d2_ref,
    dp_ref,
    down_ref,
    gain_ref,
    acc_ref,
    dkv_ref,
):
    i = pl.program_id(0)
    tile = q_ref.shape[1]

    @pl.when(i == 0)
    def _():
        dkv_ref[...] = jnp.zeros_like(dkv_ref)
        gain_ref[...] = jnp.zeros_like(gain_ref)

    acc_ref[...] = jnp.zeros_like(acc_ref)
    q = q_ref[...].reshape(4 * tile, HD)
    do = do_ref[...].reshape(4 * tile, HD)
    linv = linv_ref[...].reshape(4 * tile, 128)[:, 0:1]
    inner = jnp.sum(do.astype(F32) * o_ref[...].reshape(4 * tile, HD).astype(F32), -1, keepdims=True)
    for kb in range(6):

        @pl.when(need[i * 6 + kb] > 0)
        def _(kb=kb):
            kv = kv_block((k2_ref, kp_ref, ko_ref), kb)
            keys, vals = kv[:, :HD], kv[:, HD:]
            s = mm_nt(q, keys).reshape(4, tile, 256) * HD ** (-0.5)
            p = jnp.exp(s + bias_ref[:, kb * 256 : (kb + 1) * 256][None])
            p = p.reshape(4 * tile, 256) * linv
            dp = mm_nt(do, vals)
            ds = (p * (dp - inner)).astype(BF)
            acc_ref[...] += mm(ds, keys)
            span = slice(kb * 256, (kb + 1) * 256)
            dkv_ref[span, :HD] += mm_tn(ds, q)
            dkv_ref[span, HD:] += mm_tn(p.astype(BF), do)

    cos, sin = cos_ref[...], sin_ref[...]
    gain = jnp.zeros((1, HD), F32)
    for r in range(4):
        dq = acc_ref[r * tile : (r + 1) * tile, :] * HD ** (-0.5)
        own, oth = dq[:, :128], dq[:, 128:]
        back = jnp.concatenate([own * cos + oth * sin, oth * cos - own * sin], axis=1)
        norm = qn_ref[r].astype(F32)
        gain += jnp.sum(back * norm, axis=0, keepdims=True)
        scaled = back * gq_ref[4:5, :]
        mean = jnp.mean(scaled * norm, -1, keepdims=True)
        dq_ref[r] = (fac_ref[:, r : r + 1] * (scaled - norm * mean)).astype(BF)
    gain_ref[0:1, :] += gain

    @pl.when(i == pl.num_programs(0) - 1)
    def _():
        rows = d2_ref.shape[0]
        scale = HD ** (-0.5)
        for n, ref in enumerate((d2_ref, dp_ref, down_ref)):
            block = dkv_ref[n * rows : (n + 1) * rows, :]
            ref[:, :HD] = (block[:, :HD] * scale).astype(ref.dtype)
            ref[:, HD:] = block[:, HD:].astype(ref.dtype)


def post_kernel(
    flags,
    dq_ref,
    dkv_ref,
    dp_ref,
    kn_ref,
    fac_ref,
    cos_ref,
    sin_ref,
    gk_ref,
    x_ref,
    gains_ref,
    dhid_ref,
    gq_grad,
    mid_grad,
    post_grad,
    place_ref,
    *refs,
):
    w_refs, din_ref, kvraw_ref, gain_ref = refs[:10], *refs[10:]
    fi, ty, tc = (flags[n].astype(F32) for n in range(3))
    dkv = dkv_ref[...] + dp_ref[...].astype(F32)
    cos, sin = cos_ref[...], sin_ref[...]
    own, oth = dkv[:, :128], dkv[:, 128:256]
    back = jnp.concatenate([own * cos + oth * sin, oth * cos - own * sin], axis=1)
    norm = kn_ref[...].astype(F32)
    gk_grad = jnp.sum(back * norm, axis=0, keepdims=True)
    scaled = back * gk_ref[5:6, :]
    mean = jnp.mean(scaled * norm, -1, keepdims=True)
    dkey = fac_ref[:, 4:5] * (scaled - norm * mean)
    dval = dkv[:, 256:]
    kvraw_ref[...] = jnp.concatenate([dkey, dval], axis=1).astype(BF)
    din = jnp.zeros(din_ref.shape, F32)
    zeros = jnp.zeros((dkv.shape[0], 64), F32)
    pairs = split_w(w_refs, w_refs[6].shape[0])
    rel = 0
    for dx in range(2):
        kh = dkey[:, dx * 128 : (dx + 1) * 128]
        vh = dval[:, dx * 128 : (dx + 1) * 128]
        for dy in range(2):
            half = mix(ty, kh, vh) if dy == 0 else mix(ty, vh, kh)
            for dc in range(2):
                lo, hi = half[:, :64], half[:, 64:]
                part = mix(tc, lo, hi) if dc == 0 else mix(tc, hi, lo)
                side = jnp.concatenate([part, zeros], axis=1).astype(BF)
                dprod = jnp.concatenate(
                    [dq_ref[dy * 2 + dc][:, dx * 128 : (dx + 1) * 128], side], axis=1
                )
                din += mm_nt_split(dprod, pairs[rel])
                rel += 1
    x = x_ref[...].astype(F32)
    extra, gain_pre = norm_back_tile(x, gains_ref[0:1, :], din)
    din_ref[...] = dhid_ref[...] + extra

    def spread(grad):
        own, oth = grad[:, :128], grad[:, 128:]
        whole_row = jnp.concatenate([mix(fi, own, oth), mix(fi, oth, own)], axis=1)
        return mm(jnp.broadcast_to(whole_row.astype(BF), (8, HD)), place_ref[...])[0:1, :]

    gain_ref[...] = jnp.zeros_like(gain_ref)
    gain_ref[0:1, :] = gain_pre
    gain_ref[1:2, :] = mid_grad[1:2, :]
    gain_ref[2:3, :] = mid_grad[0:1, :]
    gain_ref[3:4, :] = post_grad[0:1, :]
    gain_ref[4:5, :] = spread(gq_grad[0:1, :])
    gain_ref[5:6, :] = spread(gk_grad)


def store_rows(refs, value):
    cut = refs[0].shape[0]
    refs[0][...] = value[:cut, :]
    refs[1][...] = value[cut:, :]


def qo_grad_kernel(xin, xin_c, dq, dq_c, dpart, dpart_c, head, head_c, *outs):
    xt, xt_c, dt, dt_c = (ref[...].T for ref in (xin, xin_c, dpart, dpart_c))
    for dy in range(2):
        gq = (mm(xt, dq[2 * dy]) + mm(xt_c, dq_c[dy])).astype(BF)
        go = (mm(dt, head[2 * dy]) + mm(dt_c, head_c[dy])).astype(BF)
        for dx in range(2):
            half = slice(dx * 128, (dx + 1) * 128)
            at = 4 * dx + 2 * dy
            store_rows(outs[at : at + 2], jnp.concatenate([gq[:, half], go[:, half]], axis=1))


def kv_grad_kernel(flags, xin, xin_c, kv, kv_c, gain, gain_c, *refs):
    outs, rows_ref = refs[:8], refs[8]
    ty, tc = flags[1].astype(F32), flags[2].astype(F32)
    rows_ref[...] = jnp.zeros_like(rows_ref)
    rows_ref[64:72, :] = gain[...] + gain_c[...]
    gain_cols = rows_ref[...].T
    xt, xt_c = xin[...].T, xin_c[...].T

    def sides(ref):
        block = ref[...].astype(F32)
        picked = []
        for dy in range(2):
            for dx in range(2):
                kh = block[:, dx * 128 : (dx + 1) * 128]
                vh = block[:, 256 + dx * 128 : 256 + (dx + 1) * 128]
                half = mix(ty, kh, vh) if dy == 0 else mix(ty, vh, kh)
                picked.append(mix(tc, half[:, :64], half[:, 64:]))
        return jnp.concatenate(picked, axis=1).astype(BF)

    grad = mm(xt, sides(kv)) + mm(xt_c, sides(kv_c))
    zeros = jnp.zeros((grad.shape[0], 64), F32)
    for dy in range(2):
        for dx in range(2):
            at = 4 * dx + 2 * dy
            col = (2 * dy + dx) * 64
            part = jnp.concatenate([grad[:, col : col + 64], zeros], axis=1) + gain_cols
            store_rows(outs[at : at + 2], part.astype(BF))


def chip_first(parts):
    _, near_y, near_x, far = (parts[n : n + 2] for n in (0, 2, 4, 6))
    return swap(far[0], "fi"), swap(far[1], "ty"), swap(near_x[0], "fi"), swap(near_y[1], "ty")


def chip_second(parts, first):
    own, near_y, near_x, _ = (parts[n : n + 2] for n in (0, 2, 4, 6))
    from_x, from_y, got_x_top, got_y_bot = first
    x_bot = (near_x[1].astype(F32) + from_y.astype(F32)).astype(BF)
    y_top = (near_y[0].astype(F32) + from_x.astype(F32)).astype(BF)
    return (*own, got_x_top, swap(x_bot, "fi"), swap(y_top, "ty"), got_y_bot)


def gather_sum_kernel(*refs):
    out_ref = refs[12]
    for n, cols in ((0, slice(0, 256)), (6, slice(256, 384))):
        own_top, own_bot, x_top, x_bot, y_top, y_bot = (ref[...].astype(F32) for ref in refs[n : n + 6])
        cut = own_top.shape[0]
        out_ref[:cut, cols] = (own_top + x_top + y_top).astype(BF)
        out_ref[cut:, cols] = (own_bot + x_bot + y_bot).astype(BF)


def pad_cols(value, width):
    return jnp.pad(value, ((0, 0), (0, width - value.shape[1])))


def body(
    tokens,
    positions,
    segments,
    w_query,
    w_key,
    w_value,
    w_out,
    w_gate,
    w_up,
    w_down,
    gain_attn_pre,
    gain_query,
    gain_key,
    gain_attn_post,
    gain_ffn_pre,
    gain_ffn_post,
    cotangent,
):
    fi = lax.axis_index("fi")
    ty = lax.axis_index("ty")
    tc = lax.axis_index("tc")
    t_idx = ty * 2 + tc
    me = fi * 4 + t_idx
    first = fi == 0
    rows = tokens.shape[0]
    width = tokens.shape[1]
    shard = w_query.shape[0]
    nf = width // shard
    hid = w_gate.shape[1] // 2
    hpad = -(-hid // 128) * 128
    gshard = gain_query.shape[0]

    def pair_rows(keep, recv):
        return jnp.where(
            first,
            jnp.concatenate([keep, recv], axis=0),
            jnp.concatenate([recv, keep], axis=0),
        )

    kv_mine = jnp.where(ty == 0, w_key, w_value)
    out_t = w_out.T
    gains = pad_cols(
        jnp.stack(
            [
                gain_attn_pre,
                gain_attn_post,
                gain_ffn_pre,
                gain_ffn_post,
                jnp.pad(gain_query, (0, shard - gshard)),
                jnp.pad(gain_key, (0, shard - gshard)),
            ],
            axis=1,
        ),
        64,
    )

    def piece(h):
        kv_half = kv_mine[:, h * 128 : (h + 1) * 128]
        kv_part = jnp.where(tc == 0, kv_half[:, :64], kv_half[:, 64:])
        return jnp.concatenate(
            [
                w_query[:, h * 128 : (h + 1) * 128],
                kv_part,
                gains,
                out_t[:, h * 128 : (h + 1) * 128],
            ],
            axis=1,
        )

    piece0, piece1 = piece(0), piece(1)
    keep = jnp.where(first, piece0, piece1)
    recv = swap(jnp.where(first, piece1, piece0), "fi")

    down_t = w_down.T

    def halves(weight):
        lo, hi = pad_cols(weight[:, :hid], hpad), pad_cols(weight[:, hid:], hpad)
        return jnp.where(first, lo, hi), jnp.where(first, hi, lo)

    gate_keep, gate_send = halves(w_gate)
    up_keep, up_send = halves(w_up)
    down_keep, down_send = halves(down_t)
    ffn_keep = jnp.concatenate([gate_keep, up_keep, down_keep], axis=1)
    ffn_send = jnp.concatenate([gate_send, up_send, down_send], axis=1)
    ffn_send, ffn_keep, recv = lax.optimization_barrier((ffn_send, ffn_keep, recv))
    ffn_recv = swap(ffn_send, "fi")
    attn_col = lax.all_gather(pair_rows(keep, recv), "fo", axis=0, tiled=True)
    attn_col, ffn_pair = lax.optimization_barrier((attn_col, pair_rows(ffn_keep, ffn_recv)))
    w_ffn = lax.all_gather(ffn_pair, "fo", axis=0, tiled=True)

    elem = lax.broadcasted_iota(jnp.int32, (HD, width), 0)
    spot = lax.broadcasted_iota(jnp.int32, (HD, width), 1)
    place = (spot == (elem // gshard) * shard + elem % gshard).astype(BF)
    cut = width // 256 * 128
    row_start = t_idx * rows
    pos_local = lax.dynamic_slice_in_dim(positions, row_start, rows)
    seg_local = lax.dynamic_slice_in_dim(segments, row_start, rows)

    def block_of(meta, back):
        return lax.dynamic_slice_in_dim(meta, ((t_idx - back) % 4) * rows, rows)

    k_pos = jnp.concatenate([block_of(positions, 2), block_of(positions, 1), pos_local])
    k_seg = jnp.concatenate(
        [
            jnp.where(t_idx == 3, block_of(segments, 2), -1),
            jnp.where(t_idx >= 1, block_of(segments, 1), -1),
            seg_local,
        ]
    )
    allowed = (
        ((k_seg[None, :] == 0) | (k_seg[None, :] == seg_local[:, None]))
        & (k_pos[None, :] <= pos_local[:, None])
        & (pos_local[:, None] - k_pos[None, :] < WINDOW)
    )
    bias = jnp.where(allowed, 0.0, NEG).astype(F32)
    need = jnp.any(allowed.reshape(4, rows // 4, 6, rows // 2), axis=(1, 3))
    need = need.astype(jnp.int32).reshape(24)
    frequency = jnp.exp(-math.log(BASE) * jnp.arange(HALF).astype(F32) / HALF)
    angles = pos_local.astype(F32)[:, None] * frequency
    cosine = jnp.cos(angles)
    sine = jnp.sin(angles) * jnp.where(first, 1.0, -1.0)

    w_parts, (bias, need, cosine, sine, place) = plane_gather(
        attn_col, cut, (bias, need, cosine, sine, place)
    )
    w_parts = [in_hbm(piece) for pieces in w_parts for piece in pieces]
    flags = jnp.stack([fi, ty, tc]).astype(jnp.int32)
    qkv_spec = [pl.BlockSpec((part.shape[0], 256), lambda *_: (0, 0)) for part in w_parts]
    wo_spec = [pl.BlockSpec((part.shape[0], 128), lambda *_: (0, 2)) for part in w_parts]
    full, gains8 = whole((rows, width)), whole((8, width))
    heads = whole((4, rows, HD))
    lanes = whole((rows, 128))
    kv_full = whole((rows, 2 * HD))
    attn_in, q_rot, q_norm, kv_own, k_norm, factors, gain_rows, head_gains = run(
        qkv_kernel,
        [
            ((rows, width), BF),
            ((4, rows, HD), BF),
            ((4, rows, HD), BF),
            ((rows, 2 * HD), BF),
            ((rows, HD), BF),
            ((rows, 128), F32),
            ((8, width), F32),
            ((8, HD), F32),
        ],
        (flags, tokens, place, cosine, sine, *w_parts),
        9,
        grid=(1,),
        in_specs=[full, whole((HD, width)), lanes, lanes] + qkv_spec,
        out_specs=[full, heads, heads, kv_full, whole((rows, HD)), lanes, gains8, whole((8, HD))],
        prefetch=1,
    )
    kv_prev = lax.ppermute(kv_own, ("ty", "tc"), [(i, (i + 1) % 4) for i in range(4)])
    kv_two = swap(kv_prev, "tc")
    tile = rows // 4
    q_tile = pl.BlockSpec((4, tile, HD), lambda i, *_: (0, i, 0))
    l_tile = pl.BlockSpec((4, tile, 128), lambda i, *_: (0, i, 0))
    bias_tile = pl.BlockSpec((tile, 3 * rows), lambda i, *_: (i, 0))
    head_out, linv = run(
        attn_kernel,
        [((4, rows, HD), BF), ((4, rows, 128), F32)],
        (need, q_rot, kv_two, kv_prev, kv_own, bias),
        8,
        grid=(4,),
        in_specs=[q_tile, kv_full, kv_full, kv_full, bias_tile],
        out_specs=[q_tile, l_tile],
        scratch=[pltpu.VMEM((4 * tile, HD), F32), pltpu.VMEM((4 * tile, 128), F32)],
        prefetch=1,
    )
    attn_part, hidden, ffn_local = run(
        out_kernel,
        [((rows, width), F32), ((rows, width), F32), ((rows, width), BF)],
        (head_out, tokens, gain_rows, *w_parts),
        6,
        grid=(1,),
        in_specs=[heads, full, gains8] + wo_spec,
        out_specs=[full, full, full],
    )

    half = rows // 2
    def far_pieces(top, bot, after):
        top, bot, after = lax.optimization_barrier((top, bot, after))
        return (top, bot), (swap(top, "tc"), swap(bot, "tc")), after

    by_x, by_y, by_c = swap(ffn_local, "fi"), swap(ffn_local, "ty"), swap(ffn_local, "tc")
    top, bot = swap(by_y[:half], "fi"), swap(by_x[half:], "ty")
    by_xc, by_yc = swap(by_x, "tc"), swap(by_y, "tc")
    w_ffn = hold(w_ffn)
    top, bot, w_ffn = lax.optimization_barrier((top, bot, w_ffn))
    top_c, bot_c = swap(top, "tc"), swap(bot, "tc")
    whole_of = lambda value: [(value, 0, rows)]
    halves_of = lambda low, high: [(low, 0, half), (high, half, half)]
    both_of = lambda top, bot: [(top, 0, half), (bot, 0, half)]
    far = [both_of(top, bot), both_of(top_c, bot_c)]
    bufs, parts_f = ffn_call(ffn_kernel, far, 6, [], w_ffn, None)
    sent = far_sum(*parts_f, half)
    by_x, by_y, by_xc, by_yc, sent = lax.optimization_barrier((by_x, by_y, by_xc, by_yc, sent))
    got = far_swap(sent)
    first_rows = [halves_of(by_x, by_y), halves_of(by_xc, by_yc)]
    bufs, parts_1 = ffn_call(ffn_kernel, first_rows, 2, [], w_ffn, bufs)
    by_x, by_y, by_xc, by_yc, got = lax.optimization_barrier((by_x, by_y, by_xc, by_yc, got))
    second_rows = [
        [(by_x, half, half), (by_y, 0, half)],
        [(by_xc, half, half), (by_yc, 0, half)],
    ]
    bufs, parts_2 = ffn_call(ffn_kernel, second_rows, 4, [], w_ffn, bufs)
    first_in = near_swap(near_first(parts_1))
    second_out = near_second(parts_2, got)
    first_in, second_out = lax.optimization_barrier((first_in, second_out))
    second_in = near_swap(second_out)
    (x_all, act_all, slope_all, gelu_all), parts_o = ffn_call(
        ffn_kernel, [whole_of(ffn_local), whole_of(by_c)], 0, [], w_ffn, bufs
    )
    pieces = plane_pieces(parts_o, first_in, second_in)
    quarter = whole((half, width))
    piece_spec = [full, full] + [quarter] * 4

    other = swap(jnp.stack([head_out[1], head_out[3]]), "tc"), swap(attn_in, "tc")
    pieces, (head_out_c, attn_in_c) = lax.optimization_barrier((pieces, other))
    output, d_local, ffn_post_grad = run(
        ffn_mid_kernel,
        [((rows, width), BF), ((rows, width), BF), ((8, width), F32)],
        (*pieces, hidden, cotangent, gain_rows),
        6,
        grid=(1,),
        in_specs=piece_spec + [full, full, gains8],
        out_specs=[full, full, gains8],
    )
    by_x, by_y, by_c = swap(d_local, "fi"), swap(d_local, "ty"), swap(d_local, "tc")
    saved = [slope_all, gelu_all]
    own_rows = [whole_of(d_local), whole_of(by_c)]
    bufs, parts_o = ffn_call(ffn_back_kernel, own_rows, 0, saved, w_ffn, None)
    by_x, by_y, parts_o = lax.optimization_barrier((by_x, by_y, parts_o))
    top, bot = swap(by_y[:half], "fi"), swap(by_x[half:], "ty")
    by_xc, by_yc = swap(by_x, "tc"), swap(by_y, "tc")
    first_rows = [halves_of(by_x, by_y), halves_of(by_xc, by_yc)]
    bufs, parts_1 = ffn_call(ffn_back_kernel, first_rows, 2, saved, w_ffn, bufs)
    (top, bot), (top_c, bot_c), parts_1 = far_pieces(top, bot, parts_1)
    first_in = near_swap(near_first(parts_1))
    far = [both_of(top, bot), both_of(top_c, bot_c)]
    bufs, parts_f = ffn_call(ffn_back_kernel, far, 6, saved, w_ffn, bufs)
    second_rows = [
        [(by_x, half, half), (by_y, 0, half)],
        [(by_xc, half, half), (by_yc, 0, half)],
    ]
    (d_all, dgu_all), parts_2 = ffn_call(
        ffn_back_kernel, second_rows, 4, saved, w_ffn, bufs
    )
    sent = far_sum(*parts_f, half)
    d_all, sent, first_in = lax.optimization_barrier((d_all, sent, first_in))
    got = far_swap(sent)
    grad_dt = dot_left_t(d_all, act_all).astype(BF)
    dgu_all, grad_dt, got = lax.optimization_barrier((dgu_all, grad_dt, got))
    second_in = near_swap(near_second(parts_2, got))
    grad_gu = dot_left_t(x_all, dgu_all).astype(BF)
    pieces = plane_pieces(parts_o, first_in, second_in)
    pieces, grad_gu = lax.optimization_barrier((pieces, grad_gu))
    sum_dt = lax.psum_scatter(grad_dt, "fo", scatter_dimension=0, tiled=True)
    sum_gu = lax.psum_scatter(grad_gu, "fo", scatter_dimension=0, tiled=True)

    def unpair(summed):
        top_rows, bot_rows = summed[:shard], summed[shard:]
        mine = jnp.where(first, top_rows, bot_rows)
        theirs = swap(jnp.where(first, bot_rows, top_rows), "fi")
        return jnp.where(first, mine, theirs), jnp.where(first, theirs, mine)

    def join(lo, hi):
        return jnp.concatenate([lo[:, :hid], hi[:, :hid]], axis=1).astype(F32)

    hidden_grad, attn_part_grad, head_grad, mid_gains = run(
        mid_kernel,
        [((rows, width), F32), ((rows, width), BF), ((4, rows, HD), BF), ((8, width), F32)],
        (
            *map(in_hbm, (*pieces, hidden, attn_part, cotangent)),
            gain_rows,
            *w_parts,
        ),
        10,
        grid=(1,),
        in_specs=piece_spec + [full, full, full, gains8] + wo_spec,
        out_specs=[full, full, heads, whole((8, width))],
    )
    fac_tile = pl.BlockSpec((tile, 128), lambda i, *_: (i, 0))
    line = whole((8, HD))
    q_raw_grad, kv_grad_two, kv_grad_prev, kv_grad_own, gain_q = run(
        attn_back_kernel,
        [
            ((4, rows, HD), BF),
            ((rows, 2 * HD), BF),
            ((rows, 2 * HD), BF),
            ((rows, 2 * HD), F32),
            ((8, HD), F32),
        ],
        (
            need,
            q_rot,
            kv_two,
            kv_prev,
            kv_own,
            bias,
            head_out,
            head_grad,
            linv,
            q_norm,
            factors,
            cosine,
            sine,
            head_gains,
        ),
        12,
        grid=(4,),
        in_specs=[
            q_tile,
            kv_full,
            kv_full,
            kv_full,
            bias_tile,
            q_tile,
            q_tile,
            l_tile,
            q_tile,
            fac_tile,
            fac_tile,
            fac_tile,
            line,
        ],
        out_specs=[q_tile, kv_full, kv_full, kv_full, whole((8, HD))],
        scratch=[pltpu.VMEM((4 * tile, HD), F32), pltpu.VMEM((3 * rows, 2 * HD), F32)],
        prefetch=1,
    )
    q_raw_grad, attn_part_c = lax.optimization_barrier((q_raw_grad, swap(attn_part_grad, "tc")))
    back_two = kv_grad_prev.astype(F32) + swap(kv_grad_two, "tc").astype(F32)
    q_raw_grad, back_two = lax.optimization_barrier((q_raw_grad, back_two.astype(BF)))
    back_prev = lax.ppermute(back_two, ("ty", "tc"), [(i, (i + 3) % 4) for i in range(4)])
    def row_pieces(cols):
        return [((n, cols), BF) for n in (cut, width - cut)] * 4

    other_heads = lambda value: swap(jnp.stack([value[1], value[3]]), "tc")
    two_heads = whole((2, rows, HD))
    qo_grads = run(
        qo_grad_kernel,
        row_pieces(256),
        (
            attn_in,
            attn_in_c,
            q_raw_grad,
            other_heads(q_raw_grad),
            attn_part_grad,
            attn_part_c,
            head_out,
            head_out_c,
        ),
        5,
        grid=(1,),
        in_specs=[full, full, heads, two_heads, full, full, heads, two_heads],
        out_specs=[whole(shape) for shape, _ in row_pieces(256)],
    )
    back_prev, sum_dt, qo_grads = lax.optimization_barrier((back_prev, sum_dt, qo_grads))
    qo_first = chip_first(qo_grads)
    input_grad, kv_raw_grad, gain_grads = run(
        post_kernel,
        [((rows, width), F32), ((rows, 2 * HD), BF), ((8, width), F32)],
        (
            flags,
            q_raw_grad,
            in_hbm(kv_grad_own),
            back_prev,
            k_norm,
            factors,
            cosine,
            sine,
            head_gains,
            in_hbm(tokens),
            gain_rows,
            in_hbm(hidden_grad),
            gain_q,
            mid_gains,
            ffn_post_grad,
            place,
            *w_parts,
        ),
        9,
        grid=(1,),
        in_specs=[heads, kv_full, kv_full, whole((rows, HD)), lanes, lanes, lanes, line]
        + [full, gains8, full, whole((8, HD)), gains8, gains8]
        + [whole((HD, width))]
        + qkv_spec,
        out_specs=[full, kv_full, gains8],
        prefetch=1,
    )
    kv_raw_grad, qo_first = lax.optimization_barrier((kv_raw_grad, qo_first))
    kv_grads = run(
        kv_grad_kernel,
        row_pieces(128),
        (
            flags,
            attn_in,
            attn_in_c,
            kv_raw_grad,
            swap(kv_raw_grad, "tc"),
            gain_grads,
            swap(gain_grads, "tc"),
        ),
        3,
        grid=(1,),
        in_specs=[full, full, kv_full, kv_full, gains8, gains8],
        out_specs=[whole(shape) for shape, _ in row_pieces(128)],
        scratch=[pltpu.VMEM((128, width), F32)],
        prefetch=1,
    )
    qo_pieces = chip_second(qo_grads, qo_first)
    kv_pieces = chip_second(kv_grads, chip_first(kv_grads))
    qo_pieces, kv_pieces, sum_gu = lax.optimization_barrier((qo_pieces, kv_pieces, sum_gu))
    (attn_grads,) = run(
        gather_sum_kernel,
        [((width, 384), BF)],
        (*qo_pieces, *kv_pieces),
        2,
        grid=(1,),
        in_specs=[whole(piece.shape) for piece in (*qo_pieces, *kv_pieces)],
        out_specs=[whole((width, 384))],
    )
    sum_attn = lax.psum_scatter(attn_grads, "fo", scatter_dimension=0, tiled=True)
    dt_lo, dt_hi = unpair(sum_dt)
    gu_lo, gu_hi = unpair(sum_gu)
    grad_gate = join(gu_lo[:, :hpad], gu_hi[:, :hpad])
    grad_up = join(gu_lo[:, hpad:], gu_hi[:, hpad:])
    grad_down = join(dt_lo, dt_hi).T

    a_lo, a_hi = unpair(sum_attn)
    grad_out = jnp.concatenate([a_lo[:, 128:256], a_hi[:, 128:256]], axis=1).astype(F32).T
    grad_query = jnp.concatenate([a_lo[:, :128], a_hi[:, :128]], axis=1).astype(F32)
    kv_part = jnp.concatenate([a_lo[:, 256:320], a_hi[:, 256:320]], axis=1)
    others = [
        lax.ppermute(kv_part, ("ty", "tc"), [(i, i ^ step) for i in range(4)]) for step in (1, 2, 3)
    ]
    row_here = jnp.where(tc == 0, 0, 1)

    def kv_lines(near, far):
        even = jnp.where(row_here == 0, near, far)
        odd = jnp.where(row_here == 0, far, near)
        return jnp.concatenate([even[:, :64], odd[:, :64], even[:, 64:], odd[:, 64:]], axis=1)

    kv_here, kv_far = kv_lines(kv_part, others[0]), kv_lines(others[1], others[2])
    grad_key = jnp.where(ty == 0, kv_here, kv_far).astype(F32)
    grad_value = jnp.where(ty == 0, kv_far, kv_here).astype(F32)
    gain_out = a_lo[:, 320:328].astype(F32).T
    return (
        output.astype(BF),
        input_grad,
        grad_query,
        grad_key,
        grad_value,
        grad_out,
        grad_gate,
        grad_up,
        grad_down,
        gain_out[0],
        gain_out[4, :gshard],
        gain_out[5, :gshard],
        gain_out[1],
        gain_out[2],
        gain_out[3],
    )


def solution(mesh):
    nf, nt = mesh.shape["fsdp"], mesh.shape["tensor"]
    fine = Mesh(mesh.devices.reshape(nf // 2, 2, nt // 2, 2), ("fo", "fi", "ty", "tc"))
    f_axes, t_axes = ("fo", "fi"), ("ty", "tc")
    rows = P(f_axes + t_axes, None)
    col = P(f_axes, t_axes)
    flat = P(f_axes, None)
    out_w = P(t_axes, f_axes)
    vec = P(f_axes)
    in_specs = (rows, vec, vec, col, flat, flat, out_w, col, col, out_w) + (vec,) * 6 + (rows,)
    out_specs = (rows, rows, col, flat, flat, out_w, col, col, out_w) + (vec,) * 6
    return jax.shard_map(body, mesh=fine, in_specs=in_specs, out_specs=out_specs, check_vma=False)
```

```python
import math
from functools import partial

import jax
import jax.numpy as jnp
from jax import lax
from jax.experimental import pallas as pl
from jax.experimental.pallas import tpu as pltpu
from jax.sharding import Mesh, PartitionSpec as P

HD = 256
WINDOW = 512
PROMPT = 1024
CONT = 8
CLEN = 128


EPS = 1e-06
NEG = -1e30
BASE = 10000.0
HALF = HD // 2
BF = jnp.bfloat16
F32 = jnp.float32


def dot_left_t(left_op, right_op):
    return lax.dot_general(
        left_op, right_op, (((0,), (0,)), ((), ())), preferred_element_type=jnp.float32
    )


def swap(value, axis):
    return lax.ppermute(value, axis, [(0, 1), (1, 0)])


RELS = [(dx, dy, dc) for dx in (0, 1) for dy in (0, 1) for dc in (0, 1)]


def plane_gather(own, cut, side):
    by_x = swap(own, "fi")
    by_y = swap(own, "ty")
    by_c = swap(own, "tc")
    by_x, by_y, side = lax.optimization_barrier((by_x, by_y, side))
    diag_top = swap(by_y[:cut], "fi")
    diag_bot = swap(by_x[cut:], "ty")
    by_xc = swap(by_x, "tc")
    by_yc = swap(by_y, "tc")
    return [
        (own,),
        (by_c,),
        (by_y,),
        (by_yc,),
        (by_x,),
        (by_xc,),
        (diag_top, diag_bot),
        (swap(diag_top, "tc"), swap(diag_bot, "tc")),
    ], side


def core_add(mine, other):
    return mine.astype(F32) + swap(other, "tc").astype(F32)


def far_sum(far, far_c, cut):
    if len(far) == 1:
        far, far_c = (far[0][:cut], far[0][cut:]), (far_c[0][:cut], far_c[0][cut:])
    return core_add(far[0], far_c[0]).astype(BF), core_add(far[1], far_c[1]).astype(BF)


def far_swap(sent):
    return swap(sent[0], "fi"), swap(sent[1], "ty")


def near_first(parts):
    (x_top, y_bot), (x_top_c, y_bot_c) = parts
    return core_add(x_top, x_top_c).astype(BF), core_add(y_bot, y_bot_c).astype(BF)


def near_second(parts, got):
    (x_bot, y_top), (x_bot_c, y_top_c) = parts
    x_bot = core_add(x_bot, x_bot_c) + got[1].astype(F32)
    y_top = core_add(y_top, y_top_c) + got[0].astype(F32)
    return x_bot.astype(BF), y_top.astype(BF)


def near_swap(first):
    return swap(first[0], "fi"), swap(first[1], "ty")


def plane_pieces(parts_o, first, second):
    own, own_c = parts_o
    return own[0], swap(own_c[0], "tc"), first[0], second[0], second[1], first[1]


def piece_sum(pieces):
    own, sib, x_top, x_bot, y_top, y_bot = (piece[...].astype(F32) for piece in pieces)
    cross = jnp.concatenate([x_top + y_top, x_bot + y_bot], axis=0)
    return own + sib + cross


def mix(flag, at_zero, at_one):
    return at_zero * (1.0 - flag) + at_one * flag


def nbytes(shapes):
    return sum(math.prod(shape) * jnp.dtype(dtype).itemsize for shape, dtype in shapes)


def price(us, moved):
    return pl.CostEstimate(flops=int(us * 1.0e9), transcendentals=0, bytes_accessed=moved)


def run(kernel, outs, ins, us, *, grid=(), in_specs=None, out_specs=None, scratch=(), prefetch=0):
    return pl.pallas_call(
        kernel,
        out_shape=[jax.ShapeDtypeStruct(shape, dtype) for shape, dtype in outs],
        grid_spec=pltpu.PrefetchScalarGridSpec(
            num_scalar_prefetch=prefetch,
            grid=grid,
            in_specs=in_specs,
            out_specs=out_specs,
            scratch_shapes=list(scratch),
        ),
        compiler_params=pltpu.CompilerParams(
            vmem_limit_bytes=44 << 20, dimension_semantics=("arbitrary",) * len(grid)
        ),
        cost_estimate=price(us, nbytes(outs) + nbytes([(v.shape, v.dtype) for v in ins])),
    )(*ins)


def whole(shape):
    return pl.BlockSpec(shape, lambda *_: (0,) * len(shape))


def mm(left, right):
    return jnp.dot(left, right, preferred_element_type=F32)


def mm_nt(left, right):
    return lax.dot_general(left, right, (((1,), (1,)), ((), ())), preferred_element_type=F32)


def mm_tn(left, right):
    return lax.dot_general(left, right, (((0,), (0,)), ((), ())), preferred_element_type=F32)


def qkv_kernel(flags, x_ref, place_ref, cos_ref, sin_ref, *refs):
    w_refs, (xin_ref, qrot_ref, qn_ref, kv_ref, kn_ref, fac_ref) = refs[:10], refs[10:16]
    gains_ref, heads_ref = refs[16:]
    fi, ty, tc = (flags[n].astype(F32) for n in range(3))
    gains_ref[...] = w_refs[0][:, 128:256].astype(F32).T[64:72, :]
    line = mm_nt(gains_ref[...].astype(BF), place_ref[...])
    lo, hi = line[:, :128], line[:, 128:]
    heads_ref[...] = jnp.concatenate([mix(fi, lo, hi), mix(fi, hi, lo)], axis=1)
    x = x_ref[...].astype(F32)
    x_factor = lax.rsqrt(jnp.mean(x * x, -1, keepdims=True) + EPS)
    xin = (x * x_factor * gains_ref[0:1, :]).astype(BF)
    xin_ref[...] = xin
    prod = [mm_split(xin, pair) for pair in split_w(w_refs, w_refs[6].shape[0])]
    cos, sin = cos_ref[...], sin_ref[...]
    rows = x.shape[0]
    lane = lax.broadcasted_iota(jnp.int32, (rows, 128), 1)
    factors = jnp.zeros((rows, 128), F32)

    def normed(own, oth, row):
        total = jnp.sum(own * own + oth * oth, -1, keepdims=True)
        factor = lax.rsqrt(total * (1.0 / HD) + EPS)
        own, oth = own * factor, oth * factor
        g_own = own * heads_ref[row : row + 1, :128]
        g_oth = oth * heads_ref[row : row + 1, 128:]
        rot = jnp.concatenate([g_own * cos - g_oth * sin, g_oth * cos + g_own * sin], axis=1)
        return jnp.concatenate([own, oth], axis=1), rot, factor

    for r in range(4):
        norm, rot, factor = normed(prod[r][:, :128], prod[4 + r][:, :128], 4)
        qn_ref[r] = norm.astype(BF)
        qrot_ref[r] = rot.astype(BF)
        factors = jnp.where(lane == r, factor, factors)
    keys, vals = [], []
    for dx in range(2):
        sides = []
        for dy in range(2):
            zero = prod[dx * 4 + dy * 2][:, 128:192]
            one = prod[dx * 4 + dy * 2 + 1][:, 128:192]
            sides.append(jnp.concatenate([mix(tc, zero, one), mix(tc, one, zero)], axis=1))
        keys.append(mix(ty, sides[0], sides[1]))
        vals.append(mix(ty, sides[1], sides[0]))
    norm, rot, factor = normed(keys[0], keys[1], 5)
    kn_ref[...] = norm.astype(BF)
    fac_ref[...] = jnp.where(lane == 4, factor, factors)
    kv_ref[...] = jnp.concatenate([rot, vals[0], vals[1]], axis=1).astype(BF)


def split_w(refs, cut):
    pairs = [(ref[:cut, :], ref[cut:, :]) for ref in refs[:6]]
    return pairs + [(refs[6][...], refs[7][...]), (refs[8][...], refs[9][...])]


def head_w(pairs, r):
    return tuple(jnp.concatenate([pairs[r][n], pairs[4 + r][n]], axis=1) for n in (0, 1))


def mm_split(left, pair):
    cut = pair[0].shape[0]
    return mm(left[:, :cut], pair[0]) + mm(left[:, cut:], pair[1])


def mm_nt_split(left, pair):
    return jnp.concatenate([mm_nt(left, pair[0]), mm_nt(left, pair[1])], axis=1)


def kv_block(refs, kb):
    start = (kb % 2) * 256
    return refs[kb // 2][start : start + 256, :]


def attn_kernel(need, q_ref, k2_ref, kp_ref, ko_ref, bias_ref, o_ref, linv_ref, acc_ref, l_ref):
    i = pl.program_id(0)
    acc_ref[...] = jnp.zeros_like(acc_ref)
    l_ref[...] = jnp.zeros_like(l_ref)
    tile = q_ref.shape[1]
    for kb in range(6):

        @pl.when(need[i * 6 + kb] > 0)
        def _(kb=kb):
            kv = kv_block((k2_ref, kp_ref, ko_ref), kb)
            q = q_ref[...].reshape(4 * tile, HD)
            s = mm_nt(q, kv[:, :HD]).reshape(4, tile, 256) * HD ** (-0.5)
            p = jnp.exp(s + bias_ref[:, kb * 256 : (kb + 1) * 256][None])
            p = p.reshape(4 * tile, 256)
            l_ref[...] += p[:, :128] + p[:, 128:]
            acc_ref[...] += mm(p.astype(BF), kv[:, HD:])

    linv = 1.0 / jnp.sum(l_ref[...], -1, keepdims=True)
    linv_ref[...] = jnp.broadcast_to(linv, (4 * tile, 128)).reshape(4, tile, 128)
    o_ref[...] = (acc_ref[...] * linv).astype(BF).reshape(4, tile, HD)


def out_kernel(o_ref, x_ref, gains_ref, *refs):
    w_refs, (part_ref, hid_ref, ffn_ref) = refs[:10], refs[10:]
    pairs = split_w(w_refs, w_refs[6].shape[0])
    part = jnp.zeros(part_ref.shape, F32)
    for r in range(4):
        part += mm_nt_split(o_ref[r], head_w(pairs, r))
    part_ref[...] = part
    factor = lax.rsqrt(jnp.mean(part * part, -1, keepdims=True) + EPS)
    hidden = x_ref[...].astype(F32) + part * factor * gains_ref[1:2, :]
    hid_ref[...] = hidden
    factor = lax.rsqrt(jnp.mean(hidden * hidden, -1, keepdims=True) + EPS)
    ffn_ref[...] = (hidden * factor * gains_ref[2:3, :]).astype(BF)


def gelu_parts(gate, up):
    c0 = math.sqrt(2.0 / math.pi)
    square = gate * gate
    th = jnp.tanh(gate * (c0 + (0.044715 * c0) * square))
    side = 0.5 + 0.5 * th
    gelu = gate * side
    slope = side + gelu * (1.0 - th) * (c0 + (3.0 * 0.044715 * c0) * square)
    return gelu * up, slope * up, gelu


def ffn_layout(refs, layout):
    at, groups = 0, []
    for block, spans in enumerate(layout):
        row = 0
        for start, count in spans:
            groups.append((block, at, pl.ds(row, count), pl.ds(start, count), refs[at]))
            row += count
            at += 1
    return groups


def ffn_kernel(*refs, layout, base, hpad):
    n_x, blocks = sum(len(spans) for spans in layout), len(layout)
    x_refs, w_ref = refs[:n_x], refs[n_x]
    outs, scr = refs[-(13 + n_x) : -9], refs[-9:]
    all_refs, part_refs = outs[:4], outs[4:]
    xs, act_s, slope_s, gelu_s, part_s, x_sem, out_sem, part_sem, _ = scr
    rows = xs.shape[1]
    stage = (xs, act_s, slope_s, gelu_s)
    loads = [[] for _ in range(blocks)]
    for block, at, row, span, ref in ffn_layout(x_refs, layout):
        copy = pltpu.make_async_copy(ref.at[span, :], xs.at[block, row, :], x_sem.at[at])
        copy.start()
        loads[block].append(copy)

    def stack(block, n):
        dst = all_refs[n].at[pl.ds((base + block) * rows, rows), :]
        return pltpu.make_async_copy(stage[n].at[block], dst, out_sem.at[block, n])

    def part_copies(block):
        groups = [group for group in ffn_layout(part_refs, layout) if group[0] == block]
        return [
            pltpu.make_async_copy(part_s.at[block, row, :], ref, part_sem.at[at])
            for _, at, row, _, ref in groups
        ]

    def one_block(i, carry):
        per_block(i, blocks, lambda block: [copy.wait() for copy in loads[block]])
        stack(i, 0).start()
        x = xs[i]
        for c in range(0, hpad, 256):
            wide = min(256, hpad - c)
            gate = mm(x, w_ref[:, c : c + wide])
            up = mm(x, w_ref[:, hpad + c : hpad + c + wide])
            act, slope, gelu = gelu_parts(gate, up)
            act_s[i, :, c : c + wide] = act.astype(BF)
            slope_s[i, :, c : c + wide] = slope.astype(BF)
            gelu_s[i, :, c : c + wide] = gelu.astype(BF)
        for n in (1, 2, 3):
            stack(i, n).start()
        part_s[i] = mm_nt(act_s[i], w_ref[:, 2 * hpad :]).astype(BF)
        per_block(i, blocks, lambda block: [copy.start() for copy in part_copies(block)])
        return carry

    lax.fori_loop(0, blocks, one_block, 0)
    for block in range(blocks):
        for n in range(4):
            stack(block, n).wait()
        for copy in part_copies(block):
            copy.wait()


def per_block(i, blocks, act):
    for block in range(blocks):

        @pl.when(i == block)
        def _(block=block):
            act(block)


def ffn_back_kernel(*refs, layout, base, hpad):
    n_x, blocks = sum(len(spans) for spans in layout), len(layout)
    x_refs, w_ref, saved_refs = refs[:n_x], refs[n_x], refs[n_x + 1 : n_x + 3]
    outs, scr = refs[-(11 + n_x) : -9], refs[-9:]
    all_refs, part_refs = outs[:2], outs[2:]
    xs, dgu_s, slope_s, gelu_s, part_s, x_sem, out_sem, part_sem, saved_sem = scr
    rows = xs.shape[1]
    stage = (xs, dgu_s)
    loads = [[] for _ in range(blocks)]

    def saved(block, n):
        src = saved_refs[n].at[pl.ds((base + block) * rows, rows), :]
        dst = (slope_s, gelu_s)[n].at[block]
        copy = pltpu.make_async_copy(src, dst, saved_sem.at[block, n])
        copy.start()
        loads[block].append(copy)

    for block, at, row, span, ref in ffn_layout(x_refs, layout):
        copy = pltpu.make_async_copy(ref.at[span, :], xs.at[block, row, :], x_sem.at[at])
        copy.start()
        loads[block].append(copy)

    for block in range(blocks):
        saved(block, 0)
        saved(block, 1)

    def stack(block, n):
        dst = all_refs[n].at[pl.ds((base + block) * rows, rows), :]
        return pltpu.make_async_copy(stage[n].at[block], dst, out_sem.at[block, n])

    def part_copies(block):
        groups = [group for group in ffn_layout(part_refs, layout) if group[0] == block]
        return [
            pltpu.make_async_copy(part_s.at[block, row, :], ref, part_sem.at[at])
            for _, at, row, _, ref in groups
        ]

    def one_block(i, carry):
        per_block(i, blocks, lambda block: [copy.wait() for copy in loads[block]])
        stack(i, 0).start()
        dout = xs[i]
        for c in range(0, hpad, 256):
            wide = min(256, hpad - c)
            d_act = mm(dout, w_ref[:, 2 * hpad + c : 2 * hpad + c + wide])
            slope = slope_s[i, :, c : c + wide].astype(F32)
            gelu = gelu_s[i, :, c : c + wide].astype(F32)
            dgu_s[i, :, c : c + wide] = (d_act * slope).astype(BF)
            dgu_s[i, :, hpad + c : hpad + c + wide] = (d_act * gelu).astype(BF)
        stack(i, 1).start()
        part_s[i] = mm_nt(dgu_s[i], w_ref[:, : 2 * hpad]).astype(BF)
        per_block(i, blocks, lambda block: [copy.start() for copy in part_copies(block)])
        return carry

    lax.fori_loop(0, blocks, one_block, 0)
    for block in range(blocks):
        for n in range(2):
            stack(block, n).wait()
        for copy in part_copies(block):
            copy.wait()


def hold_kernel(src_ref, dst_ref, sem):
    copy = pltpu.make_async_copy(src_ref, dst_ref, sem.at[0])
    copy.start()
    copy.wait()


def hold(value):
    return pl.pallas_call(
        hold_kernel,
        out_shape=pltpu.VMEM(value.shape, value.dtype),
        in_specs=[pl.BlockSpec(memory_space=pltpu.HBM)],
        out_specs=pl.BlockSpec(memory_space=pltpu.VMEM),
        scratch_shapes=[pltpu.SemaphoreType.DMA((1,))],
        compiler_params=pltpu.CompilerParams(vmem_limit_bytes=16 << 20),
        cost_estimate=price(3, 1000000),
    )(in_hbm(value))


def in_hbm(value):
    return pltpu.with_memory_space_constraint(value, pltpu.HBM)


def ffn_call(kernel, blocks, base, saved, w_ffn, bufs):
    pieces = [value for block in blocks for value, _, _ in block]
    layout = tuple(tuple((start, count) for _, start, count in block) for block in blocks)
    n, back = len(blocks), bool(saved)
    width, hpad = w_ffn.shape[0], w_ffn.shape[1] // 3
    rows = sum(count for _, count in layout[0])
    widths = [width, 2 * hpad] if back else [width, hpad, hpad, hpad]
    ins = [in_hbm(v) for v in pieces] + [w_ffn] + [in_hbm(v) for v in saved]
    aliases = {}
    if bufs is not None:
        aliases = {len(ins) + k: k for k in range(len(widths))}
        ins = ins + [in_hbm(v) for v in bufs]
    hbm = pl.BlockSpec(memory_space=pltpu.HBM)
    in_specs = [hbm] * len(ins)
    in_specs[len(pieces)] = pl.BlockSpec(memory_space=pltpu.VMEM)
    counts = [count for spans in layout for _, count in spans]
    shapes = [((8 * rows, w), BF) for w in widths] + [((count, width), BF) for count in counts]
    mid = [2 * hpad, hpad, hpad] if back else [hpad, hpad, hpad]
    scratch = [pltpu.VMEM((n, rows, w), BF) for w in [width] + mid + [width]]
    scratch += [
        pltpu.SemaphoreType.DMA((len(pieces),)),
        pltpu.SemaphoreType.DMA((n, 4)),
        pltpu.SemaphoreType.DMA((len(pieces),)),
        pltpu.SemaphoreType.DMA((n, 2)),
    ]
    outs = pl.pallas_call(
        partial(kernel, layout=layout, base=base, hpad=hpad),
        out_shape=[pltpu.HBM(shape, dtype) for shape, dtype in shapes],
        in_specs=in_specs,
        out_specs=[hbm] * len(shapes),
        scratch_shapes=scratch,
        input_output_aliases=aliases,
        compiler_params=pltpu.CompilerParams(vmem_limit_bytes=28 << 20),
        cost_estimate=price(6 * n, 1000000 * n),
    )(*ins)
    grouped, at = [], len(widths)
    for spans in layout:
        grouped.append(tuple(outs[at : at + len(spans)]))
        at += len(spans)
    return outs[: len(widths)], grouped


def ffn_mid_kernel(*refs):
    hid_ref, cot_ref, gains_ref, out_ref, dout_ref, gain_ref = refs[6:]
    part = piece_sum(refs[:6])
    gain = gains_ref[3:4, :]
    factor = lax.rsqrt(jnp.mean(part * part, -1, keepdims=True) + EPS)
    out_ref[...] = (hid_ref[...] + part * factor * gain).astype(BF)
    back, gain_grad = norm_back_tile(part, gain, cot_ref[...].astype(F32))
    dout_ref[...] = back.astype(BF)
    gain_ref[0:1, :] = gain_grad


def norm_back_tile(raw, gain, upstream):
    factor = lax.rsqrt(jnp.mean(raw * raw, -1, keepdims=True) + EPS)
    normed = raw * factor
    gain_grad = jnp.sum(upstream * normed, axis=0, keepdims=True)
    scaled = upstream * gain
    back = factor * (scaled - normed * jnp.mean(scaled * normed, -1, keepdims=True))
    return back, gain_grad


def mid_kernel(*refs):
    hid_ref, part_ref, cot_ref, gains_ref = refs[6:10]
    w_refs, (dhid_ref, dpart_ref, dhead_ref, gain_ref) = refs[10:20], refs[20:]
    din = piece_sum(refs[:6])
    extra, gain_ffn = norm_back_tile(hid_ref[...], gains_ref[2:3, :], din)
    dhid = cot_ref[...].astype(F32) + extra
    dhid_ref[...] = dhid
    dpart, gain_post = norm_back_tile(part_ref[...], gains_ref[1:2, :], dhid)
    dpart = dpart.astype(BF)
    dpart_ref[...] = dpart
    gain_ref[0:1, :] = gain_ffn
    gain_ref[1:2, :] = gain_post
    pairs = split_w(w_refs, w_refs[6].shape[0])
    for r in range(4):
        dhead_ref[r] = mm_split(dpart, head_w(pairs, r)).astype(BF)


def attn_back_kernel(
    need,
    q_ref,
    k2_ref,
    kp_ref,
    ko_ref,
    bias_ref,
    o_ref,
    do_ref,
    linv_ref,
    qn_ref,
    fac_ref,
    cos_ref,
    sin_ref,
    gq_ref,
    dq_ref,
    d2_ref,
    dp_ref,
    down_ref,
    gain_ref,
    acc_ref,
    dkv_ref,
):
    i = pl.program_id(0)
    tile = q_ref.shape[1]

    @pl.when(i == 0)
    def _():
        dkv_ref[...] = jnp.zeros_like(dkv_ref)
        gain_ref[...] = jnp.zeros_like(gain_ref)

    acc_ref[...] = jnp.zeros_like(acc_ref)
    q = q_ref[...].reshape(4 * tile, HD)
    do = do_ref[...].reshape(4 * tile, HD)
    linv = linv_ref[...].reshape(4 * tile, 128)[:, 0:1]
    inner = jnp.sum(do.astype(F32) * o_ref[...].reshape(4 * tile, HD).astype(F32), -1, keepdims=True)
    for kb in range(6):

        @pl.when(need[i * 6 + kb] > 0)
        def _(kb=kb):
            kv = kv_block((k2_ref, kp_ref, ko_ref), kb)
            keys, vals = kv[:, :HD], kv[:, HD:]
            s = mm_nt(q, keys).reshape(4, tile, 256) * HD ** (-0.5)
            p = jnp.exp(s + bias_ref[:, kb * 256 : (kb + 1) * 256][None])
            p = p.reshape(4 * tile, 256) * linv
            dp = mm_nt(do, vals)
            ds = (p * (dp - inner)).astype(BF)
            acc_ref[...] += mm(ds, keys)
            span = slice(kb * 256, (kb + 1) * 256)
            dkv_ref[span, :HD] += mm_tn(ds, q)
            dkv_ref[span, HD:] += mm_tn(p.astype(BF), do)

    cos, sin = cos_ref[...], sin_ref[...]
    gain = jnp.zeros((1, HD), F32)
    for r in range(4):
        dq = acc_ref[r * tile : (r + 1) * tile, :] * HD ** (-0.5)
        own, oth = dq[:, :128], dq[:, 128:]
        back = jnp.concatenate([own * cos + oth * sin, oth * cos - own * sin], axis=1)
        norm = qn_ref[r].astype(F32)
        gain += jnp.sum(back * norm, axis=0, keepdims=True)
        scaled = back * gq_ref[4:5, :]
        mean = jnp.mean(scaled * norm, -1, keepdims=True)
        dq_ref[r] = (fac_ref[:, r : r + 1] * (scaled - norm * mean)).astype(BF)
    gain_ref[0:1, :] += gain

    @pl.when(i == pl.num_programs(0) - 1)
    def _():
        rows = d2_ref.shape[0]
        scale = HD ** (-0.5)
        for n, ref in enumerate((d2_ref, dp_ref, down_ref)):
            block = dkv_ref[n * rows : (n + 1) * rows, :]
            ref[:, :HD] = (block[:, :HD] * scale).astype(ref.dtype)
            ref[:, HD:] = block[:, HD:].astype(ref.dtype)


def post_kernel(
    flags,
    dq_ref,
    dkv_ref,
    dp_ref,
    kn_ref,
    fac_ref,
    cos_ref,
    sin_ref,
    gk_ref,
    x_ref,
    gains_ref,
    dhid_ref,
    gq_grad,
    mid_grad,
    post_grad,
    place_ref,
    *refs,
):
    w_refs, din_ref, kvraw_ref, gain_ref = refs[:10], *refs[10:]
    fi, ty, tc = (flags[n].astype(F32) for n in range(3))
    dkv = dkv_ref[...] + dp_ref[...].astype(F32)
    cos, sin = cos_ref[...], sin_ref[...]
    own, oth = dkv[:, :128], dkv[:, 128:256]
    back = jnp.concatenate([own * cos + oth * sin, oth * cos - own * sin], axis=1)
    norm = kn_ref[...].astype(F32)
    gk_grad = jnp.sum(back * norm, axis=0, keepdims=True)
    scaled = back * gk_ref[5:6, :]
    mean = jnp.mean(scaled * norm, -1, keepdims=True)
    dkey = fac_ref[:, 4:5] * (scaled - norm * mean)
    dval = dkv[:, 256:]
    kvraw_ref[...] = jnp.concatenate([dkey, dval], axis=1).astype(BF)
    din = jnp.zeros(din_ref.shape, F32)
    zeros = jnp.zeros((dkv.shape[0], 64), F32)
    pairs = split_w(w_refs, w_refs[6].shape[0])
    rel = 0
    for dx in range(2):
        kh = dkey[:, dx * 128 : (dx + 1) * 128]
        vh = dval[:, dx * 128 : (dx + 1) * 128]
        for dy in range(2):
            half = mix(ty, kh, vh) if dy == 0 else mix(ty, vh, kh)
            for dc in range(2):
                lo, hi = half[:, :64], half[:, 64:]
                part = mix(tc, lo, hi) if dc == 0 else mix(tc, hi, lo)
                side = jnp.concatenate([part, zeros], axis=1).astype(BF)
                dprod = jnp.concatenate(
                    [dq_ref[dy * 2 + dc][:, dx * 128 : (dx + 1) * 128], side], axis=1
                )
                din += mm_nt_split(dprod, pairs[rel])
                rel += 1
    x = x_ref[...].astype(F32)
    extra, gain_pre = norm_back_tile(x, gains_ref[0:1, :], din)
    din_ref[...] = dhid_ref[...] + extra

    def spread(grad):
        own, oth = grad[:, :128], grad[:, 128:]
        whole_row = jnp.concatenate([mix(fi, own, oth), mix(fi, oth, own)], axis=1)
        return mm(jnp.broadcast_to(whole_row.astype(BF), (8, HD)), place_ref[...])[0:1, :]

    gain_ref[...] = jnp.zeros_like(gain_ref)
    gain_ref[0:1, :] = gain_pre
    gain_ref[1:2, :] = mid_grad[1:2, :]
    gain_ref[2:3, :] = mid_grad[0:1, :]
    gain_ref[3:4, :] = post_grad[0:1, :]
    gain_ref[4:5, :] = spread(gq_grad[0:1, :])
    gain_ref[5:6, :] = spread(gk_grad)


def store_rows(refs, value):
    cut = refs[0].shape[0]
    refs[0][...] = value[:cut, :]
    refs[1][...] = value[cut:, :]


def qo_grad_kernel(xin, xin_c, dq, dq_c, dpart, dpart_c, head, head_c, *outs):
    xt, xt_c, dt, dt_c = (ref[...].T for ref in (xin, xin_c, dpart, dpart_c))
    for dy in range(2):
        gq = (mm(xt, dq[2 * dy]) + mm(xt_c, dq_c[dy])).astype(BF)
        go = (mm(dt, head[2 * dy]) + mm(dt_c, head_c[dy])).astype(BF)
        for dx in range(2):
            half = slice(dx * 128, (dx + 1) * 128)
            at = 4 * dx + 2 * dy
            store_rows(outs[at : at + 2], jnp.concatenate([gq[:, half], go[:, half]], axis=1))


def kv_grad_kernel(flags, xin, xin_c, kv, kv_c, gain, gain_c, *refs):
    outs, rows_ref = refs[:8], refs[8]
    ty, tc = flags[1].astype(F32), flags[2].astype(F32)
    rows_ref[...] = jnp.zeros_like(rows_ref)
    rows_ref[64:72, :] = gain[...] + gain_c[...]
    gain_cols = rows_ref[...].T
    xt, xt_c = xin[...].T, xin_c[...].T

    def sides(ref):
        block = ref[...].astype(F32)
        picked = []
        for dy in range(2):
            for dx in range(2):
                kh = block[:, dx * 128 : (dx + 1) * 128]
                vh = block[:, 256 + dx * 128 : 256 + (dx + 1) * 128]
                half = mix(ty, kh, vh) if dy == 0 else mix(ty, vh, kh)
                picked.append(mix(tc, half[:, :64], half[:, 64:]))
        return jnp.concatenate(picked, axis=1).astype(BF)

    grad = mm(xt, sides(kv)) + mm(xt_c, sides(kv_c))
    zeros = jnp.zeros((grad.shape[0], 64), F32)
    for dy in range(2):
        for dx in range(2):
            at = 4 * dx + 2 * dy
            col = (2 * dy + dx) * 64
            part = jnp.concatenate([grad[:, col : col + 64], zeros], axis=1) + gain_cols
            store_rows(outs[at : at + 2], part.astype(BF))


def chip_first(parts):
    _, near_y, near_x, far = (parts[n : n + 2] for n in (0, 2, 4, 6))
    return swap(far[0], "fi"), swap(far[1], "ty"), swap(near_x[0], "fi"), swap(near_y[1], "ty")


def chip_second(parts, first):
    own, near_y, near_x, _ = (parts[n : n + 2] for n in (0, 2, 4, 6))
    from_x, from_y, got_x_top, got_y_bot = first
    x_bot = (near_x[1].astype(F32) + from_y.astype(F32)).astype(BF)
    y_top = (near_y[0].astype(F32) + from_x.astype(F32)).astype(BF)
    return (*own, got_x_top, swap(x_bot, "fi"), swap(y_top, "ty"), got_y_bot)


def gather_sum_kernel(*refs):
    out_ref = refs[12]
    for n, cols in ((0, slice(0, 256)), (6, slice(256, 384))):
        own_top, own_bot, x_top, x_bot, y_top, y_bot = (ref[...].astype(F32) for ref in refs[n : n + 6])
        cut = own_top.shape[0]
        out_ref[:cut, cols] = (own_top + x_top + y_top).astype(BF)
        out_ref[cut:, cols] = (own_bot + x_bot + y_bot).astype(BF)


def pad_cols(value, width):
    return jnp.pad(value, ((0, 0), (0, width - value.shape[1])))


def body(
    tokens,
    positions,
    segments,
    w_query,
    w_key,
    w_value,
    w_out,
    w_gate,
    w_up,
    w_down,
    gain_attn_pre,
    gain_query,
    gain_key,
    gain_attn_post,
    gain_ffn_pre,
    gain_ffn_post,
    cotangent,
):
    fi = lax.axis_index("fi")
    ty = lax.axis_index("ty")
    tc = lax.axis_index("tc")
    t_idx = ty * 2 + tc
    me = fi * 4 + t_idx
    first = fi == 0
    rows = tokens.shape[0]
    width = tokens.shape[1]
    shard = w_query.shape[0]
    nf = width // shard
    hid = w_gate.shape[1] // 2
    hpad = -(-hid // 128) * 128
    gshard = gain_query.shape[0]

    def pair_rows(keep, recv):
        return jnp.where(
            first,
            jnp.concatenate([keep, recv], axis=0),
            jnp.concatenate([recv, keep], axis=0),
        )

    kv_mine = jnp.where(ty == 0, w_key, w_value)
    out_t = w_out.T
    gains = pad_cols(
        jnp.stack(
            [
                gain_attn_pre,
                gain_attn_post,
                gain_ffn_pre,
                gain_ffn_post,
                jnp.pad(gain_query, (0, shard - gshard)),
                jnp.pad(gain_key, (0, shard - gshard)),
            ],
            axis=1,
        ),
        64,
    )

    def piece(h):
        kv_half = kv_mine[:, h * 128 : (h + 1) * 128]
        kv_part = jnp.where(tc == 0, kv_half[:, :64], kv_half[:, 64:])
        return jnp.concatenate(
            [
                w_query[:, h * 128 : (h + 1) * 128],
                kv_part,
                gains,
                out_t[:, h * 128 : (h + 1) * 128],
            ],
            axis=1,
        )

    piece0, piece1 = piece(0), piece(1)
    keep = jnp.where(first, piece0, piece1)
    recv = swap(jnp.where(first, piece1, piece0), "fi")

    down_t = w_down.T

    def halves(weight):
        lo, hi = pad_cols(weight[:, :hid], hpad), pad_cols(weight[:, hid:], hpad)
        return jnp.where(first, lo, hi), jnp.where(first, hi, lo)

    gate_keep, gate_send = halves(w_gate)
    up_keep, up_send = halves(w_up)
    down_keep, down_send = halves(down_t)
    ffn_keep = jnp.concatenate([gate_keep, up_keep, down_keep], axis=1)
    ffn_send = jnp.concatenate([gate_send, up_send, down_send], axis=1)
    ffn_send, ffn_keep, recv = lax.optimization_barrier((ffn_send, ffn_keep, recv))
    ffn_recv = swap(ffn_send, "fi")
    attn_col = lax.all_gather(pair_rows(keep, recv), "fo", axis=0, tiled=True)
    attn_col, ffn_pair = lax.optimization_barrier((attn_col, pair_rows(ffn_keep, ffn_recv)))
    w_ffn = lax.all_gather(ffn_pair, "fo", axis=0, tiled=True)

    elem = lax.broadcasted_iota(jnp.int32, (HD, width), 0)
    spot = lax.broadcasted_iota(jnp.int32, (HD, width), 1)
    place = (spot == (elem // gshard) * shard + elem % gshard).astype(BF)
    cut = width // 256 * 128
    row_start = t_idx * rows
    pos_local = lax.dynamic_slice_in_dim(positions, row_start, rows)
    seg_local = lax.dynamic_slice_in_dim(segments, row_start, rows)

    def block_of(meta, back):
        return lax.dynamic_slice_in_dim(meta, ((t_idx - back) % 4) * rows, rows)

    k_pos = jnp.concatenate([block_of(positions, 2), block_of(positions, 1), pos_local])
    k_seg = jnp.concatenate(
        [
            jnp.where(t_idx == 3, block_of(segments, 2), -1),
            jnp.where(t_idx >= 1, block_of(segments, 1), -1),
            seg_local,
        ]
    )
    allowed = (
        ((k_seg[None, :] == 0) | (k_seg[None, :] == seg_local[:, None]))
        & (k_pos[None, :] <= pos_local[:, None])
        & (pos_local[:, None] - k_pos[None, :] < WINDOW)
    )
    bias = jnp.where(allowed, 0.0, NEG).astype(F32)
    need = jnp.any(allowed.reshape(4, rows // 4, 6, rows // 2), axis=(1, 3))
    need = need.astype(jnp.int32).reshape(24)
    frequency = jnp.exp(-math.log(BASE) * jnp.arange(HALF).astype(F32) / HALF)
    angles = pos_local.astype(F32)[:, None] * frequency
    cosine = jnp.cos(angles)
    sine = jnp.sin(angles) * jnp.where(first, 1.0, -1.0)

    w_parts, (bias, need, cosine, sine, place) = plane_gather(
        attn_col, cut, (bias, need, cosine, sine, place)
    )
    w_parts = [in_hbm(piece) for pieces in w_parts for piece in pieces]
    flags = jnp.stack([fi, ty, tc]).astype(jnp.int32)
    qkv_spec = [pl.BlockSpec((part.shape[0], 256), lambda *_: (0, 0)) for part in w_parts]
    wo_spec = [pl.BlockSpec((part.shape[0], 128), lambda *_: (0, 2)) for part in w_parts]
    full, gains8 = whole((rows, width)), whole((8, width))
    heads = whole((4, rows, HD))
    lanes = whole((rows, 128))
    kv_full = whole((rows, 2 * HD))
    attn_in, q_rot, q_norm, kv_own, k_norm, factors, gain_rows, head_gains = run(
        qkv_kernel,
        [
            ((rows, width), BF),
            ((4, rows, HD), BF),
            ((4, rows, HD), BF),
            ((rows, 2 * HD), BF),
            ((rows, HD), BF),
            ((rows, 128), F32),
            ((8, width), F32),
            ((8, HD), F32),
        ],
        (flags, tokens, place, cosine, sine, *w_parts),
        9,
        grid=(1,),
        in_specs=[full, whole((HD, width)), lanes, lanes] + qkv_spec,
        out_specs=[full, heads, heads, kv_full, whole((rows, HD)), lanes, gains8, whole((8, HD))],
        prefetch=1,
    )
    kv_prev = lax.ppermute(kv_own, ("ty", "tc"), [(i, (i + 1) % 4) for i in range(4)])
    kv_two = swap(kv_prev, "tc")
    tile = rows // 4
    q_tile = pl.BlockSpec((4, tile, HD), lambda i, *_: (0, i, 0))
    l_tile = pl.BlockSpec((4, tile, 128), lambda i, *_: (0, i, 0))
    bias_tile = pl.BlockSpec((tile, 3 * rows), lambda i, *_: (i, 0))
    head_out, linv = run(
        attn_kernel,
        [((4, rows, HD), BF), ((4, rows, 128), F32)],
        (need, q_rot, kv_two, kv_prev, kv_own, bias),
        8,
        grid=(4,),
        in_specs=[q_tile, kv_full, kv_full, kv_full, bias_tile],
        out_specs=[q_tile, l_tile],
        scratch=[pltpu.VMEM((4 * tile, HD), F32), pltpu.VMEM((4 * tile, 128), F32)],
        prefetch=1,
    )
    attn_part, hidden, ffn_local = run(
        out_kernel,
        [((rows, width), F32), ((rows, width), F32), ((rows, width), BF)],
        (head_out, tokens, gain_rows, *w_parts),
        6,
        grid=(1,),
        in_specs=[heads, full, gains8] + wo_spec,
        out_specs=[full, full, full],
    )

    half = rows // 2
    def far_pieces(top, bot, after):
        top, bot, after = lax.optimization_barrier((top, bot, after))
        return (top, bot), (swap(top, "tc"), swap(bot, "tc")), after

    by_x, by_y, by_c = swap(ffn_local, "fi"), swap(ffn_local, "ty"), swap(ffn_local, "tc")
    top, bot = swap(by_y[:half], "fi"), swap(by_x[half:], "ty")
    by_xc, by_yc = swap(by_x, "tc"), swap(by_y, "tc")
    w_ffn = hold(w_ffn)
    whole_of = lambda value: [(value, 0, rows)]
    halves_of = lambda low, high: [(low, 0, half), (high, half, half)]
    both_of = lambda top, bot: [(top, 0, half), (bot, 0, half)]
    first_rows = [halves_of(by_x, by_y), halves_of(by_xc, by_yc)]
    bufs, parts_1 = ffn_call(ffn_kernel, first_rows, 2, [], w_ffn, None)
    (top, bot), (top_c, bot_c), parts_1 = far_pieces(top, bot, parts_1)
    far = [both_of(top, bot), both_of(top_c, bot_c)]
    bufs, parts_f = ffn_call(ffn_kernel, far, 6, [], w_ffn, bufs)
    ffn_local, first_out = lax.optimization_barrier((ffn_local, near_first(parts_1)))
    first_in = near_swap(first_out)
    bufs, parts_o = ffn_call(
        ffn_kernel, [whole_of(ffn_local), whole_of(by_c)], 0, [], w_ffn, bufs
    )
    by_x, by_y, by_xc, by_yc, first_in, sent = lax.optimization_barrier(
        (by_x, by_y, by_xc, by_yc, first_in, far_sum(*parts_f, half))
    )
    got = far_swap(sent)
    second_rows = [
        [(by_x, half, half), (by_y, 0, half)],
        [(by_xc, half, half), (by_yc, 0, half)],
    ]
    (x_all, act_all, slope_all, gelu_all), parts_2 = ffn_call(
        ffn_kernel, second_rows, 4, [], w_ffn, bufs
    )
    parts_2, got = lax.optimization_barrier((parts_2, got))
    second_in = near_swap(near_second(parts_2, got))
    pieces = plane_pieces(parts_o, first_in, second_in)
    quarter = whole((half, width))
    piece_spec = [full, full] + [quarter] * 4

    other = swap(jnp.stack([head_out[1], head_out[3]]), "tc"), swap(attn_in, "tc")
    pieces, (head_out_c, attn_in_c) = lax.optimization_barrier((pieces, other))
    output, d_local, ffn_post_grad = run(
        ffn_mid_kernel,
        [((rows, width), BF), ((rows, width), BF), ((8, width), F32)],
        (*pieces, hidden, cotangent, gain_rows),
        6,
        grid=(1,),
        in_specs=piece_spec + [full, full, gains8],
        out_specs=[full, full, gains8],
    )
    by_x, by_y, by_c = swap(d_local, "fi"), swap(d_local, "ty"), swap(d_local, "tc")
    saved = [slope_all, gelu_all]
    own_rows = [whole_of(d_local), whole_of(by_c)]
    bufs, parts_o = ffn_call(ffn_back_kernel, own_rows, 0, saved, w_ffn, None)
    by_x, by_y, parts_o = lax.optimization_barrier((by_x, by_y, parts_o))
    top, bot = swap(by_y[:half], "fi"), swap(by_x[half:], "ty")
    by_xc, by_yc = swap(by_x, "tc"), swap(by_y, "tc")
    first_rows = [halves_of(by_x, by_y), halves_of(by_xc, by_yc)]
    bufs, parts_1 = ffn_call(ffn_back_kernel, first_rows, 2, saved, w_ffn, bufs)
    (top, bot), (top_c, bot_c), parts_1 = far_pieces(top, bot, parts_1)
    first_in = near_swap(near_first(parts_1))
    far = [both_of(top, bot), both_of(top_c, bot_c)]
    bufs, parts_f = ffn_call(ffn_back_kernel, far, 6, saved, w_ffn, bufs)
    second_rows = [
        [(by_x, half, half), (by_y, 0, half)],
        [(by_xc, half, half), (by_yc, 0, half)],
    ]
    (d_all, dgu_all), parts_2 = ffn_call(
        ffn_back_kernel, second_rows, 4, saved, w_ffn, bufs
    )
    sent = far_sum(*parts_f, half)
    d_all, sent, first_in = lax.optimization_barrier((d_all, sent, first_in))
    got = far_swap(sent)
    grad_dt = dot_left_t(d_all, act_all).astype(BF)
    dgu_all, grad_dt, got = lax.optimization_barrier((dgu_all, grad_dt, got))
    second_in = near_swap(near_second(parts_2, got))
    grad_gu = dot_left_t(x_all, dgu_all).astype(BF)
    pieces = plane_pieces(parts_o, first_in, second_in)
    pieces, grad_gu = lax.optimization_barrier((pieces, grad_gu))
    sum_dt = lax.psum_scatter(grad_dt, "fo", scatter_dimension=0, tiled=True)
    sum_gu = lax.psum_scatter(grad_gu, "fo", scatter_dimension=0, tiled=True)

    def unpair(summed):
        top_rows, bot_rows = summed[:shard], summed[shard:]
        mine = jnp.where(first, top_rows, bot_rows)
        theirs = swap(jnp.where(first, bot_rows, top_rows), "fi")
        return jnp.where(first, mine, theirs), jnp.where(first, theirs, mine)

    def join(lo, hi):
        return jnp.concatenate([lo[:, :hid], hi[:, :hid]], axis=1).astype(F32)

    hidden_grad, attn_part_grad, head_grad, mid_gains = run(
        mid_kernel,
        [((rows, width), F32), ((rows, width), BF), ((4, rows, HD), BF), ((8, width), F32)],
        (
            *map(in_hbm, (*pieces, hidden, attn_part, cotangent)),
            gain_rows,
            *w_parts,
        ),
        10,
        grid=(1,),
        in_specs=piece_spec + [full, full, full, gains8] + wo_spec,
        out_specs=[full, full, heads, whole((8, width))],
    )
    fac_tile = pl.BlockSpec((tile, 128), lambda i, *_: (i, 0))
    line = whole((8, HD))
    q_raw_grad, kv_grad_two, kv_grad_prev, kv_grad_own, gain_q = run(
        attn_back_kernel,
        [
            ((4, rows, HD), BF),
            ((rows, 2 * HD), BF),
            ((rows, 2 * HD), BF),
            ((rows, 2 * HD), F32),
            ((8, HD), F32),
        ],
        (
            need,
            q_rot,
            kv_two,
            kv_prev,
            kv_own,
            bias,
            head_out,
            head_grad,
            linv,
            q_norm,
            factors,
            cosine,
            sine,
            head_gains,
        ),
        12,
        grid=(4,),
        in_specs=[
            q_tile,
            kv_full,
            kv_full,
            kv_full,
            bias_tile,
            q_tile,
            q_tile,
            l_tile,
            q_tile,
            fac_tile,
            fac_tile,
            fac_tile,
            line,
        ],
        out_specs=[q_tile, kv_full, kv_full, kv_full, whole((8, HD))],
        scratch=[pltpu.VMEM((4 * tile, HD), F32), pltpu.VMEM((3 * rows, 2 * HD), F32)],
        prefetch=1,
    )
    q_raw_grad, attn_part_c = lax.optimization_barrier((q_raw_grad, swap(attn_part_grad, "tc")))
    back_two = kv_grad_prev.astype(F32) + swap(kv_grad_two, "tc").astype(F32)
    q_raw_grad, back_two = lax.optimization_barrier((q_raw_grad, back_two.astype(BF)))
    back_prev = lax.ppermute(back_two, ("ty", "tc"), [(i, (i + 3) % 4) for i in range(4)])
    def row_pieces(cols):
        return [((n, cols), BF) for n in (cut, width - cut)] * 4

    other_heads = lambda value: swap(jnp.stack([value[1], value[3]]), "tc")
    two_heads = whole((2, rows, HD))
    qo_grads = run(
        qo_grad_kernel,
        row_pieces(256),
        (
            attn_in,
            attn_in_c,
            q_raw_grad,
            other_heads(q_raw_grad),
            attn_part_grad,
            attn_part_c,
            head_out,
            head_out_c,
        ),
        5,
        grid=(1,),
        in_specs=[full, full, heads, two_heads, full, full, heads, two_heads],
        out_specs=[whole(shape) for shape, _ in row_pieces(256)],
    )
    back_prev, sum_dt, qo_grads = lax.optimization_barrier((back_prev, sum_dt, qo_grads))
    qo_first = chip_first(qo_grads)
    input_grad, kv_raw_grad, gain_grads = run(
        post_kernel,
        [((rows, width), F32), ((rows, 2 * HD), BF), ((8, width), F32)],
        (
            flags,
            q_raw_grad,
            in_hbm(kv_grad_own),
            back_prev,
            k_norm,
            factors,
            cosine,
            sine,
            head_gains,
            in_hbm(tokens),
            gain_rows,
            in_hbm(hidden_grad),
            gain_q,
            mid_gains,
            ffn_post_grad,
            place,
            *w_parts,
        ),
        9,
        grid=(1,),
        in_specs=[heads, kv_full, kv_full, whole((rows, HD)), lanes, lanes, lanes, line]
        + [full, gains8, full, whole((8, HD)), gains8, gains8]
        + [whole((HD, width))]
        + qkv_spec,
        out_specs=[full, kv_full, gains8],
        prefetch=1,
    )
    kv_raw_grad, qo_first = lax.optimization_barrier((kv_raw_grad, qo_first))
    kv_grads = run(
        kv_grad_kernel,
        row_pieces(128),
        (
            flags,
            attn_in,
            attn_in_c,
            kv_raw_grad,
            swap(kv_raw_grad, "tc"),
            gain_grads,
            swap(gain_grads, "tc"),
        ),
        3,
        grid=(1,),
        in_specs=[full, full, kv_full, kv_full, gains8, gains8],
        out_specs=[whole(shape) for shape, _ in row_pieces(128)],
        scratch=[pltpu.VMEM((128, width), F32)],
        prefetch=1,
    )
    qo_pieces = chip_second(qo_grads, qo_first)
    kv_pieces = chip_second(kv_grads, chip_first(kv_grads))
    qo_pieces, kv_pieces, sum_gu = lax.optimization_barrier((qo_pieces, kv_pieces, sum_gu))
    (attn_grads,) = run(
        gather_sum_kernel,
        [((width, 384), BF)],
        (*qo_pieces, *kv_pieces),
        2,
        grid=(1,),
        in_specs=[whole(piece.shape) for piece in (*qo_pieces, *kv_pieces)],
        out_specs=[whole((width, 384))],
    )
    sum_attn = lax.psum_scatter(attn_grads, "fo", scatter_dimension=0, tiled=True)
    dt_lo, dt_hi = unpair(sum_dt)
    gu_lo, gu_hi = unpair(sum_gu)
    grad_gate = join(gu_lo[:, :hpad], gu_hi[:, :hpad])
    grad_up = join(gu_lo[:, hpad:], gu_hi[:, hpad:])
    grad_down = join(dt_lo, dt_hi).T

    a_lo, a_hi = unpair(sum_attn)
    grad_out = jnp.concatenate([a_lo[:, 128:256], a_hi[:, 128:256]], axis=1).astype(F32).T
    grad_query = jnp.concatenate([a_lo[:, :128], a_hi[:, :128]], axis=1).astype(F32)
    kv_part = jnp.concatenate([a_lo[:, 256:320], a_hi[:, 256:320]], axis=1)
    others = [
        lax.ppermute(kv_part, ("ty", "tc"), [(i, i ^ step) for i in range(4)]) for step in (1, 2, 3)
    ]
    row_here = jnp.where(tc == 0, 0, 1)

    def kv_lines(near, far):
        even = jnp.where(row_here == 0, near, far)
        odd = jnp.where(row_here == 0, far, near)
        return jnp.concatenate([even[:, :64], odd[:, :64], even[:, 64:], odd[:, 64:]], axis=1)

    kv_here, kv_far = kv_lines(kv_part, others[0]), kv_lines(others[1], others[2])
    grad_key = jnp.where(ty == 0, kv_here, kv_far).astype(F32)
    grad_value = jnp.where(ty == 0, kv_far, kv_here).astype(F32)
    gain_out = a_lo[:, 320:328].astype(F32).T
    return (
        output.astype(BF),
        input_grad,
        grad_query,
        grad_key,
        grad_value,
        grad_out,
        grad_gate,
        grad_up,
        grad_down,
        gain_out[0],
        gain_out[4, :gshard],
        gain_out[5, :gshard],
        gain_out[1],
        gain_out[2],
        gain_out[3],
    )


def solution(mesh):
    nf, nt = mesh.shape["fsdp"], mesh.shape["tensor"]
    fine = Mesh(mesh.devices.reshape(nf // 2, 2, nt // 2, 2), ("fo", "fi", "ty", "tc"))
    f_axes, t_axes = ("fo", "fi"), ("ty", "tc")
    rows = P(f_axes + t_axes, None)
    col = P(f_axes, t_axes)
    flat = P(f_axes, None)
    out_w = P(t_axes, f_axes)
    vec = P(f_axes)
    in_specs = (rows, vec, vec, col, flat, flat, out_w, col, col, out_w) + (vec,) * 6 + (rows,)
    out_specs = (rows, rows, col, flat, flat, out_w, col, col, out_w) + (vec,) * 6
    return jax.shard_map(body, mesh=fine, in_specs=in_specs, out_specs=out_specs, check_vma=False)
```
